32 devices in a mesh: groups: 2 (over y), tm: 4 (over z), head: 4 (over x, core).
Axes of the slice: x: 2, y: 2, z: 4, core: 2. Of those that a mesh axis runs over, the one named last changes fastest.
Arguments:
- queries: bfloat16 [8, 256, 3072], P(('groups', 'tm'), 'head'), parts along dimension 0, may hold values from -128 to 128
- keys: bfloat16 [8, 256, 3072], P(('groups', 'tm'), 'head'), parts along dimension 0, may hold values from -6 to 6
- values: bfloat16 [8, 256, 3072], P(('groups', 'tm'), 'head'), parts along dimension 0, may hold values from -6 to 6
- residual: bfloat16 [8, 256, 5120], P(('groups', 'tm'), None, 'head'), parts along dimension 0, may hold values from -3 to 3
- fresh_frame: bfloat16 [512, 5120], P('groups', 'head'), parts along dimension 0, may hold values from -6 to 6
- out_weight: bfloat16 [3072, 5120], P('tm', 'head'), may hold values from -0.875 to 0.875
- time_weight: bfloat16 [256, 5120], P(None, 'head'), may hold values from -0.375 to 0.375
- noise_steps: int32 [8], P(('groups', 'tm')), parts along dimension 0, may hold values from 0 to 49, as said below
- frame_mask: int32 [8, 4], P(('groups', 'tm')), parts along dimension 0, may hold values from 0 to 1, as said below
Outputs:
- rolled: bfloat16 [8, 256, 5120], P(('groups', 'tm'), None, 'head'), parts along dimension 0
The draws below stay inside these ranges and needn't reach their ends.
There are 2 independent parts, one for each index of `groups`. The reference program is written for one: setup_inputs(seed, part) draws one part's arguments, and reference() takes and returns one part's arrays. A program takes and returns all parts, laid end to end along the dimension named above; an argument that names none is the same for every part. Nothing has to cross between parts.
Inputs may be any that keep to these rules, and one draw needn't show every extreme that they name: frame_mask[i, j] is 1 exactly for i - L_i < j <= i, with a whole number L_i from 1 to 4 for each frame i; the last frame has L_i = 4. `noise_steps`: never falling along the frames; the first frame has 0 and the last 49.
All inputs are finite; a program needn't handle non-finite values.
Results may differ from the reference program's by a relative error of at most 0.0065.
Values may be sent and summed in bfloat16 or wider, within the bound.
A program may use at most 64 MiB of HBM per device.

```python
import math
import jax
import jax.numpy as jnp
from jax import lax

D = 5120
HD = 128
HEADS = 24
FREQ = 256
STEPS = 50
TOK = 256
FRAMES = 4
WIN = 4


def draw_pair(key):
    base = jax.random.fold_in(key, 11)
    key_normal, key_query = jax.random.split(base, 2)
    shape = (FRAMES, TOK, HEADS * HD)
    keys_raw = jnp.clip(jax.random.normal(key_normal, shape, jnp.float32), -6.0, 6.0)
    query_raw = jnp.clip(2.0 * jax.random.normal(key_query, shape, jnp.float32), -12.0, 12.0)
    return (query_raw, keys_raw)


def draw_queries(key, part):
    return draw_pair(key)[0].astype(jnp.bfloat16)


def draw_keys(key, part):
    return draw_pair(key)[1].astype(jnp.bfloat16)


def draw_noise_steps(key, part):
    picks = jax.random.randint(jax.random.fold_in(key, 23), (FRAMES,), 0, STEPS)
    ordered = jnp.sort(picks)
    position = jnp.arange(FRAMES)
    ordered = jnp.where(position == 0, 0, jnp.where(position == FRAMES - 1, STEPS - 1, ordered))
    return ordered.astype(jnp.int32)


def draw_frame_mask(key, part):
    spans = jax.random.randint(jax.random.fold_in(key, 31), (FRAMES,), 1, WIN + 1)
    position = jnp.arange(FRAMES)
    spans = jnp.where(position == FRAMES - 1, WIN, spans)
    spans = jnp.minimum(spans, position + 1)
    rows = position[:, None]
    cols = position[None, :]
    return ((cols <= rows) & (cols > rows - spans[:, None])).astype(jnp.int32)


def steps_of(stream_key, dims, cuts, least, high):
    factor_of, own = 1.0, jax.random.fold_in(stream_key, 6)
    for dim, shards_of in cuts:
        draws = jnp.exp(jax.random.uniform(jax.random.fold_in(own, dim), (shards_of,), jnp.float32, least / len(cuts), high / len(cuts)))
        factor_of = factor_of * jnp.repeat(draws, dims[dim] // shards_of).reshape([-1 if axis == dim else 1 for axis in range(len(dims))])
    return factor_of


def scatter_about(key, dims, scale, reach, cuts=(), kind=jnp.bfloat16):
    gain = steps_of(key, dims, cuts, -0.22, 0.18) if cuts else 1.0
    drawn = jax.random.normal(key, dims, jnp.float32) * scale * gain
    return jnp.minimum(jnp.maximum(drawn, -reach), reach).astype(kind)


def setup_inputs(seed: int = 0, part: int = 0) -> dict:
    arg_keys = jax.random.split(jax.random.key(seed), 10)
    part_splits = jax.random.split(jax.random.fold_in(arg_keys[9], part), 10)
    queries = draw_queries(jax.random.fold_in(jax.random.fold_in(arg_keys[9], part), 71), part)
    keys = draw_keys(jax.random.fold_in(jax.random.fold_in(arg_keys[9], part), 71), part)
    values = scatter_about(part_splits[2], (FRAMES, TOK, HEADS * HD), 1.0, 6.0, ((0, 4), (1, 4)))
    residual = scatter_about(part_splits[3], (FRAMES, TOK, D), 0.5, 3.0, ((0, 4), (2, 4)))
    fresh_frame = scatter_about(part_splits[4], (TOK, D), 1.0, 6.0, ((1, 4),))
    out_weight = scatter_about(arg_keys[5], (HEADS * HD, D), (HEADS * HD // 64) ** -0.5, 0.875, ((0, 4), (1, 4)))
    time_weight = scatter_about(arg_keys[6], (FREQ, D), FREQ ** -0.5, 0.375, ((1, 4),))
    noise_steps = draw_noise_steps(jax.random.fold_in(jax.random.fold_in(arg_keys[9], part), 71), part)
    frame_mask = draw_frame_mask(jax.random.fold_in(jax.random.fold_in(arg_keys[9], part), 71), part)
    return dict(queries=queries, keys=keys, values=values, residual=residual, fresh_frame=fresh_frame, out_weight=out_weight, time_weight=time_weight, noise_steps=noise_steps, frame_mask=frame_mask)


def time_features(noise_steps):
    timestep = 1000.0 * (noise_steps.astype(jnp.float32) + 1.0) / STEPS
    half = FREQ // 2
    rates = jnp.exp(-math.log(10000.0) * jnp.arange(half).astype(jnp.float32) / half)
    angles = timestep[:, None] * rates[None, :]
    return jnp.concatenate([jnp.cos(angles), jnp.sin(angles)], axis=1)

def reference(queries, keys, values, residual, fresh_frame, out_weight, time_weight, noise_steps, frame_mask):
    width = HEADS * HD
    scale = 1.0 / math.sqrt(HD)
    blank = jnp.zeros((WIN - 1, TOK, width), keys.dtype)
    keys_padded = jnp.concatenate([blank, keys], axis=0)
    values_padded = jnp.concatenate([blank, values], axis=0)
    mask_padded = jnp.concatenate([jnp.zeros((FRAMES, WIN - 1), jnp.int32), frame_mask.astype(jnp.int32)], axis=1)

    def one_frame(frame):
        query_rows = lax.dynamic_index_in_dim(queries, frame, 0, keepdims=False).astype(jnp.float32).reshape(TOK, HEADS, HD)
        key_rows = lax.dynamic_slice_in_dim(keys_padded, frame, WIN, 0).astype(jnp.float32).reshape(WIN * TOK, HEADS, HD)
        value_rows = lax.dynamic_slice_in_dim(values_padded, frame, WIN, 0).astype(jnp.float32).reshape(WIN * TOK, HEADS, HD)
        mask_row = lax.dynamic_index_in_dim(mask_padded, frame, 0, keepdims=False)
        allowed = jnp.repeat(lax.dynamic_slice_in_dim(mask_row, frame, WIN, 0), TOK)
        scores = jnp.einsum('qhd,khd->hqk', query_rows, key_rows) * scale
        scores = jnp.where(allowed[None, None, :] > 0, scores, -1e+30)
        peak = lax.optimization_barrier(jnp.max(scores, axis=2, keepdims=True))
        lifted = jnp.exp(scores - peak)
        totals = lax.optimization_barrier(jnp.sum(lifted, axis=2))
        rounded = lax.optimization_barrier(lifted.astype(jnp.bfloat16)).astype(jnp.float32)
        mixed = jnp.einsum('hqk,khd->qhd', rounded, value_rows) / jnp.transpose(totals)[:, :, None]
        return mixed.reshape(TOK, width).astype(jnp.bfloat16)
    attention = lax.map(one_frame, jnp.arange(FRAMES, dtype=jnp.int32))
    projected = jnp.dot(attention.reshape(FRAMES * TOK, width), out_weight, preferred_element_type=jnp.float32).reshape(FRAMES, TOK, D)
    gate = jnp.dot(time_features(noise_steps), time_weight.astype(jnp.float32), precision=lax.Precision.HIGHEST)
    updated = (residual.astype(jnp.float32) + gate[:, None, :] * projected).astype(jnp.bfloat16)
    return jnp.concatenate([updated[1:], fresh_frame[None]], axis=0)
```

```python
import functools
import math

import jax
import jax.numpy as jnp
from jax import lax
from jax.experimental import pallas as pl
from jax.experimental.pallas import tpu as pltpu
from jax.sharding import PartitionSpec as P

HD = 128
FREQ = 256
STEPS = 50


def shifted(value, axis, steps):
    count = lax.axis_size(axis)
    leading, last = (max(0, -steps), min(count, count - steps))
    return lax.ppermute(value, axis, [(source, source + steps) for source in range(leading, last)])


def time_features(noise_steps):
    timestep = 1000.0 * (noise_steps.astype(jnp.float32) + 1.0) / STEPS
    half = FREQ // 2
    rates = jnp.exp(-math.log(10000.0) * jnp.arange(half).astype(jnp.float32) / half)
    angles = timestep[:, None] * rates[None, :]
    return jnp.concatenate([jnp.cos(angles), jnp.sin(angles)], axis=1)


def on_device(
    queries, keys, values, residual, fresh_frame, out_weight, time_weight, noise_steps, frame_mask
):
    query_local, key_local, value_local = (
        lax.all_to_all(queries, "head", split_axis=2, concat_axis=1, tiled=True),
        lax.all_to_all(keys, "head", split_axis=2, concat_axis=1, tiled=True),
        lax.all_to_all(values, "head", split_axis=2, concat_axis=1, tiled=True),
    )
    tokens = query_local.shape[1]
    heads_here = query_local.shape[2] // HD
    scale = 1.0 / math.sqrt(HD)
    query_heads = query_local[0].reshape(tokens, heads_here, HD)
    key_value = jnp.stack([key_local[0], value_local[0]], axis=0)
    frame = lax.axis_index("tm")
    frames_total = lax.axis_size("tm")
    window = min(8, frames_total)
    mask_row = frame_mask[0]
    columns = jnp.arange(mask_row.shape[0], dtype=jnp.int32)

    def allowed_at(offset):
        hits = jnp.sum(jnp.where(columns == frame - offset, mask_row, 0))
        return hits > 0

    def absorb(state, block, allowed):
        running_max, weight_sum, accumulated = state
        key_heads = block[0].reshape(tokens, heads_here, HD)
        value_heads = block[1].reshape(tokens, heads_here, HD)
        scores = (
            jnp.einsum("qhd,khd->hqk", query_heads, key_heads, preferred_element_type=jnp.float32)
            * scale
        )
        new_max = jnp.where(allowed, jnp.maximum(running_max, jnp.max(scores, axis=2)), running_max)
        lifted = jnp.where(allowed, jnp.exp(jnp.minimum(scores - new_max[:, :, None], 0.0)), 0.0)
        factor = jnp.exp(running_max - new_max)
        weight_sum = weight_sum * factor + jnp.sum(lifted, axis=2)
        rounded = lifted.astype(jnp.bfloat16)
        accumulated = accumulated * jnp.transpose(factor)[:, :, None] + jnp.einsum(
            "hqk,khd->qhd", rounded, value_heads, preferred_element_type=jnp.float32
        )
        return (new_max, weight_sum, accumulated)

    state = (
        jnp.full((heads_here, tokens), -1e30, jnp.float32),
        jnp.zeros((heads_here, tokens), jnp.float32),
        jnp.zeros((tokens, heads_here, HD), jnp.float32),
    )
    state = absorb(state, key_value, allowed_at(0))
    moving = key_value
    for offset in range(1, window):
        moving = shifted(moving, "tm", 1)
        state = absorb(state, moving, allowed_at(offset))
    running_max, weight_sum, accumulated = state
    attention = (
        (accumulated / jnp.transpose(weight_sum)[:, :, None])
        .reshape(tokens, heads_here * HD)
        .astype(jnp.bfloat16)
    )
    weight_cols = lax.all_gather(out_weight, "tm", axis=0, tiled=True)
    projected = jnp.dot(
        lax.all_gather(attention, "head", axis=1, tiled=True),
        weight_cols,
        preferred_element_type=jnp.float32,
    )
    gate = jnp.dot(
        time_features(noise_steps), time_weight.astype(jnp.float32), precision=lax.Precision.HIGHEST
    )
    updated = (residual[0].astype(jnp.float32) + gate * projected).astype(jnp.bfloat16)
    moved = shifted(updated, "tm", -1)
    rolled = jnp.where(frame == frames_total - 1, fresh_frame, moved)
    return rolled[None]


def fused_kernel(
    T, G, C, hp, pieces, groups,
    q_ref, k_ref, v_ref, res_ref, fresh_ref, w_ref, tw_ref, meta_ref,
    out_ref,
    qb, kb, vb, ab, mb, fb, gb, wb, w3, twb, rb, pb, ob, down_out, down_in, up_out, up_in,
    load_sem, out_sem, meta_send, meta_recv, qkv_send, qkv_recv, pass_send, pass_recv,
    ax_send, ax_recv, ac_send, ac_recv, dn_send, dn_recv, up_send, up_recv,
    w_send, w_recv, tr_send, tr_recv, raise_send,
):
    t = lax.axis_index("tm")
    h = lax.axis_index("head")
    group = lax.axis_index("groups")
    x = h // C
    c = lax.rem(h, C)
    H = G * C
    tl = q_ref.shape[1]
    cw = hp * HD
    tokens = tl * H
    half = G * tl
    nb = w_ref.shape[1] // pieces
    mask_row = FREQ // HD
    share = w_ref.shape[0] // groups
    top, low = T - 1, T - 2
    scale = 1.0 / math.sqrt(HD)

    def to(tt, hh):
        return dict(device_id={"tm": tt, "head": hh}, device_id_type=pl.DeviceIdType.MESH)

    def beside(dg):
        return dict(
            device_id={"groups": lax.rem(group + dg, groups)}, device_id_type=pl.DeviceIdType.MESH
        )

    def landed(ref, sem):
        pltpu.make_async_copy(ref, ref, sem).wait()

    def cols_of(p):
        return slice(p * nb, (p + 1) * nb)

    others = [(dt, dx) for dt in range(T) for dx in reversed(range(G)) if (dt, dx) != (0, 0)]

    loads = [
        pltpu.make_async_copy(tw_ref, twb, load_sem.at[0]),
        pltpu.make_async_copy(w_ref, wb, load_sem.at[1]),
        pltpu.make_async_copy(res_ref.at[0], rb, load_sem.at[2]),
    ]
    for copy in loads:
        copy.start()

    @pl.when(t == top)
    def _():
        pltpu.make_async_copy(fresh_ref, ob, load_sem.at[3]).start()

    barrier = pltpu.get_barrier_semaphore()
    for dt, dx in others:
        pl.semaphore_signal(
            barrier, inc=1, **to(lax.rem(t + dt, T), lax.rem(x + dx, G) * C + c)
        )
    for dc in range(1, C):
        pl.semaphore_signal(barrier, inc=1, **to(t, x * C + lax.rem(c + dc, C)))
    for dg in range(1, groups):
        pl.semaphore_signal(barrier, inc=1, **beside(dg))
    with jax.named_scope("barrier"):
        pl.semaphore_wait(barrier, len(others) + C - 1 + groups - 1)

    own_meta = pltpu.make_async_copy(meta_ref, mb.at[t], meta_recv.at[t])
    own_meta.start()
    meta_copies = []
    for dt in range(1, T):
        meta_copies.append(
            pltpu.make_async_remote_copy(
                src_ref=meta_ref, dst_ref=mb.at[t], send_sem=meta_send.at[dt],
                recv_sem=meta_recv.at[t], **to(lax.rem(t + dt, T), h),
            )
        )
        meta_copies[-1].start()

    sources = ((q_ref, qb), (k_ref, kb), (v_ref, vb))

    def slot(kind, s, f, xs):
        return qb.at[s, f, xs] if kind == 0 else sources[kind][1].at[s, f, xs * C + c]

    def block(kind, w, xx):
        column = pl.multiple_of((w * G + xx) * cw, HD)
        return sources[kind][0].at[0, :, pl.ds(column, cw)]

    def aim(f, key):
        w = min(key, top)
        if key < top:
            return w, 0, w
        return w, 1, (low if key == top and f < top else top)

    def outgoing(kind, f, key, dx):
        w, s, level = aim(f, key)
        xx = lax.rem(x + dx, G)
        return pltpu.make_async_remote_copy(
            src_ref=block(kind, w, xx), dst_ref=slot(kind, s, f, x),
            send_sem=qkv_send.at[kind, key, dx], recv_sem=qkv_recv.at[s, kind, f, x],
            **to(level, xx * C + c),
        )

    def own(kind, f, key):
        w, s, _ = aim(f, key)
        return pltpu.make_async_copy(
            block(kind, w, x), slot(kind, s, f, x), qkv_recv.at[s, kind, f, x]
        )

    def passed(kind, s, dc, f, xs):
        return pltpu.make_async_remote_copy(
            src_ref=slot(kind, s, f, xs), dst_ref=slot(kind, s, f, xs),
            send_sem=pass_send.at[s, kind - 1, dc, f, xs],
            recv_sem=pass_recv.at[s, kind - 1, dc, f, xs],
            **to(t, x * C + lax.rem(c + dc, C)),
        )

    def raised(kind, f, xs):
        return pltpu.make_async_remote_copy(
            src_ref=slot(kind, 1, f, xs), dst_ref=slot(kind, 1, f, xs),
            send_sem=raise_send.at[kind - 1, f, xs], recv_sem=qkv_recv.at[1, kind, f, xs],
            **to(top, h),
        )

    own_rows = pl.ds(pl.multiple_of(group * share, 8), share)

    def lift(p):
        return pltpu.make_async_remote_copy(
            src_ref=w_ref.at[own_rows, cols_of(p)], dst_ref=w3.at[own_rows, cols_of(p)],
            send_sem=w_send.at[p], recv_sem=w_recv.at[p], **to(low, h),
        )

    def trade(p, dg):
        return pltpu.make_async_remote_copy(
            src_ref=w3.at[own_rows, cols_of(p)], dst_ref=w3.at[own_rows, cols_of(p)],
            send_sem=tr_send.at[p, dg], recv_sem=tr_recv.at[p, dg], **beside(dg),
        )

    def across(s, r, dx):
        xx = lax.rem(x + dx, G)
        here = ab.at[s, r, c, :, pl.ds(pl.multiple_of(x * cw, HD), cw)]
        return pltpu.make_async_remote_copy(
            src_ref=here, dst_ref=here,
            send_sem=ax_send.at[s, r, dx], recv_sem=ax_recv.at[s, r, dx], **to(t, xx * C + c),
        )

    def aside(s, r, dx, dc):
        xs = lax.rem(x + dx, G)
        here = ab.at[s, r, c, :, pl.ds(pl.multiple_of(xs * cw, HD), cw)]
        return pltpu.make_async_remote_copy(
            src_ref=here, dst_ref=here,
            send_sem=ac_send.at[s, r, dx, dc], recv_sem=ac_recv.at[s, r, dx, dc],
            **to(t, x * C + lax.rem(c + dc, C)),
        )

    def down(level, r, p):
        return pltpu.make_async_remote_copy(
            src_ref=down_out.at[r, p], dst_ref=down_in.at[r, p],
            send_sem=dn_send.at[r, p], recv_sem=dn_recv.at[r, p], **to(level - 1, h),
        )

    def up(level, r, p):
        return pltpu.make_async_remote_copy(
            src_ref=up_out.at[r, p], dst_ref=up_in.at[r, p],
            send_sem=up_send.at[r, p], recv_sem=up_recv.at[r, p], **to(level + 1, h),
        )

    def gates():
        with jax.named_scope("loads"):
            for copy in loads:
                copy.wait()
        with jax.named_scope("meta"):
            fb[...] = jnp.zeros_like(fb)
            for f in range(T):
                landed(mb.at[f], meta_recv.at[f])
                for b in range(mask_row):
                    fb[f : f + 1, b * HD : (b + 1) * HD] = mb[f, b : b + 1, :]
        with jax.named_scope("gate"):
            gb[...] = jnp.dot(
                fb[...], twb[...].astype(jnp.float32),
                precision=lax.Precision.HIGHEST, preferred_element_type=jnp.float32,
            )

    def program(level):
        sent = []

        def send(kinds, key, dxs=tuple(reversed(range(G)))):
            for dx in dxs:
                for kind in kinds:
                    if kind == 0 and level == 0:
                        continue
                    if dx == 0 and aim(level, key)[2] == level:
                        own(kind, level, key).start()
                    else:
                        sent.append(outgoing(kind, level, key, dx))
                        sent[-1].start()

        def take(s, f, kinds=(1, 2)):
            for dx in range(G):
                xs = lax.rem(x + dx, G)
                for kind in kinds:
                    landed(slot(kind, s, f, xs), qkv_recv.at[s, kind, f, xs])
                    if kind > 0 and s == 1 and level == low and f < low:
                        sent.append(raised(kind, f, xs))
                        sent[-1].start()
                    if kind > 0:
                        for dc in range(1, C):
                            copy = passed(kind, s, dc, f, xs)
                            copy.start()
                            sent.append(copy)

        def settle(s, f):
            for xs in range(G):
                for kind in (1, 2):
                    for dc in range(1, C):
                        from_c = xs * C + lax.rem(c + C - dc, C)
                        landed(
                            sources[kind][1].at[s, f, from_c],
                            pass_recv.at[s, kind - 1, dc, f, xs],
                        )

        def attend(s, r):
            f = r + 1
            keys_here = (f + 1) * tokens
            allowed = jnp.concatenate(
                [
                    jnp.broadcast_to(mb[f, mask_row + g : mask_row + g + 1, 0:1], (1, tokens))
                    for g in range(f + 1)
                ],
                axis=1,
            )
            for j in range(hp):
                cols = slice(j * HD, (j + 1) * HD)
                query = qb[s, f, :, :, cols].reshape(half, HD)
                key = kb[s, 0 : f + 1, :, :, cols].reshape(keys_here, HD)
                value = vb[s, 0 : f + 1, :, :, cols].reshape(keys_here, HD)
                scores = (
                    lax.dot_general(
                        query, key, (((1,), (1,)), ((), ())), preferred_element_type=jnp.float32
                    )
                    * scale
                )
                scores = jnp.where(allowed > 0.5, scores, -1e30)
                peak = jnp.max(scores, axis=1, keepdims=True)
                lifted = jnp.exp(scores - peak)
                total = jnp.sum(lifted, axis=1, keepdims=True)
                mixed = jnp.dot(
                    lifted.astype(jnp.bfloat16), value, preferred_element_type=jnp.float32
                )
                place = pl.ds(pl.multiple_of(x * cw + j * HD, HD), HD)
                ab[s, r, c, :, place] = (mixed / total).astype(jnp.bfloat16)
            for dx in range(1, G):
                sent.append(across(s, r, dx))
                sent[-1].start()
            for dc in range(1, C):
                sent.append(aside(s, r, 0, dc))
                sent[-1].start()

        def hand_over(s, r):
            for dx in range(1, G):
                xs = lax.rem(x + G - dx, G)
                there = ab.at[s, r, c, :, pl.ds(pl.multiple_of(xs * cw, HD), cw)]
                landed(there, ax_recv.at[s, r, dx])
                for dc in range(1, C):
                    sent.append(aside(s, r, G - dx, dc))
                    sent[-1].start()

        def gathered(s, r):
            for dx in range(G):
                for dc in range(1, C):
                    xs, cs = lax.rem(x + dx, G), lax.rem(c + C - dc, C)
                    landed(
                        ab.at[s, r, cs, :, pl.ds(pl.multiple_of(xs * cw, HD), cw)],
                        ac_recv.at[s, r, dx, dc],
                    )

        def product(r, p):
            weights = {0: wb, 1: w3}
            if level == top:
                parts = ((1, wb),)
            elif level == low and r < low:
                parts = ((0, wb), (1, w3))
            else:
                parts = ((0, wb),)
            partial = 0.0
            for s, weight in parts:
                partial += jnp.dot(
                    ab[s, r].reshape(tokens, G * cw), weight[:, cols_of(p)],
                    preferred_element_type=jnp.float32,
                )
            partial = partial * gb[r + 1 : r + 2, cols_of(p)]
            if level == r + 1:
                moved = [
                    rb[(xs * C + cs) * tl : (xs * C + cs + 1) * tl, cols_of(p)]
                    for cs in range(C)
                    for xs in range(G)
                ]
                partial += jnp.concatenate(moved, axis=0).astype(jnp.float32)
            return partial

        def send_down(r, p, value):
            down_out[r, p] = value.astype(jnp.bfloat16)
            sent.append(down(level, r, p))
            sent[-1].start()

        def send_up(r, p, value):
            up_out[r, p] = value.astype(jnp.bfloat16)
            sent.append(up(level, r, p))
            sent[-1].start()

        def from_down(r, p):
            landed(down_in.at[r, p], dn_recv.at[r, p])
            return down_in[r, p].astype(jnp.float32)

        def from_up(r, p):
            landed(up_in.at[r, p], up_recv.at[r, p])
            return up_in[r, p].astype(jnp.float32)

        def finish(p):
            r = level
            total = pb[r, p] + from_down(r, p)
            if r > 0:
                total += from_up(r, p)
            total = total.astype(ob.dtype)
            for cs in range(C):
                for xs in range(G):
                    row, token = (cs * G + xs) * tl, (xs * C + cs) * tl
                    ob[token : token + tl, cols_of(p)] = total[row : row + tl]
            copy = pltpu.make_async_copy(
                ob.at[:, cols_of(p)], out_ref.at[:, cols_of(p)], out_sem.at[p]
            )
            copy.start()
            outs.append(copy)

        outs = []
        scope = jax.named_scope
        early = (3 * pieces) // 5
        order = [(low - 1, p) for p in range(early)]
        order += [(r, p) for r in range(low - 1) for p in range(pieces)]
        order += [(low - 1, p) for p in range(early, pieces)]
        known = set()

        if level == top:
            send((0, 1, 2), top)
            lifts = [lift(p) for p in range(pieces)]
            for p in range(early):
                lifts[p].start()
            for w in range(low):
                send((1, 2, 0), w)
            for p in range(early, pieces):
                lifts[p].start()
            send((1, 2, 0), low)
            pltpu.make_async_copy(fresh_ref, ob, load_sem.at[3]).wait()
            fresh_out = pltpu.make_async_copy(ob, out_ref, load_sem.at[3])
            fresh_out.start()
            gates()
            for f in range(T):
                with scope(f"take{f}"):
                    take(1, f)
            with scope("settle"):
                take(1, top, (0,))
                for f in range(T):
                    settle(1, f)
            with scope("attend"):
                attend(1, low)
            with scope("gather"):
                hand_over(1, low)
                gathered(1, low)
            with scope("project"):
                for p in range(pieces):
                    send_down(low, p, product(low, p))
            fresh_out.wait()
            for p in range(pieces):
                lifts[p].wait_send()
        elif level == low:
            for w in reversed(range(low)):
                send((1, 2, 0), w)
            send((1, 2, 0), low)
            send((1, 2, 0), top)
            send((1, 2), T)

            def exchange(p):
                with scope(f"trade{p}"):
                    landed(w3.at[own_rows, cols_of(p)], w_recv.at[p])
                for dg in range(1, groups):
                    sent.append(trade(p, dg))
                    sent[-1].start()

            def exchanged(p):
                for dg in range(1, groups):
                    theirs = pl.ds(
                        pl.multiple_of(lax.rem(group + groups - dg, groups) * share, 8), share
                    )
                    landed(w3.at[theirs, cols_of(p)], tr_recv.at[p, dg])

            gates()
            for p in range(early):
                exchange(p)
            for f in range(low + 1):
                for s in (0, 1):
                    with scope(f"take{f}{s}"):
                        take(s, f)
            for s in (0, 1):
                with scope(f"q{low}{s}"):
                    take(s, low, (0,))
                    for f in range(low + 1):
                        settle(s, f)
                with scope(f"attend{s}{low - 1}"):
                    attend(s, low - 1)
            for r in reversed(range(low - 1)):
                for s in (0, 1):
                    with scope(f"q{r + 1}{s}"):
                        take(s, r + 1, (0,))
                    with scope(f"attend{s}{r}"):
                        attend(s, r)
                    with scope(f"hand{s}{r + 1}"):
                        hand_over(s, r + 1)
            for s in (0, 1):
                with scope(f"hand{s}0"):
                    hand_over(s, 0)
            ready = set()
            weighed = set(range(early))
            for n, (r, p) in enumerate(order):
                if p >= early and len(weighed) < pieces:
                    for q in range(early, pieces):
                        exchange(q)
                        weighed.add(q)
                if r not in ready:
                    ready.add(r)
                    with scope(f"gather{r}"):
                        for s in (0, 1):
                            gathered(s, r)
                if p not in known:
                    known.add(p)
                    with scope(f"w{p}"):
                        exchanged(p)
                with scope(f"project{r}{p}"):
                    send_down(r, p, product(r, p))
            with scope("take3"):
                take(0, top)
                take(0, top, (0,))
                settle(0, top)
            with scope("attend3"):
                attend(0, low)
            with scope("gather3"):
                hand_over(0, low)
                gathered(0, low)
            with scope("project3"):
                for p in range(pieces):
                    pb[low, p] = product(low, p)
            for p in range(pieces):
                with scope(f"finish{p}"):
                    finish(p)
        else:
            send((1, 2), top)
            for w in range(level + 1, low + 1):
                send((1, 2), w)
            for w in range(level):
                send((1, 2, 0), w)
            for w in (top, *range(level + 1, low + 1)):
                send((0,), w)
            send((1, 2, 0), level)
            gates()
            for f in range(T - 1):
                with scope(f"take{f}"):
                    take(0, f)
                    if f > 0:
                        take(0, f, (0,))
            with scope("settle"):
                for f in range(T - 1):
                    settle(0, f)
            early = sorted(range(T - 2), key=lambda r: -r if level == 0 else r)
            for r in early:
                with scope(f"attend{r}"):
                    attend(0, r)
            for r in early:
                with scope(f"gather{r}"):
                    hand_over(0, r)
                    gathered(0, r)
                with scope(f"project{r}"):
                    for p in range(pieces):
                        value = product(r, p)
                        if level == 0 and r > 0:
                            send_up(r, p, value)
                        else:
                            pb[r, p] = value
            with scope("take3"):
                take(0, top)
                take(0, top, (0,))
                settle(0, top)
            with scope("attend3"):
                attend(0, low)
            with scope("gather3"):
                hand_over(0, low)
                gathered(0, low)
            with scope("project3"):
                for p in range(pieces):
                    value = product(low, p)
                    if level == 0:
                        send_up(low, p, value)
                    else:
                        pb[low, p] = value
            for r, p in order:
                if r > level:
                    continue
                if r == level:
                    with scope(f"finish{p}"):
                        finish(p)
                    continue
                if r == 0:
                    for q in reversed(range(level + 1, T - 1)):
                        with scope(f"up{q}{p}"):
                            send_up(q, p, pb[q, p] + from_up(q, p))
                with scope(f"down{r}{p}"):
                    send_down(r, p, pb[r, p] + from_down(r, p))
        with scope("outs"):
            for copy in outs:
                copy.wait()
        with scope("sends"):
            for copy in meta_copies:
                copy.wait_send()
            for copy in sent:
                copy.wait_send()

    for level in range(T):
        pl.when(t == level)(functools.partial(program, level))


def fused(T, H, heads, groups):
    def on_device_fused(
        queries, keys, values, residual, fresh_frame, out_weight, time_weight, noise_steps, frame_mask
    ):
        level_heads = heads // T
        G = math.gcd(level_heads, H)
        C = H // G
        hp = level_heads // G
        tl = queries.shape[1]
        tokens = tl * H
        width = out_weight.shape[1]
        pieces = width // (2 * HD)
        nb = width // pieces
        meta_rows = -(-(FREQ // HD + T) // 8) * 8
        meta = jnp.concatenate(
            [
                time_features(noise_steps).reshape(FREQ // HD, HD),
                jnp.broadcast_to(frame_mask[0].astype(jnp.float32)[:, None], (T, HD)),
                jnp.zeros((meta_rows - FREQ // HD - T, HD), jnp.float32),
            ],
            axis=0,
        )
        cw = hp * HD
        bf16, f32 = jnp.bfloat16, jnp.float32
        dma = pltpu.SemaphoreType.DMA
        chunk = (T - 1, pieces, tokens, nb)
        out = pl.pallas_call(
            functools.partial(fused_kernel, T, G, C, hp, pieces, groups),
            out_shape=jax.ShapeDtypeStruct((tokens, width), bf16),
            in_specs=[pl.BlockSpec(memory_space=pl.ANY)] * 8,
            out_specs=pl.BlockSpec(memory_space=pl.ANY),
            scratch_shapes=[
                pltpu.VMEM((2, T, G, tl, cw), bf16),
                pltpu.VMEM((2, T, H, tl, cw), bf16),
                pltpu.VMEM((2, T, H, tl, cw), bf16),
                pltpu.VMEM((2, T - 1, C, G * tl, G * cw), bf16),
                pltpu.VMEM((T, meta_rows, HD), f32),
                pltpu.VMEM((8, FREQ), f32),
                pltpu.VMEM((8, width), f32),
                pltpu.VMEM(out_weight.shape, bf16),
                pltpu.VMEM(out_weight.shape, bf16),
                pltpu.VMEM(time_weight.shape, bf16),
                pltpu.VMEM((tokens, width), bf16),
                pltpu.VMEM(chunk, f32),
                pltpu.VMEM((tokens, width), bf16),
                pltpu.VMEM(chunk, bf16),
                pltpu.VMEM(chunk, bf16),
                pltpu.VMEM(chunk, bf16),
                pltpu.VMEM(chunk, bf16),
                dma((4,)),
                dma((pieces,)),
                dma((T,)),
                dma((T,)),
                dma((3, T + 1, G)),
                dma((2, 3, T, G)),
                dma((2, 2, C, T, G)),
                dma((2, 2, C, T, G)),
                dma((2, T - 1, G)),
                dma((2, T - 1, G)),
                dma((2, T - 1, G, C)),
                dma((2, T - 1, G, C)),
                dma((T - 1, pieces)),
                dma((T - 1, pieces)),
                dma((T - 1, pieces)),
                dma((T - 1, pieces)),
                dma((pieces,)),
                dma((pieces,)),
                dma((pieces, groups)),
                dma((pieces, groups)),
                dma((2, T, G)),
            ],
            compiler_params=pltpu.CompilerParams(
                collective_id=0, has_side_effects=True, vmem_limit_bytes=56 * 1024 * 1024
            ),
        )(queries, keys, values, residual, fresh_frame, out_weight, time_weight, meta)
        return out[None]

    return on_device_fused


def solution(mesh):
    placed = (
        P(("groups", "tm"), "head", None),
        P(("groups", "tm"), "head", None),
        P(("groups", "tm"), "head", None),
        P(("groups", "tm"), None, "head"),
        P("groups", "head"),
        P("tm", "head"),
        P(None, "head"),
        P(("groups", "tm")),
        P(("groups", "tm"), None),
    )
    def whole(*args):
        frames, spread = mesh.shape["tm"], mesh.shape["head"]
        heads = args[0].shape[2] // HD
        fits = 2 < frames <= 4 and heads % frames == 0 and args[5].shape[1] % (spread * 2 * HD) == 0
        return jax.shard_map(
            fused(frames, spread, heads, mesh.shape["groups"]) if fits else on_device,
            mesh=mesh,
            in_specs=placed,
            out_specs=P(("groups", "tm"), None, "head"),
            check_vma=False,
        )(*args)

    return whole
```

```python
import functools
import math

import jax
import jax.numpy as jnp
from jax import lax
from jax.experimental import pallas as pl
from jax.experimental.pallas import tpu as pltpu
from jax.sharding import PartitionSpec as P

HD = 128
FREQ = 256
STEPS = 50


def shifted(value, axis, steps):
    count = lax.axis_size(axis)
    leading, last = (max(0, -steps), min(count, count - steps))
    return lax.ppermute(value, axis, [(source, source + steps) for source in range(leading, last)])


def time_features(noise_steps):
    timestep = 1000.0 * (noise_steps.astype(jnp.float32) + 1.0) / STEPS
    half = FREQ // 2
    rates = jnp.exp(-math.log(10000.0) * jnp.arange(half).astype(jnp.float32) / half)
    angles = timestep[:, None] * rates[None, :]
    return jnp.concatenate([jnp.cos(angles), jnp.sin(angles)], axis=1)


def on_device(
    queries, keys, values, residual, fresh_frame, out_weight, time_weight, noise_steps, frame_mask
):
    query_local, key_local, value_local = (
        lax.all_to_all(queries, "head", split_axis=2, concat_axis=1, tiled=True),
        lax.all_to_all(keys, "head", split_axis=2, concat_axis=1, tiled=True),
        lax.all_to_all(values, "head", split_axis=2, concat_axis=1, tiled=True),
    )
    tokens = query_local.shape[1]
    heads_here = query_local.shape[2] // HD
    scale = 1.0 / math.sqrt(HD)
    query_heads = query_local[0].reshape(tokens, heads_here, HD)
    key_value = jnp.stack([key_local[0], value_local[0]], axis=0)
    frame = lax.axis_index("tm")
    frames_total = lax.axis_size("tm")
    window = min(8, frames_total)
    mask_row = frame_mask[0]
    columns = jnp.arange(mask_row.shape[0], dtype=jnp.int32)

    def allowed_at(offset):
        hits = jnp.sum(jnp.where(columns == frame - offset, mask_row, 0))
        return hits > 0

    def absorb(state, block, allowed):
        running_max, weight_sum, accumulated = state
        key_heads = block[0].reshape(tokens, heads_here, HD)
        value_heads = block[1].reshape(tokens, heads_here, HD)
        scores = (
            jnp.einsum("qhd,khd->hqk", query_heads, key_heads, preferred_element_type=jnp.float32)
            * scale
        )
        new_max = jnp.where(allowed, jnp.maximum(running_max, jnp.max(scores, axis=2)), running_max)
        lifted = jnp.where(allowed, jnp.exp(jnp.minimum(scores - new_max[:, :, None], 0.0)), 0.0)
        factor = jnp.exp(running_max - new_max)
        weight_sum = weight_sum * factor + jnp.sum(lifted, axis=2)
        rounded = lifted.astype(jnp.bfloat16)
        accumulated = accumulated * jnp.transpose(factor)[:, :, None] + jnp.einsum(
            "hqk,khd->qhd", rounded, value_heads, preferred_element_type=jnp.float32
        )
        return (new_max, weight_sum, accumulated)

    state = (
        jnp.full((heads_here, tokens), -1e30, jnp.float32),
        jnp.zeros((heads_here, tokens), jnp.float32),
        jnp.zeros((tokens, heads_here, HD), jnp.float32),
    )
    state = absorb(state, key_value, allowed_at(0))
    moving = key_value
    for offset in range(1, window):
        moving = shifted(moving, "tm", 1)
        state = absorb(state, moving, allowed_at(offset))
    running_max, weight_sum, accumulated = state
    attention = (
        (accumulated / jnp.transpose(weight_sum)[:, :, None])
        .reshape(tokens, heads_here * HD)
        .astype(jnp.bfloat16)
    )
    weight_cols = lax.all_gather(out_weight, "tm", axis=0, tiled=True)
    projected = jnp.dot(
        lax.all_gather(attention, "head", axis=1, tiled=True),
        weight_cols,
        preferred_element_type=jnp.float32,
    )
    gate = jnp.dot(
        time_features(noise_steps), time_weight.astype(jnp.float32), precision=lax.Precision.HIGHEST
    )
    updated = (residual[0].astype(jnp.float32) + gate * projected).astype(jnp.bfloat16)
    moved = shifted(updated, "tm", -1)
    rolled = jnp.where(frame == frames_total - 1, fresh_frame, moved)
    return rolled[None]


def fused_kernel(
    T, G, C, hp, pieces, groups,
    q_ref, k_ref, v_ref, res_ref, fresh_ref, w_ref, tw_ref, meta_ref,
    out_ref,
    qb, kv, ab, mb, fb, gb, wb, w3, twb, rb, pb, down_out, down_in, up_out, up_in,
    load_sem, meta_send, meta_recv, kv_send, q_send, kv_recv, q_recv, pass_send, pass_recv,
    raise_send, ax_send, ax_recv, ac_send, ac_recv, dn_send, dn_recv, up_send, up_recv,
    w_send, w_recv, tr_send, tr_recv,
):
    t = lax.axis_index("tm")
    h = lax.axis_index("head")
    group = lax.axis_index("groups")
    x = h // C
    c = lax.rem(h, C)
    H = G * C
    tl = q_ref.shape[1]
    cw = hp * HD
    tokens = tl * H
    half = G * tl
    nb = w_ref.shape[1] // pieces
    mask_row = FREQ // HD
    share = w_ref.shape[0] // groups
    top, low = T - 1, T - 2
    scale = 1.0 / math.sqrt(HD)

    def to(tt, hh):
        return dict(device_id={"tm": tt, "head": hh}, device_id_type=pl.DeviceIdType.MESH)

    def beside(dg):
        return dict(
            device_id={"groups": lax.rem(group + dg, groups)}, device_id_type=pl.DeviceIdType.MESH
        )

    def landed(ref, sem):
        pltpu.make_async_copy(ref, ref, sem).wait()

    def cols_of(p):
        return slice(p * nb, (p + 1) * nb)

    others = [(dt, dx) for dt in range(T) for dx in reversed(range(G)) if (dt, dx) != (0, 0)]

    loads = [
        pltpu.make_async_copy(tw_ref, twb, load_sem.at[0]),
        pltpu.make_async_copy(w_ref, wb, load_sem.at[1]),
        pltpu.make_async_copy(res_ref.at[0], rb, load_sem.at[2]),
    ]
    for copy in loads:
        copy.start()

    @pl.when(t == top)
    def _():
        pltpu.make_async_copy(fresh_ref, out_ref, load_sem.at[3]).start()

    barrier = pltpu.get_barrier_semaphore()
    for dt, dx in others:
        pl.semaphore_signal(
            barrier, inc=1, **to(lax.rem(t + dt, T), lax.rem(x + dx, G) * C + c)
        )
    for dc in range(1, C):
        pl.semaphore_signal(barrier, inc=1, **to(t, x * C + lax.rem(c + dc, C)))
    for dg in range(1, groups):
        pl.semaphore_signal(barrier, inc=1, **beside(dg))
    with jax.named_scope("barrier"):
        pl.semaphore_wait(barrier, len(others) + C - 1 + groups - 1)

    own_meta = pltpu.make_async_copy(meta_ref, mb.at[t], meta_recv.at[0])
    own_meta.start()
    for dt in range(1, T):
        pltpu.make_async_remote_copy(
            src_ref=meta_ref, dst_ref=mb.at[t], send_sem=meta_send.at[0],
            recv_sem=meta_recv.at[0], **to(lax.rem(t + dt, T), h),
        ).start()

    sources = (q_ref, k_ref, v_ref)

    def slot(kind, s, f, xs):
        return qb.at[s * T + f, xs] if kind == 0 else kv.at[s * T + f, c, kind - 1, xs]

    def sems(kind, s, f):
        return (q_send if kind == 0 else kv_send).at[0], (q_recv if kind == 0 else kv_recv).at[s * T + f]

    def block(kind, w, xx):
        column = pl.multiple_of((w * G + xx) * cw, HD)
        return sources[kind].at[0, :, pl.ds(column, cw)]

    def aim(f, key):
        w = min(key, top)
        if key < top:
            return w, 0, w
        return w, 1, (low if key == top and f < top else top)

    def outgoing(kind, f, key, dx):
        w, s, level = aim(f, key)
        xx = lax.rem(x + dx, G)
        leaves, lands = sems(kind, s, f)
        return pltpu.make_async_remote_copy(
            src_ref=block(kind, w, xx), dst_ref=slot(kind, s, f, x),
            send_sem=leaves, recv_sem=lands, **to(level, xx * C + c),
        )

    def own(kind, f, key):
        w, s, _ = aim(f, key)
        return pltpu.make_async_copy(block(kind, w, x), slot(kind, s, f, x), sems(kind, s, f)[1])

    def passed(i, dc):
        return pltpu.make_async_remote_copy(
            src_ref=kv.at[i, c], dst_ref=kv.at[i, c],
            send_sem=pass_send.at[0], recv_sem=pass_recv.at[i, dc - 1],
            **to(t, x * C + lax.rem(c + dc, C)),
        )

    def raised(i):
        return pltpu.make_async_remote_copy(
            src_ref=kv.at[i, c], dst_ref=kv.at[i, c],
            send_sem=raise_send.at[0], recv_sem=kv_recv.at[i], **to(top, h),
        )

    own_rows = pl.ds(pl.multiple_of(group * share, 8), share)

    def lift(p):
        return pltpu.make_async_remote_copy(
            src_ref=w_ref.at[own_rows, cols_of(p)], dst_ref=w3.at[own_rows, cols_of(p)],
            send_sem=w_send.at[0], recv_sem=w_recv.at[p], **to(low, h),
        )

    def trade(p, dg):
        return pltpu.make_async_remote_copy(
            src_ref=w3.at[own_rows, cols_of(p)], dst_ref=w3.at[own_rows, cols_of(p)],
            send_sem=tr_send.at[0], recv_sem=tr_recv.at[p, dg - 1], **beside(dg),
        )

    def mine(i, column, size):
        return ab.at[i, c, :, pl.ds(pl.multiple_of(column, HD), size)]

    def across(i, j, dx):
        here = mine(i, x * cw + j * HD, HD)
        return pltpu.make_async_remote_copy(
            src_ref=here, dst_ref=here, send_sem=ax_send.at[0], recv_sem=ax_recv.at[i, dx - 1],
            **to(t, lax.rem(x + dx, G) * C + c),
        )

    def aside(i, xs, dc):
        here = mine(i, xs * cw, cw)
        return pltpu.make_async_remote_copy(
            src_ref=here, dst_ref=here, send_sem=ac_send.at[0], recv_sem=ac_recv.at[i, dc - 1],
            **to(t, x * C + lax.rem(c + dc, C)),
        )

    def spot(r):
        return r % (T - 2)

    def down(level, r, p):
        return pltpu.make_async_remote_copy(
            src_ref=down_out.at[spot(r), p], dst_ref=down_in.at[spot(r), p],
            send_sem=dn_send.at[0], recv_sem=dn_recv.at[spot(r), p], **to(level - 1, h),
        )

    def up(level, r, p):
        return pltpu.make_async_remote_copy(
            src_ref=up_out.at[spot(r), p], dst_ref=up_in.at[spot(r), p],
            send_sem=up_send.at[0], recv_sem=up_recv.at[spot(r), p], **to(level + 1, h),
        )

    def gates():
        with jax.named_scope("loads"):
            for copy in loads:
                copy.wait()
        with jax.named_scope("meta"):
            fb[...] = jnp.zeros_like(fb)
            landed(mb, meta_recv.at[0])
            for f in range(T):
                for b in range(mask_row):
                    fb[f : f + 1, b * HD : (b + 1) * HD] = mb[f, b : b + 1, :]
        with jax.named_scope("gate"):
            gb[...] = jnp.dot(
                fb[...], twb[...].astype(jnp.float32),
                precision=lax.Precision.HIGHEST, preferred_element_type=jnp.float32,
            )

    def program(level):
        count = dict(kv=0, q=0, passed=0, raised=0, ax=0, ac=0, down=0, up=0, traded=0)

        def send(kinds, key, dxs=tuple(reversed(range(G)))):
            for dx in dxs:
                for kind in kinds:
                    if kind == 0 and level == 0:
                        continue
                    if dx == 0 and aim(level, key)[2] == level:
                        own(kind, level, key).start()
                    else:
                        outgoing(kind, level, key, dx).start()
                        count["q" if kind == 0 else "kv"] += 1

        def take(s, f):
            i = s * T + f
            landed(kv.at[i, c], kv_recv.at[i])
            for dc in range(1, C):
                passed(i, dc).start()
                count["passed"] += 1
            if s == 1 and level == low and f < low:
                raised(i).start()
                count["raised"] += 1

        def take_queries(s, f):
            landed(qb.at[s * T + f], q_recv.at[s * T + f])

        def settle(s, f):
            i = s * T + f
            for dc in range(1, C):
                landed(kv.at[i, lax.rem(c + C - dc, C)], pass_recv.at[i, dc - 1])

        def attend(s, r):
            f = r + 1
            i = s * (T - 1) + r
            keys_here = (f + 1) * tokens
            allowed = jnp.concatenate(
                [
                    jnp.broadcast_to(mb[f, mask_row + g : mask_row + g + 1, 0:1], (1, tokens))
                    for g in range(f + 1)
                ],
                axis=1,
            )
            for j in range(hp):
                cols = slice(j * HD, (j + 1) * HD)
                query = qb[s * T + f, :, :, cols].reshape(half, HD)
                key = kv[s * T : s * T + f + 1, :, 0, :, :, cols].reshape(keys_here, HD)
                value = kv[s * T : s * T + f + 1, :, 1, :, :, cols].reshape(keys_here, HD)
                scores = (
                    lax.dot_general(
                        query, key, (((1,), (1,)), ((), ())), preferred_element_type=jnp.float32
                    )
                    * scale
                )
                scores = jnp.where(allowed > 0.5, scores, -1e30)
                peak = jnp.max(scores, axis=1, keepdims=True)
                lifted = jnp.exp(scores - peak)
                total = jnp.sum(lifted, axis=1, keepdims=True)
                mixed = jnp.dot(
                    lifted.astype(jnp.bfloat16), value, preferred_element_type=jnp.float32
                )
                place = pl.ds(pl.multiple_of(x * cw + j * HD, HD), HD)
                ab[i, c, :, place] = (mixed / total).astype(jnp.bfloat16)
                for dx in range(1, G):
                    across(i, j, dx).start()
                    count["ax"] += 1
            for dc in range(1, C):
                aside(i, x, dc).start()
                count["ac"] += 1

        def hand_over(s, r):
            i = s * (T - 1) + r
            for dx in range(1, G):
                xs = lax.rem(x + G - dx, G)
                landed(mine(i, xs * cw, cw), ax_recv.at[i, dx - 1])
                for dc in range(1, C):
                    aside(i, xs, dc).start()
                    count["ac"] += 1

        def gathered(s, r):
            i = s * (T - 1) + r
            for dc in range(1, C):
                landed(ab.at[i, lax.rem(c + C - dc, C)], ac_recv.at[i, dc - 1])

        def product(r, p):
            if level == top:
                parts = ((1, wb),)
            elif level == low and r < low:
                parts = ((0, wb), (1, w3))
            else:
                parts = ((0, wb),)
            partial = 0.0
            for s, weight in parts:
                partial += jnp.dot(
                    ab[s * (T - 1) + r].reshape(tokens, G * cw), weight[:, cols_of(p)],
                    preferred_element_type=jnp.float32,
                )
            partial = partial * gb[r + 1 : r + 2, cols_of(p)]
            if level == r + 1:
                moved = [
                    rb[(xs * C + cs) * tl : (xs * C + cs + 1) * tl, cols_of(p)]
                    for cs in range(C)
                    for xs in range(G)
                ]
                partial += jnp.concatenate(moved, axis=0).astype(jnp.float32)
            return partial

        def send_down(r, p, value):
            down_out[spot(r), p] = value.astype(jnp.bfloat16)
            down(level, r, p).start()
            count["down"] += 1

        def send_up(r, p, value):
            up_out[spot(r), p] = value.astype(jnp.bfloat16)
            up(level, r, p).start()
            count["up"] += 1

        def from_down(r, p):
            landed(down_in.at[spot(r), p], dn_recv.at[spot(r), p])
            return down_in[spot(r), p].astype(jnp.float32)

        def from_up(r, p):
            landed(up_in.at[spot(r), p], up_recv.at[spot(r), p])
            return up_in[spot(r), p].astype(jnp.float32)

        def finish(p):
            r = level
            total = pb[r, p] + from_down(r, p)
            if r > 0:
                total += from_up(r, p)
            total = total.astype(out_ref.dtype)
            for cs in range(C):
                for xs in range(G):
                    row, token = (cs * G + xs) * tl, (xs * C + cs) * tl
                    out_ref[token : token + tl, cols_of(p)] = total[row : row + tl]

        scope = jax.named_scope
        early = (3 * pieces) // 5
        order = [(low - 1, p) for p in range(early)]
        order += [(r, p) for r in range(low - 1) for p in range(pieces)]
        order += [(low - 1, p) for p in range(early, pieces)]

        if level == top:
            send((0, 1, 2), top)
            lifts = [lift(p) for p in range(pieces)]
            for p in range(early):
                lifts[p].start()
            for w in range(low):
                send((1, 2, 0), w)
            for p in range(early, pieces):
                lifts[p].start()
            send((1, 2, 0), low)
            gates()
            for f in range(T):
                with scope(f"take{f}"):
                    take(1, f)
            with scope("settle"):
                take_queries(1, top)
                for f in range(T):
                    settle(1, f)
            with scope("attend"):
                attend(1, low)
            with scope("gather"):
                hand_over(1, low)
                gathered(1, low)
            with scope("project"):
                for p in range(pieces):
                    send_down(low, p, product(low, p))
            pltpu.make_async_copy(fresh_ref, out_ref, load_sem.at[3]).wait()
            landed(w3.at[own_rows], w_send.at[0])
        elif level == low:
            for w in reversed(range(low)):
                send((1, 2, 0), w)
            send((1, 2, 0), low)
            send((1, 2, 0), top)
            send((1, 2), T)

            def exchange(p):
                with scope(f"trade{p}"):
                    landed(w3.at[own_rows, cols_of(p)], w_recv.at[p])
                for dg in range(1, groups):
                    trade(p, dg).start()

            def exchanged(p):
                for dg in range(1, groups):
                    theirs = pl.ds(
                        pl.multiple_of(lax.rem(group + groups - dg, groups) * share, 8), share
                    )
                    landed(w3.at[theirs, cols_of(p)], tr_recv.at[p, dg - 1])

            gates()
            for p in range(early):
                exchange(p)
            for f in (*range(low - 1), low, low - 1):
                for s in (0, 1):
                    with scope(f"take{f}{s}"):
                        take(s, f)
            for s in (0, 1):
                with scope(f"q{low}{s}"):
                    take_queries(s, low)
                    for f in range(low + 1):
                        settle(s, f)
                with scope(f"attend{s}{low - 1}"):
                    attend(s, low - 1)
            for r in reversed(range(low - 1)):
                for s in (0, 1):
                    with scope(f"q{r + 1}{s}"):
                        take_queries(s, r + 1)
                    with scope(f"attend{s}{r}"):
                        attend(s, r)
                    with scope(f"hand{s}{r + 1}"):
                        hand_over(s, r + 1)
            ready = set()
            known = set()
            swapped = False

            def last_frame():
                with scope("take3"):
                    take(0, top)
                    take_queries(0, top)
                    settle(0, top)
                with scope("attend3"):
                    attend(0, low)

            for r, p in order:
                if p >= early and not swapped:
                    swapped = True
                    for q in range(early, pieces):
                        exchange(q)
                if r not in ready:
                    ready.add(r)
                    with scope(f"gather{r}"):
                        for s in (0, 1):
                            if r == 0 and low > 1 or low == 1:
                                hand_over(s, r)
                        for s in (0, 1):
                            gathered(s, r)
                if p not in known:
                    known.add(p)
                    if p == pieces - 1:
                        last_frame()
                    with scope(f"w{p}"):
                        exchanged(p)
                with scope(f"project{r}{p}"):
                    send_down(r, p, product(r, p))
            with scope("gather3"):
                hand_over(0, low)
                gathered(0, low)
            with scope("project3"):
                for p in range(pieces):
                    pb[low, p] = product(low, p)
            for p in range(pieces):
                with scope(f"finish{p}"):
                    finish(p)
            landed(w3.at[own_rows], tr_send.at[0])
        else:
            send((1, 2), top)
            for w in range(level + 1, low + 1):
                send((1, 2), w)
            for w in range(level):
                send((1, 2, 0), w)
            for w in (top, *range(level + 1, low + 1)):
                send((0,), w)
            send((1, 2, 0), level)
            gates()
            for f in range(T - 1):
                with scope(f"take{f}"):
                    take(0, f)
                    if f > 0:
                        take_queries(0, f)
            with scope("settle"):
                for f in range(T - 1):
                    settle(0, f)
            early = sorted(range(T - 2), key=lambda r: -r if level == 0 else r)
            for r in early:
                with scope(f"attend{r}"):
                    attend(0, r)
            for r in early:
                with scope(f"gather{r}"):
                    hand_over(0, r)
                    gathered(0, r)
                with scope(f"project{r}"):
                    for p in range(pieces):
                        value = product(r, p)
                        if level == 0 and r > 0:
                            send_up(r, p, value)
                        else:
                            pb[r, p] = value
            with scope("take3"):
                take(0, top)
                take_queries(0, top)
                settle(0, top)
            with scope("attend3"):
                attend(0, low)
            with scope("gather3"):
                hand_over(0, low)
                gathered(0, low)
            with scope("project3"):
                for p in range(pieces):
                    value = product(low, p)
                    if level == 0:
                        send_up(low, p, value)
                    else:
                        pb[low, p] = value
            for r, p in order:
                if r > level:
                    continue
                if r == level:
                    with scope(f"finish{p}"):
                        finish(p)
                    continue
                if r == 0:
                    for q in reversed(range(level + 1, T - 1)):
                        with scope(f"up{q}{p}"):
                            send_up(q, p, pb[q, p] + from_up(q, p))
                with scope(f"down{r}{p}"):
                    send_down(r, p, pb[r, p] + from_down(r, p))
        with scope("sends"):
            landed(mb.at[: T - 1], meta_send.at[0])
            landed(kv.at[: count["kv"] // 2, 0, :, 0], kv_send.at[0])
            if count["q"]:
                landed(qb.at[: count["q"], 0], q_send.at[0])
            if count["passed"]:
                landed(kv.at[: count["passed"], 0], pass_send.at[0])
            if count["raised"]:
                landed(kv.at[: count["raised"], 0], raise_send.at[0])
            if count["ax"]:
                landed(ab.at[: count["ax"] // hp, 0, :, :cw], ax_send.at[0])
            if count["ac"]:
                landed(ab.at[: count["ac"] // G, 0], ac_send.at[0])
            if count["down"]:
                landed(down_out.at[: count["down"] // pieces], dn_send.at[0])
            if count["up"]:
                landed(up_out.at[: count["up"] // pieces], up_send.at[0])

    for level in range(T):
        pl.when(t == level)(functools.partial(program, level))


def fused(T, H, heads, groups):
    def on_device_fused(
        queries, keys, values, residual, fresh_frame, out_weight, time_weight, noise_steps, frame_mask
    ):
        level_heads = heads // T
        G = math.gcd(level_heads, H)
        C = H // G
        hp = level_heads // G
        tl = queries.shape[1]
        tokens = tl * H
        width = out_weight.shape[1]
        pieces = width // (2 * HD)
        nb = width // pieces
        meta_rows = -(-(FREQ // HD + T) // 8) * 8
        meta = jnp.concatenate(
            [
                time_features(noise_steps).reshape(FREQ // HD, HD),
                jnp.broadcast_to(frame_mask[0].astype(jnp.float32)[:, None], (T, HD)),
                jnp.zeros((meta_rows - FREQ // HD - T, HD), jnp.float32),
            ],
            axis=0,
        )
        cw = hp * HD
        bf16, f32 = jnp.bfloat16, jnp.float32
        dma = pltpu.SemaphoreType.DMA
        chunk = (T - 2, pieces, tokens, nb)
        out = pl.pallas_call(
            functools.partial(fused_kernel, T, G, C, hp, pieces, groups),
            out_shape=jax.ShapeDtypeStruct((tokens, width), bf16),
            in_specs=[pl.BlockSpec(memory_space=pltpu.HBM)] * 7
            + [pl.BlockSpec(memory_space=pl.ANY)],
            out_specs=pl.BlockSpec(memory_space=pltpu.VMEM),
            scratch_shapes=[
                pltpu.VMEM((2 * T, G, tl, cw), bf16),
                pltpu.VMEM((2 * T, C, 2, G, tl, cw), bf16),
                pltpu.VMEM((2 * (T - 1), C, G * tl, G * cw), bf16),
                pltpu.VMEM((T, meta_rows, HD), f32),
                pltpu.VMEM((8, FREQ), f32),
                pltpu.VMEM((8, width), f32),
                pltpu.VMEM(out_weight.shape, bf16),
                pltpu.VMEM(out_weight.shape, bf16),
                pltpu.VMEM(time_weight.shape, bf16),
                pltpu.VMEM((tokens, width), bf16),
                pltpu.VMEM((T - 1, pieces, tokens, nb), f32),
                pltpu.VMEM(chunk, bf16),
                pltpu.VMEM(chunk, bf16),
                pltpu.VMEM(chunk, bf16),
                pltpu.VMEM(chunk, bf16),
                dma((4,)),
                dma((1,)),
                dma((1,)),
                dma((1,)),
                dma((1,)),
                dma((2 * T,)),
                dma((2 * T,)),
                dma((1,)),
                dma((2 * T, C - 1)),
                dma((1,)),
                dma((1,)),
                dma((2 * (T - 1), G - 1)),
                dma((1,)),
                dma((2 * (T - 1), C - 1)),
                dma((1,)),
                dma((T - 2, pieces)),
                dma((1,)),
                dma((T - 2, pieces)),
                dma((1,)),
                dma((pieces,)),
                dma((1,)),
                dma((pieces, groups - 1)),
            ],
            compiler_params=pltpu.CompilerParams(
                collective_id=0, has_side_effects=True, vmem_limit_bytes=32 * 1024 * 1024
            ),
        )(
            *(
                pltpu.with_memory_space_constraint(array, pltpu.HBM)
                for array in (
                    queries, keys, values, residual, fresh_frame, out_weight, time_weight
                )
            ),
            meta,
        )
        return out[None]

    return on_device_fused


def solution(mesh):
    placed = (
        P(("groups", "tm"), "head", None),
        P(("groups", "tm"), "head", None),
        P(("groups", "tm"), "head", None),
        P(("groups", "tm"), None, "head"),
        P("groups", "head"),
        P("tm", "head"),
        P(None, "head"),
        P(("groups", "tm")),
        P(("groups", "tm"), None),
    )
    def whole(*args):
        frames, spread = mesh.shape["tm"], mesh.shape["head"]
        heads = args[0].shape[2] // HD
        fits = 2 < frames <= 4 and heads % frames == 0 and args[5].shape[1] % (spread * 2 * HD) == 0
        return jax.shard_map(
            fused(frames, spread, heads, mesh.shape["groups"]) if fits else on_device,
            mesh=mesh,
            in_specs=placed,
            out_specs=P(("groups", "tm"), None, "head"),
            check_vma=False,
        )(*args)

    return whole
```

```python
import functools
import math

import jax
import jax.numpy as jnp
from jax import lax
from jax.experimental import pallas as pl
from jax.experimental.pallas import tpu as pltpu
from jax.sharding import PartitionSpec as P

HD = 128
FREQ = 256
STEPS = 50


def shifted(value, axis, steps):
    count = lax.axis_size(axis)
    leading, last = (max(0, -steps), min(count, count - steps))
    return lax.ppermute(value, axis, [(source, source + steps) for source in range(leading, last)])


def time_features(noise_steps):
    timestep = 1000.0 * (noise_steps.astype(jnp.float32) + 1.0) / STEPS
    half = FREQ // 2
    rates = jnp.exp(-math.log(10000.0) * jnp.arange(half).astype(jnp.float32) / half)
    angles = timestep[:, None] * rates[None, :]
    return jnp.concatenate([jnp.cos(angles), jnp.sin(angles)], axis=1)


def on_device(
    queries, keys, values, residual, fresh_frame, out_weight, time_weight, noise_steps, frame_mask
):
    query_local, key_local, value_local = (
        lax.all_to_all(queries, "head", split_axis=2, concat_axis=1, tiled=True),
        lax.all_to_all(keys, "head", split_axis=2, concat_axis=1, tiled=True),
        lax.all_to_all(values, "head", split_axis=2, concat_axis=1, tiled=True),
    )
    tokens = query_local.shape[1]
    heads_here = query_local.shape[2] // HD
    scale = 1.0 / math.sqrt(HD)
    query_heads = query_local[0].reshape(tokens, heads_here, HD)
    key_value = jnp.stack([key_local[0], value_local[0]], axis=0)
    frame = lax.axis_index("tm")
    frames_total = lax.axis_size("tm")
    window = min(8, frames_total)
    mask_row = frame_mask[0]
    columns = jnp.arange(mask_row.shape[0], dtype=jnp.int32)

    def allowed_at(offset):
        hits = jnp.sum(jnp.where(columns == frame - offset, mask_row, 0))
        return hits > 0

    def absorb(state, block, allowed):
        running_max, weight_sum, accumulated = state
        key_heads = block[0].reshape(tokens, heads_here, HD)
        value_heads = block[1].reshape(tokens, heads_here, HD)
        scores = (
            jnp.einsum("qhd,khd->hqk", query_heads, key_heads, preferred_element_type=jnp.float32)
            * scale
        )
        new_max = jnp.where(allowed, jnp.maximum(running_max, jnp.max(scores, axis=2)), running_max)
        lifted = jnp.where(allowed, jnp.exp(jnp.minimum(scores - new_max[:, :, None], 0.0)), 0.0)
        factor = jnp.exp(running_max - new_max)
        weight_sum = weight_sum * factor + jnp.sum(lifted, axis=2)
        rounded = lifted.astype(jnp.bfloat16)
        accumulated = accumulated * jnp.transpose(factor)[:, :, None] + jnp.einsum(
            "hqk,khd->qhd", rounded, value_heads, preferred_element_type=jnp.float32
        )
        return (new_max, weight_sum, accumulated)

    state = (
        jnp.full((heads_here, tokens), -1e30, jnp.float32),
        jnp.zeros((heads_here, tokens), jnp.float32),
        jnp.zeros((tokens, heads_here, HD), jnp.float32),
    )
    state = absorb(state, key_value, allowed_at(0))
    moving = key_value
    for offset in range(1, window):
        moving = shifted(moving, "tm", 1)
        state = absorb(state, moving, allowed_at(offset))
    running_max, weight_sum, accumulated = state
    attention = (
        (accumulated / jnp.transpose(weight_sum)[:, :, None])
        .reshape(tokens, heads_here * HD)
        .astype(jnp.bfloat16)
    )
    weight_cols = lax.all_gather(out_weight, "tm", axis=0, tiled=True)
    projected = jnp.dot(
        lax.all_gather(attention, "head", axis=1, tiled=True),
        weight_cols,
        preferred_element_type=jnp.float32,
    )
    gate = jnp.dot(
        time_features(noise_steps), time_weight.astype(jnp.float32), precision=lax.Precision.HIGHEST
    )
    updated = (residual[0].astype(jnp.float32) + gate * projected).astype(jnp.bfloat16)
    moved = shifted(updated, "tm", -1)
    rolled = jnp.where(frame == frames_total - 1, fresh_frame, moved)
    return rolled[None]


def fused_kernel(
    T, G, C, hp, pieces, groups,
    q_ref, k_ref, v_ref, res_ref, fresh_ref, w_ref, tw_ref, steps_ref, mask_ref,
    out_ref,
    qb, kv, ab, lb, tb, mb, fb, gb, wb, w3, twb, rb, pb, down_out, down_in, up_out, up_in,
    load_sem, meta_send, meta_recv, kv_send, q_send, kv_recv, q_recv, pass_send, pass_recv,
    raise_send, ax_send, ax_recv, ac_send, ac_recv, dn_send, dn_recv, up_send, up_recv,
    w_send, w_recv, tr_send, tr_recv,
):
    t = lax.axis_index("tm")
    h = lax.axis_index("head")
    group = lax.axis_index("groups")
    x = h // C
    c = lax.rem(h, C)
    H = G * C
    tl = q_ref.shape[1]
    cw = hp * HD
    tokens = tl * H
    half = G * tl
    nb = w_ref.shape[1] // pieces
    mask_row = FREQ // HD
    share = w_ref.shape[0] // groups
    top, low = T - 1, T - 2
    scale = 1.0 / math.sqrt(HD)

    def to(tt, hh):
        return dict(device_id={"tm": tt, "head": hh}, device_id_type=pl.DeviceIdType.MESH)

    def beside(dg):
        return dict(
            device_id={"groups": lax.rem(group + dg, groups)}, device_id_type=pl.DeviceIdType.MESH
        )

    def landed(ref, sem):
        pltpu.make_async_copy(ref, ref, sem).wait()

    def cols_of(p):
        return slice(p * nb, (p + 1) * nb)

    def reaches(one, other):
        return one == other or (other < top or one == low)

    barrier = pltpu.get_barrier_semaphore()

    def entered(level):
        awaited = C - 1 + (groups - 1 if level == low else 0)
        for other in range(T):
            awaited += (G - 1 if other == level else G) * reaches(level, other)
        return awaited

    def announce(level):
        for other in reversed(range(T)):
            for dx in range(1 if other == level else 0, G):
                if reaches(other, level):
                    pl.semaphore_signal(
                        barrier, inc=1, **to(other, lax.rem(x + dx, G) * C + c)
                    )
        for dc in range(1, C):
            pl.semaphore_signal(barrier, inc=1, **to(level, x * C + lax.rem(c + dc, C)))
        if level == low:
            for dg in range(1, groups):
                pl.semaphore_signal(barrier, inc=1, **beside(dg))

    for level in range(T):
        pl.when(t == level)(functools.partial(announce, level))

    loads = [
        pltpu.make_async_copy(tw_ref, twb, load_sem.at[0]),
        pltpu.make_async_copy(w_ref, wb, load_sem.at[1]),
        pltpu.make_async_copy(res_ref.at[0], rb, load_sem.at[2]),
    ]
    for copy in loads:
        copy.start()

    @pl.when(t == top)
    def _():
        pltpu.make_async_copy(fresh_ref, out_ref, load_sem.at[3]).start()

    timestep = 1000.0 * (jnp.full((1, HD), steps_ref[0], jnp.int32).astype(jnp.float32) + 1.0) / STEPS
    place = lax.broadcasted_iota(jnp.int32, (1, HD), 1).astype(jnp.float32)
    angles = timestep * jnp.exp(-math.log(10000.0) * place / (FREQ // 2))
    mb[t, 0:1, :] = jnp.cos(angles)
    mb[t, 1:2, :] = jnp.sin(angles)
    for g in range(T):
        row = mask_row + g
        mb[t, row : row + 1, :] = jnp.full((1, HD), mask_ref[0, g], jnp.int32).astype(jnp.float32)

    sources = (q_ref, k_ref, v_ref)

    def slot(kind, s, f, xs):
        return qb.at[s * T + f, xs] if kind == 0 else kv.at[s * T + f, c, kind - 1, xs]

    def sems(kind, s, f):
        if kind == 0:
            return q_send.at[0], q_recv.at[s * T + f]
        return kv_send.at[0], kv_recv.at[kind - 1, s * T + f]

    def block(kind, w, xx):
        column = pl.multiple_of((w * G + xx) * cw, HD)
        return sources[kind].at[0, :, pl.ds(column, cw)]

    def aim(f, key):
        w = min(key, top)
        if key < top:
            return w, 0, w
        return w, 1, (low if key == top and f < top else top)

    def outgoing(kind, f, key, dx):
        w, s, level = aim(f, key)
        xx = lax.rem(x + dx, G)
        leaves, lands = sems(kind, s, f)
        return pltpu.make_async_remote_copy(
            src_ref=block(kind, w, xx), dst_ref=slot(kind, s, f, x),
            send_sem=leaves, recv_sem=lands, **to(level, xx * C + c),
        )

    def own(kind, f, key):
        w, s, _ = aim(f, key)
        return pltpu.make_async_copy(block(kind, w, x), slot(kind, s, f, x), sems(kind, s, f)[1])

    def passed(i, kind, dc):
        return pltpu.make_async_remote_copy(
            src_ref=kv.at[i, c, kind - 1], dst_ref=kv.at[i, c, kind - 1],
            send_sem=pass_send.at[0], recv_sem=pass_recv.at[kind - 1, i, dc - 1],
            **to(t, x * C + lax.rem(c + dc, C)),
        )

    def raised(i, kind):
        return pltpu.make_async_remote_copy(
            src_ref=kv.at[i, c, kind - 1], dst_ref=kv.at[i, c, kind - 1],
            send_sem=raise_send.at[0], recv_sem=kv_recv.at[kind - 1, i], **to(top, h),
        )

    own_rows = pl.ds(pl.multiple_of(group * share, 8), share)

    def lift(p):
        return pltpu.make_async_remote_copy(
            src_ref=w_ref.at[own_rows, cols_of(p)], dst_ref=w3.at[own_rows, cols_of(p)],
            send_sem=w_send.at[0], recv_sem=w_recv.at[p], **to(low, h),
        )

    def trade(p, dg):
        return pltpu.make_async_remote_copy(
            src_ref=w3.at[own_rows, cols_of(p)], dst_ref=w3.at[own_rows, cols_of(p)],
            send_sem=tr_send.at[0], recv_sem=tr_recv.at[p, dg - 1], **beside(dg),
        )

    def mine(i, column, size):
        return ab.at[i, c, :, pl.ds(pl.multiple_of(column, HD), size)]

    def across(i, dx):
        here = mine(i, x * cw, cw)
        return pltpu.make_async_remote_copy(
            src_ref=here, dst_ref=here, send_sem=ax_send.at[0], recv_sem=ax_recv.at[i, dx - 1],
            **to(t, lax.rem(x + dx, G) * C + c),
        )

    def aside(i, xs, dc):
        here = mine(i, xs * cw, cw)
        return pltpu.make_async_remote_copy(
            src_ref=here, dst_ref=here, send_sem=ac_send.at[0], recv_sem=ac_recv.at[i, dc - 1],
            **to(t, x * C + lax.rem(c + dc, C)),
        )

    def spot(r):
        return r % (T - 2)

    def down(level, r, p):
        return pltpu.make_async_remote_copy(
            src_ref=down_out.at[spot(r), p], dst_ref=down_in.at[spot(r), p],
            send_sem=dn_send.at[0], recv_sem=dn_recv.at[spot(r), p], **to(level - 1, h),
        )

    def up(level, r, p):
        return pltpu.make_async_remote_copy(
            src_ref=up_out.at[spot(r), p], dst_ref=up_in.at[spot(r), p],
            send_sem=up_send.at[0], recv_sem=up_recv.at[spot(r), p], **to(level + 1, h),
        )

    def gates(level):
        with jax.named_scope("loads"):
            for copy in loads:
                copy.wait()
        with jax.named_scope("meta"):
            fb[...] = jnp.zeros_like(fb)
            away = [f for f in range(1, T) if level != f and level < top]
            if away:
                landed(mb.at[: len(away)], meta_recv.at[0])
            for f in range(1, T) if level < top else (top,):
                for b in range(mask_row):
                    fb[f : f + 1, b * HD : (b + 1) * HD] = mb[f, b : b + 1, :]
        with jax.named_scope("gate"):
            gb[...] = jnp.dot(
                fb[...], twb[...].astype(jnp.float32),
                precision=lax.Precision.HIGHEST, preferred_element_type=jnp.float32,
            )

    def program(level):
        with jax.named_scope("barrier"):
            pl.semaphore_wait(barrier, entered(level))

        told = [other for other in range(top) if other != level and level > 0]
        for other in told:
            pltpu.make_async_remote_copy(
                src_ref=mb.at[t], dst_ref=mb.at[t], send_sem=meta_send.at[0],
                recv_sem=meta_recv.at[0], **to(other, h),
            ).start()
        count = dict(kv=0, q=0, passed=0, raised=0, ax=0, ac=0, down=0, up=0, traded=0)

        def send(kinds, key, dxs=tuple(reversed(range(G)))):
            for dx in dxs:
                for kind in kinds:
                    if kind == 0 and level == 0:
                        continue
                    if dx == 0 and aim(level, key)[2] == level:
                        own(kind, level, key).start()
                    else:
                        outgoing(kind, level, key, dx).start()
                        count["q" if kind == 0 else "kv"] += 1

        def take(s, f, kinds=(1, 2)):
            i = s * T + f
            for kind in kinds:
                landed(kv.at[i, c, kind - 1], kv_recv.at[kind - 1, i])
                for dc in range(1, C):
                    passed(i, kind, dc).start()
                    count["passed"] += 1
                if s == 1 and level == low and f < low:
                    raised(i, kind).start()
                    count["raised"] += 1

        def take_queries(s, f):
            landed(qb.at[s * T + f], q_recv.at[s * T + f])

        def settle(s, f, kinds=(1, 2)):
            i = s * T + f
            for kind in kinds:
                for dc in range(1, C):
                    landed(
                        kv.at[i, lax.rem(c + C - dc, C), kind - 1],
                        pass_recv.at[kind - 1, i, dc - 1],
                    )

        def weigh(s, r, j):
            f = r + 1
            keys_here = (f + 1) * tokens
            allowed = jnp.concatenate(
                [
                    jnp.broadcast_to(mb[f, mask_row + g : mask_row + g + 1, 0:1], (1, tokens))
                    for g in range(f + 1)
                ],
                axis=1,
            )
            cols = slice(j * HD, (j + 1) * HD)
            query = qb[s * T + f, :, :, cols].reshape(half, HD)
            key = kv[s * T : s * T + f + 1, :, 0, :, :, cols].reshape(keys_here, HD)
            scores = (
                lax.dot_general(
                    query, key, (((1,), (1,)), ((), ())), preferred_element_type=jnp.float32
                )
                * scale
            )
            scores = jnp.where(allowed > 0.5, scores, -1e30)
            peak = jnp.max(scores, axis=1, keepdims=True)
            lifted = jnp.exp(scores - peak)
            return lifted.astype(jnp.bfloat16), jnp.sum(lifted, axis=1, keepdims=True)

        def mix(s, r, j, rounded, total):
            f = r + 1
            cols = slice(j * HD, (j + 1) * HD)
            value = kv[s * T : s * T + f + 1, :, 1, :, :, cols].reshape((f + 1) * tokens, HD)
            mixed = jnp.dot(rounded, value, preferred_element_type=jnp.float32)
            here = pl.ds(pl.multiple_of(x * cw + j * HD, HD), HD)
            ab[s * (T - 1) + r, c, :, here] = (mixed / total).astype(jnp.bfloat16)

        def share_out(s, r):
            i = s * (T - 1) + r
            for dx in range(1, G):
                across(i, dx).start()
                count["ax"] += 1
            for dc in range(1, C):
                aside(i, x, dc).start()
                count["ac"] += 1

        def attend(s, r):
            for j in range(hp):
                mix(s, r, j, *weigh(s, r, j))
            share_out(s, r)

        def attend_keys(s, r):
            for j in range(hp):
                rounded, total = weigh(s, r, j)
                lb[s, j] = rounded
                tb[s, j] = jnp.broadcast_to(total, (half, HD))

        def attend_values(s, r):
            for j in range(hp):
                mix(s, r, j, lb[s, j], tb[s, j])
            share_out(s, r)

        def hand_over(s, r):
            i = s * (T - 1) + r
            for dx in range(1, G):
                xs = lax.rem(x + G - dx, G)
                landed(mine(i, xs * cw, cw), ax_recv.at[i, dx - 1])
                for dc in range(1, C):
                    aside(i, xs, dc).start()
                    count["ac"] += 1

        def gathered(s, r):
            i = s * (T - 1) + r
            for dc in range(1, C):
                landed(ab.at[i, lax.rem(c + C - dc, C)], ac_recv.at[i, dc - 1])

        def product(r, p):
            if level == top:
                parts = ((1, wb),)
            elif level == low and r < low:
                parts = ((0, wb), (1, w3))
            else:
                parts = ((0, wb),)
            partial = 0.0
            for s, weight in parts:
                partial += jnp.dot(
                    ab[s * (T - 1) + r].reshape(tokens, G * cw), weight[:, cols_of(p)],
                    preferred_element_type=jnp.float32,
                )
            partial = partial * gb[r + 1 : r + 2, cols_of(p)]
            if level == r + 1:
                moved = [
                    rb[(xs * C + cs) * tl : (xs * C + cs + 1) * tl, cols_of(p)]
                    for cs in range(C)
                    for xs in range(G)
                ]
                partial += jnp.concatenate(moved, axis=0).astype(jnp.float32)
            return partial

        def send_down(r, p, value):
            down_out[spot(r), p] = value.astype(jnp.bfloat16)
            down(level, r, p).start()
            count["down"] += 1

        def send_up(r, p, value):
            up_out[spot(r), p] = value.astype(jnp.bfloat16)
            up(level, r, p).start()
            count["up"] += 1

        def from_down(r, p):
            landed(down_in.at[spot(r), p], dn_recv.at[spot(r), p])
            return down_in[spot(r), p].astype(jnp.float32)

        def from_up(r, p):
            landed(up_in.at[spot(r), p], up_recv.at[spot(r), p])
            return up_in[spot(r), p].astype(jnp.float32)

        def finish(p):
            r = level
            total = pb[r, p] + from_down(r, p)
            if r > 0:
                total += from_up(r, p)
            total = total.astype(out_ref.dtype)
            for cs in range(C):
                for xs in range(G):
                    row, token = (cs * G + xs) * tl, (xs * C + cs) * tl
                    out_ref[token : token + tl, cols_of(p)] = total[row : row + tl]

        scope = jax.named_scope
        early = (3 * pieces) // 5
        order = [(low - 1, p) for p in range(2)]
        order += [(r, p) for r in range(low - 1) for p in range(pieces)]
        order += [(low - 1, p) for p in range(2, pieces)]

        if level == top:
            send((0, 1, 2), top)
            lifts = [lift(p) for p in range(pieces)]
            for p in range(early):
                lifts[p].start()
            for w in reversed(range(low)):
                send((1, 2, 0), w)
            for p in range(early, pieces):
                lifts[p].start()
            send((1, 2, 0), low)
            gates(level)
            for f in range(T):
                with scope(f"take{f}"):
                    take(1, f)
            with scope("settle"):
                take_queries(1, top)
                for f in range(T):
                    settle(1, f)
            with scope("attend"):
                attend(1, low)
            with scope("gather"):
                hand_over(1, low)
                gathered(1, low)
            with scope("project"):
                for p in range(pieces):
                    send_down(low, p, product(low, p))
            pltpu.make_async_copy(fresh_ref, out_ref, load_sem.at[3]).wait()
            landed(w3.at[own_rows], w_send.at[0])
        elif level == low:
            for w in range(low):
                send((1, 2, 0), w)
            send((1, 2, 0), low)
            send((1, 2, 0), top)
            send((1, 2), T)

            def exchange(p):
                with scope(f"trade{p}"):
                    landed(w3.at[own_rows, cols_of(p)], w_recv.at[p])
                for dg in range(1, groups):
                    trade(p, dg).start()

            def exchanged(p):
                for dg in range(1, groups):
                    theirs = pl.ds(
                        pl.multiple_of(lax.rem(group + groups - dg, groups) * share, 8), share
                    )
                    landed(w3.at[theirs, cols_of(p)], tr_recv.at[p, dg - 1])

            gates(level)
            for p in range(early - 1):
                exchange(p)
            with scope("take_early"):
                for f in (*range(low - 1), low):
                    for s in (0, 1):
                        take(s, f)
                for s in (0, 1):
                    take_queries(s, low)
            exchange(early - 1)
            with scope("keys"):
                for s in (0, 1):
                    take(s, low - 1, (1,))
            for s in (0, 1):
                with scope(f"settle{s}1"):
                    for f in range(low + 1):
                        settle(s, f, (1,))
                with scope(f"attend{s}{low - 1}1"):
                    attend_keys(s, low - 1)
            for s in (0, 1):
                with scope(f"values{s}"):
                    take(s, low - 1, (2,))
                with scope(f"settle{s}2"):
                    for f in range(low + 1):
                        settle(s, f, (2,))
                with scope(f"attend{s}{low - 1}2"):
                    attend_values(s, low - 1)
            for r in reversed(range(low - 1)):
                for s in (0, 1):
                    with scope(f"hand{s}{r + 1}"):
                        hand_over(s, r + 1)
                    with scope(f"q{r + 1}{s}"):
                        take_queries(s, r + 1)
                    with scope(f"attend{s}{r}"):
                        attend(s, r)
            ready = set()
            known = set()
            swapped = False

            def last_frame():
                with scope("take3"):
                    take(0, top)
                    take_queries(0, top)
                    settle(0, top)
                with scope("attend3"):
                    attend(0, low)

            for r, p in order:
                if p >= early and not swapped:
                    swapped = True
                    for q in range(early, pieces):
                        exchange(q)
                if r not in ready:
                    ready.add(r)
                    with scope(f"gather{r}"):
                        for s in (0, 1):
                            if r == 0 and low > 1 or low == 1:
                                hand_over(s, r)
                        for s in (0, 1):
                            gathered(s, r)
                if p not in known:
                    known.add(p)
                    with scope(f"w{p}"):
                        exchanged(p)
                with scope(f"project{r}{p}"):
                    send_down(r, p, product(r, p))
            last_frame()
            with scope("gather3"):
                hand_over(0, low)
                gathered(0, low)
            with scope("project3"):
                for p in range(pieces):
                    pb[low, p] = product(low, p)
            for p in range(pieces):
                with scope(f"finish{p}"):
                    finish(p)
            landed(w3.at[own_rows], tr_send.at[0])
        else:
            for kind in (1, 2, 0):
                for w in (low, top):
                    send((kind,), w)
            for w in range(level + 1, low):
                send((1, 2, 0), w)
            for w in range(level):
                send((1, 2, 0), w)
            send((1, 2, 0), level)
            gates(level)
            stages = (
                (range(T - 1), range(T - 3, -1, -1)),
                (range(T - 1, T), range(T - 2, T - 1)),
            )
            if level > 0:
                stages = (
                    (range(level + 1), range(level)),
                    (range(level + 1, T), range(level, T - 1)),
                )
            for frames, rounds in stages:
                for f in frames:
                    with scope(f"take{f}"):
                        take(0, f)
                        if f > 0:
                            take_queries(0, f)
                for f in frames:
                    with scope(f"settle{f}"):
                        settle(0, f)
                for r in rounds:
                    with scope(f"attend{r}"):
                        attend(0, r)
                for r in rounds:
                    with scope(f"gather{r}"):
                        hand_over(0, r)
                        gathered(0, r)
                    with scope(f"project{r}"):
                        for p in range(pieces):
                            value = product(r, p)
                            if level == 0 and r > 0:
                                send_up(r, p, value)
                            else:
                                pb[r, p] = value
            ups = [
                (q, p) for p in range(pieces) for q in reversed(range(level + 1, T - 1)) if level
            ]
            for n, (r, p) in enumerate(pair for pair in order if pair[0] <= level):
                if r == level:
                    with scope(f"finish{p}"):
                        finish(p)
                else:
                    with scope(f"down{r}{p}"):
                        send_down(r, p, pb[r, p] + from_down(r, p))
                if n >= 3 and ups:
                    q, p = ups.pop(0)
                    with scope(f"up{q}{p}"):
                        send_up(q, p, pb[q, p] + from_up(q, p))
            for q, p in ups:
                send_up(q, p, pb[q, p] + from_up(q, p))
        with scope("sends"):
            if told:
                landed(mb.at[: len(told)], meta_send.at[0])
            landed(kv.at[: count["kv"] // 2, 0, :, 0], kv_send.at[0])
            if count["q"]:
                landed(qb.at[: count["q"], 0], q_send.at[0])
            if count["passed"]:
                landed(kv.at[: count["passed"] // 2, 0], pass_send.at[0])
            if count["raised"]:
                landed(kv.at[: count["raised"] // 2, 0], raise_send.at[0])
            if count["ax"]:
                landed(ab.at[: count["ax"], 0, :, :cw], ax_send.at[0])
            if count["ac"]:
                landed(ab.at[: count["ac"] // G, 0], ac_send.at[0])
            if count["down"]:
                landed(down_out.at[: count["down"] // pieces], dn_send.at[0])
            if count["up"]:
                landed(up_out.at[: count["up"] // pieces], up_send.at[0])

    for level in range(T):
        pl.when(t == level)(functools.partial(program, level))


def fused(T, H, heads, groups):
    def on_device_fused(
        queries, keys, values, residual, fresh_frame, out_weight, time_weight, noise_steps, frame_mask
    ):
        level_heads = heads // T
        G = math.gcd(level_heads, H)
        C = H // G
        hp = level_heads // G
        tl = queries.shape[1]
        tokens = tl * H
        width = out_weight.shape[1]
        pieces = width // (2 * HD)
        nb = width // pieces
        meta_rows = -(-(FREQ // HD + T) // 8) * 8
        cw = hp * HD
        bf16, f32 = jnp.bfloat16, jnp.float32
        dma = pltpu.SemaphoreType.DMA
        chunk = (T - 2, pieces, tokens, nb)
        out = pl.pallas_call(
            functools.partial(fused_kernel, T, G, C, hp, pieces, groups),
            out_shape=jax.ShapeDtypeStruct((tokens, width), bf16),
            in_specs=[pl.BlockSpec(memory_space=pltpu.HBM)] * 7
            + [pl.BlockSpec(memory_space=pltpu.SMEM)] * 2,
            out_specs=pl.BlockSpec(memory_space=pltpu.VMEM),
            scratch_shapes=[
                pltpu.VMEM((2 * T, G, tl, cw), bf16),
                pltpu.VMEM((2 * T, C, 2, G, tl, cw), bf16),
                pltpu.VMEM((2 * (T - 1), C, G * tl, G * cw), bf16),
                pltpu.VMEM((2, hp, G * tl, (T - 1) * tokens), bf16),
                pltpu.VMEM((2, hp, G * tl, HD), f32),
                pltpu.VMEM((T, meta_rows, HD), f32),
                pltpu.VMEM((8, FREQ), f32),
                pltpu.VMEM((8, width), f32),
                pltpu.VMEM(out_weight.shape, bf16),
                pltpu.VMEM(out_weight.shape, bf16),
                pltpu.VMEM(time_weight.shape, bf16),
                pltpu.VMEM((tokens, width), bf16),
                pltpu.VMEM((T - 1, pieces, tokens, nb), f32),
                pltpu.VMEM(chunk, bf16),
                pltpu.VMEM(chunk, bf16),
                pltpu.VMEM(chunk, bf16),
                pltpu.VMEM(chunk, bf16),
                dma((4,)),
                dma((1,)),
                dma((1,)),
                dma((1,)),
                dma((1,)),
                dma((2, 2 * T)),
                dma((2 * T,)),
                dma((1,)),
                dma((2, 2 * T, C - 1)),
                dma((1,)),
                dma((1,)),
                dma((2 * (T - 1), G - 1)),
                dma((1,)),
                dma((2 * (T - 1), C - 1)),
                dma((1,)),
                dma((T - 2, pieces)),
                dma((1,)),
                dma((T - 2, pieces)),
                dma((1,)),
                dma((pieces,)),
                dma((1,)),
                dma((pieces, groups - 1)),
            ],
            compiler_params=pltpu.CompilerParams(
                collective_id=0, has_side_effects=True, vmem_limit_bytes=32 * 1024 * 1024
            ),
        )(
            *(
                pltpu.with_memory_space_constraint(array, pltpu.HBM)
                for array in (
                    queries, keys, values, residual, fresh_frame, out_weight, time_weight
                )
            ),
            noise_steps,
            frame_mask,
        )
        return out[None]

    return on_device_fused


def solution(mesh):
    placed = (
        P(("groups", "tm"), "head", None),
        P(("groups", "tm"), "head", None),
        P(("groups", "tm"), "head", None),
        P(("groups", "tm"), None, "head"),
        P("groups", "head"),
        P("tm", "head"),
        P(None, "head"),
        P(("groups", "tm")),
        P(("groups", "tm"), None),
    )
    def whole(*args):
        frames, spread = mesh.shape["tm"], mesh.shape["head"]
        heads = args[0].shape[2] // HD
        fits = 2 < frames <= 4 and heads % frames == 0 and args[5].shape[1] % (spread * 2 * HD) == 0
        return jax.shard_map(
            fused(frames, spread, heads, mesh.shape["groups"]) if fits else on_device,
            mesh=mesh,
            in_specs=placed,
            out_specs=P(("groups", "tm"), None, "head"),
            check_vma=False,
        )(*args)

    return whole
```

```python
import functools
import math

import jax
import jax.numpy as jnp
from jax import lax
from jax.experimental import pallas as pl
from jax.experimental.pallas import tpu as pltpu
from jax.sharding import PartitionSpec as P

HD = 128
FREQ = 256
STEPS = 50


def shifted(value, axis, steps):
    count = lax.axis_size(axis)
    leading, last = (max(0, -steps), min(count, count - steps))
    return lax.ppermute(value, axis, [(source, source + steps) for source in range(leading, last)])


def time_features(noise_steps):
    timestep = 1000.0 * (noise_steps.astype(jnp.float32) + 1.0) / STEPS
    half = FREQ // 2
    rates = jnp.exp(-math.log(10000.0) * jnp.arange(half).astype(jnp.float32) / half)
    angles = timestep[:, None] * rates[None, :]
    return jnp.concatenate([jnp.cos(angles), jnp.sin(angles)], axis=1)


def on_device(
    queries, keys, values, residual, fresh_frame, out_weight, time_weight, noise_steps, frame_mask
):
    query_local, key_local, value_local = (
        lax.all_to_all(queries, "head", split_axis=2, concat_axis=1, tiled=True),
        lax.all_to_all(keys, "head", split_axis=2, concat_axis=1, tiled=True),
        lax.all_to_all(values, "head", split_axis=2, concat_axis=1, tiled=True),
    )
    tokens = query_local.shape[1]
    heads_here = query_local.shape[2] // HD
    scale = 1.0 / math.sqrt(HD)
    query_heads = query_local[0].reshape(tokens, heads_here, HD)
    key_value = jnp.stack([key_local[0], value_local[0]], axis=0)
    frame = lax.axis_index("tm")
    frames_total = lax.axis_size("tm")
    window = min(8, frames_total)
    mask_row = frame_mask[0]
    columns = jnp.arange(mask_row.shape[0], dtype=jnp.int32)

    def allowed_at(offset):
        hits = jnp.sum(jnp.where(columns == frame - offset, mask_row, 0))
        return hits > 0

    def absorb(state, block, allowed):
        running_max, weight_sum, accumulated = state
        key_heads = block[0].reshape(tokens, heads_here, HD)
        value_heads = block[1].reshape(tokens, heads_here, HD)
        scores = (
            jnp.einsum("qhd,khd->hqk", query_heads, key_heads, preferred_element_type=jnp.float32)
            * scale
        )
        new_max = jnp.where(allowed, jnp.maximum(running_max, jnp.max(scores, axis=2)), running_max)
        lifted = jnp.where(allowed, jnp.exp(jnp.minimum(scores - new_max[:, :, None], 0.0)), 0.0)
        factor = jnp.exp(running_max - new_max)
        weight_sum = weight_sum * factor + jnp.sum(lifted, axis=2)
        rounded = lifted.astype(jnp.bfloat16)
        accumulated = accumulated * jnp.transpose(factor)[:, :, None] + jnp.einsum(
            "hqk,khd->qhd", rounded, value_heads, preferred_element_type=jnp.float32
        )
        return (new_max, weight_sum, accumulated)

    state = (
        jnp.full((heads_here, tokens), -1e30, jnp.float32),
        jnp.zeros((heads_here, tokens), jnp.float32),
        jnp.zeros((tokens, heads_here, HD), jnp.float32),
    )
    state = absorb(state, key_value, allowed_at(0))
    moving = key_value
    for offset in range(1, window):
        moving = shifted(moving, "tm", 1)
        state = absorb(state, moving, allowed_at(offset))
    running_max, weight_sum, accumulated = state
    attention = (
        (accumulated / jnp.transpose(weight_sum)[:, :, None])
        .reshape(tokens, heads_here * HD)
        .astype(jnp.bfloat16)
    )
    weight_cols = lax.all_gather(out_weight, "tm", axis=0, tiled=True)
    projected = jnp.dot(
        lax.all_gather(attention, "head", axis=1, tiled=True),
        weight_cols,
        preferred_element_type=jnp.float32,
    )
    gate = jnp.dot(
        time_features(noise_steps), time_weight.astype(jnp.float32), precision=lax.Precision.HIGHEST
    )
    updated = (residual[0].astype(jnp.float32) + gate * projected).astype(jnp.bfloat16)
    moved = shifted(updated, "tm", -1)
    rolled = jnp.where(frame == frames_total - 1, fresh_frame, moved)
    return rolled[None]


def fused_kernel(
    T, G, C, hp, pieces, groups,
    q_ref, k_ref, v_ref, res_ref, fresh_ref, w_ref, tw_ref, steps_ref, mask_ref,
    out_ref,
    qb, kv, ab, lb, tb, so, st, mb, fb, gb, wb, w3, twb, rb, pb, down_out, down_in, up_out, up_in,
    load_sem, meta_send, meta_recv, kv_send, q_send, kv_recv, q_recv, pass_send, pass_recv,
    raise_send, ax_send, ax_recv, ac_send, ac_recv, dn_send, dn_recv, up_send, up_recv,
    w_send, w_recv, tr_send, tr_recv, near_send, so_send, so_recv, st_send, st_recv,
):
    t = lax.axis_index("tm")
    h = lax.axis_index("head")
    group = lax.axis_index("groups")
    x = h // C
    c = lax.rem(h, C)
    H = G * C
    tl = q_ref.shape[1]
    cw = hp * HD
    tokens = tl * H
    half = G * tl
    nb = w_ref.shape[1] // pieces
    mask_row = FREQ // HD
    share = w_ref.shape[0] // groups
    top, low = T - 1, T - 2
    scale = 1.0 / math.sqrt(HD)

    def to(tt, hh):
        return dict(device_id={"tm": tt, "head": hh}, device_id_type=pl.DeviceIdType.MESH)

    def beside(dg):
        return dict(
            device_id={"groups": lax.rem(group + dg, groups)}, device_id_type=pl.DeviceIdType.MESH
        )

    def landed(ref, sem):
        pltpu.make_async_copy(ref, ref, sem).wait()

    def cols_of(p):
        return slice(p * nb, (p + 1) * nb)

    def reaches(one, other):
        return one == other or (other < top or one == low)

    barrier = pltpu.get_barrier_semaphore()

    def entered(level):
        awaited = C - 1 + (groups - 1 if level == low else 0)
        for other in range(T):
            awaited += (G - 1 if other == level else G) * reaches(level, other)
        return awaited

    def announce(level):
        for other in reversed(range(T)):
            for dx in range(1 if other == level else 0, G):
                if reaches(other, level):
                    pl.semaphore_signal(
                        barrier, inc=1, **to(other, lax.rem(x + dx, G) * C + c)
                    )
        for dc in range(1, C):
            pl.semaphore_signal(barrier, inc=1, **to(level, x * C + lax.rem(c + dc, C)))
        if level == low:
            for dg in range(1, groups):
                pl.semaphore_signal(barrier, inc=1, **beside(dg))

    for level in range(T):
        pl.when(t == level)(functools.partial(announce, level))

    loads = [
        pltpu.make_async_copy(tw_ref, twb, load_sem.at[0]),
        pltpu.make_async_copy(w_ref, wb, load_sem.at[1]),
        pltpu.make_async_copy(res_ref.at[0], rb, load_sem.at[2]),
    ]
    for copy in loads:
        copy.start()

    @pl.when(t == top)
    def _():
        pltpu.make_async_copy(fresh_ref, out_ref, load_sem.at[3]).start()

    def features():
        timestep = 1000.0 * (jnp.full((1, HD), steps_ref[0], jnp.int32).astype(jnp.float32) + 1.0) / STEPS
        place = lax.broadcasted_iota(jnp.int32, (1, HD), 1).astype(jnp.float32)
        angles = timestep * jnp.exp(-math.log(10000.0) * place / (FREQ // 2))
        mb[t, 0:1, :] = jnp.cos(angles)
        mb[t, 1:2, :] = jnp.sin(angles)
        for g in range(T):
            row = mask_row + g
            mb[t, row : row + 1, :] = jnp.full((1, HD), mask_ref[0, g], jnp.int32).astype(jnp.float32)

    sources = (q_ref, k_ref, v_ref)

    def slot(kind, s, f, xs):
        return qb.at[s * T + f, xs] if kind == 0 else kv.at[s * T + f, c, kind - 1, xs]

    def sems(kind, s, f):
        if kind == 0:
            return q_send.at[0], q_recv.at[s * T + f]
        return kv_send.at[0], kv_recv.at[kind - 1, s * T + f]

    def block(kind, w, xx):
        column = pl.multiple_of((w * G + xx) * cw, HD)
        return sources[kind].at[0, :, pl.ds(column, cw)]

    def aim(f, key):
        w = min(key, top)
        if key < top:
            return w, 0, w
        return w, 1, (low if key == top and f < top else top)

    def outgoing(kind, f, key, dx):
        w, s, level = aim(f, key)
        xx = lax.rem(x + dx, G)
        leaves, lands = sems(kind, s, f)
        return pltpu.make_async_remote_copy(
            src_ref=block(kind, w, xx), dst_ref=slot(kind, s, f, x),
            send_sem=leaves, recv_sem=lands, **to(level, xx * C + c),
        )

    def own(kind, f, key):
        w, s, _ = aim(f, key)
        return pltpu.make_async_copy(block(kind, w, x), slot(kind, s, f, x), sems(kind, s, f)[1])

    def passed(i, kind, dc):
        return pltpu.make_async_remote_copy(
            src_ref=kv.at[i, c, kind - 1], dst_ref=kv.at[i, c, kind - 1],
            send_sem=pass_send.at[0], recv_sem=pass_recv.at[kind - 1, i, dc - 1],
            **to(t, x * C + lax.rem(c + dc, C)),
        )

    def raised(i, kind):
        return pltpu.make_async_remote_copy(
            src_ref=kv.at[i, c, kind - 1], dst_ref=kv.at[i, c, kind - 1],
            send_sem=raise_send.at[0], recv_sem=kv_recv.at[kind - 1, i], **to(top, h),
        )

    def near(kind, w, dx):
        xx = lax.rem(x + dx, G)
        leaves, lands = sems(kind, 0, w)
        if dx == 0:
            return pltpu.make_async_copy(block(kind, w, x), slot(kind, 0, w, x), lands)
        return pltpu.make_async_remote_copy(
            src_ref=block(kind, w, xx), dst_ref=slot(kind, 0, w, x),
            send_sem=near_send.at[0] if kind == 0 else leaves, recv_sem=lands,
            **to(top, xx * C + c),
        )

    def sidestep(k, key, dx):
        return pltpu.make_async_remote_copy(
            src_ref=block(0, key, lax.rem(x + dx, G)), dst_ref=qb.at[T + k, x],
            send_sem=near_send.at[0], recv_sem=q_recv.at[T + k],
            **to(t, lax.rem(x + dx, G) * C + c),
        )

    def forward(k, key, f, xs):
        return pltpu.make_async_remote_copy(
            src_ref=qb.at[T + k, xs], dst_ref=slot(0, k, f, xs),
            send_sem=q_send.at[0], recv_sem=q_recv.at[k * T + f], **to(low, h),
        )

    def handed(w):
        return [
            pltpu.make_async_remote_copy(
                src_ref=buffer.at[w], dst_ref=buffer.at[top],
                send_sem=leaves.at[0], recv_sem=lands.at[0], **to(w, h),
            )
            for buffer, leaves, lands in ((so, so_send, so_recv), (st, st_send, st_recv))
        ]

    own_rows = pl.ds(pl.multiple_of(group * share, 8), share)

    def lift(p):
        return pltpu.make_async_remote_copy(
            src_ref=w_ref.at[own_rows, cols_of(p)], dst_ref=w3.at[own_rows, cols_of(p)],
            send_sem=w_send.at[0], recv_sem=w_recv.at[p], **to(low, h),
        )

    def trade(p, dg):
        return pltpu.make_async_remote_copy(
            src_ref=w3.at[own_rows, cols_of(p)], dst_ref=w3.at[own_rows, cols_of(p)],
            send_sem=tr_send.at[0], recv_sem=tr_recv.at[p, dg - 1], **beside(dg),
        )

    def mine(i, column, size):
        return ab.at[i, c, :, pl.ds(pl.multiple_of(column, HD), size)]

    def across(i, dx):
        here = mine(i, x * cw, cw)
        return pltpu.make_async_remote_copy(
            src_ref=here, dst_ref=here, send_sem=ax_send.at[0], recv_sem=ax_recv.at[i, dx - 1],
            **to(t, lax.rem(x + dx, G) * C + c),
        )

    def aside(i, xs, dc):
        here = mine(i, xs * cw, cw)
        return pltpu.make_async_remote_copy(
            src_ref=here, dst_ref=here, send_sem=ac_send.at[0], recv_sem=ac_recv.at[i, dc - 1],
            **to(t, x * C + lax.rem(c + dc, C)),
        )

    def spot(r):
        return r % (T - 2)

    def down(level, r, p):
        return pltpu.make_async_remote_copy(
            src_ref=down_out.at[spot(r), p], dst_ref=down_in.at[spot(r), p],
            send_sem=dn_send.at[0], recv_sem=dn_recv.at[spot(r), p], **to(level - 1, h),
        )

    def up(level, r, p):
        return pltpu.make_async_remote_copy(
            src_ref=up_out.at[spot(r), p], dst_ref=up_in.at[spot(r), p],
            send_sem=up_send.at[0], recv_sem=up_recv.at[spot(r), p], **to(level + 1, h),
        )

    def gates(level):
        with jax.named_scope("loads"):
            for copy in loads:
                copy.wait()
        with jax.named_scope("meta"):
            fb[...] = jnp.zeros_like(fb)
            away = [f for f in range(1, T) if level != f and level < top]
            if away:
                landed(mb.at[: len(away)], meta_recv.at[0])
            for f in range(1, T) if level < top else (top,):
                for b in range(mask_row):
                    fb[f : f + 1, b * HD : (b + 1) * HD] = mb[f, b : b + 1, :]
        with jax.named_scope("gate"):
            gb[...] = jnp.dot(
                fb[...], twb[...].astype(jnp.float32),
                precision=lax.Precision.HIGHEST, preferred_element_type=jnp.float32,
            )

    def program(level):
        if level < top:
            features()
        with jax.named_scope("barrier"):
            pl.semaphore_wait(barrier, entered(level))
        if level == top:
            lifts = [lift(p) for p in range(pieces)]
            lifts[0].start()
            features()
        told = [other for other in range(top) if other != level and level > 0]
        for other in told:
            pltpu.make_async_remote_copy(
                src_ref=mb.at[t], dst_ref=mb.at[t], send_sem=meta_send.at[0],
                recv_sem=meta_recv.at[0], **to(other, h),
            ).start()
        count = dict(kv=0, q=0, passed=0, raised=0, near=0, ax=0, ac=0, down=0, up=0, traded=0)

        def send(kinds, key, dxs=tuple(reversed(range(G)))):
            for dx in dxs:
                for kind in kinds:
                    if kind == 0 and level == 0:
                        continue
                    if dx == 0 and aim(level, key)[2] == level:
                        own(kind, level, key).start()
                    else:
                        outgoing(kind, level, key, dx).start()
                        count["q" if kind == 0 else "kv"] += 1

        def take(s, f, kinds=(1, 2)):
            i = s * T + f
            for kind in kinds:
                landed(kv.at[i, c, kind - 1], kv_recv.at[kind - 1, i])
                for dc in range(1, C):
                    passed(i, kind, dc).start()
                    count["passed"] += 1
                if s == 1 and level == low and f < low:
                    raised(i, kind).start()
                    count["raised"] += 1

        def take_queries(s, f):
            landed(qb.at[s * T + f], q_recv.at[s * T + f])

        def settle(s, f, kinds=(1, 2)):
            i = s * T + f
            for kind in kinds:
                for dc in range(1, C):
                    landed(
                        kv.at[i, lax.rem(c + C - dc, C), kind - 1],
                        pass_recv.at[kind - 1, i, dc - 1],
                    )

        def weigh(s, r, j):
            f = r + 1
            keys_here = (f + 1) * tokens
            allowed = jnp.concatenate(
                [
                    jnp.broadcast_to(mb[f, mask_row + g : mask_row + g + 1, 0:1], (1, tokens))
                    for g in range(f + 1)
                ],
                axis=1,
            )
            cols = slice(j * HD, (j + 1) * HD)
            query = qb[s * T + f, :, :, cols].reshape(half, HD)
            key = kv[s * T : s * T + f + 1, :, 0, :, :, cols].reshape(keys_here, HD)
            scores = (
                lax.dot_general(
                    query, key, (((1,), (1,)), ((), ())), preferred_element_type=jnp.float32
                )
                * scale
            )
            scores = jnp.where(allowed > 0.5, scores, -1e30)
            peak = jnp.max(scores, axis=1, keepdims=True)
            lifted = jnp.exp(scores - peak)
            return lifted.astype(jnp.bfloat16), jnp.sum(lifted, axis=1, keepdims=True)

        def mix(s, r, j, rounded, total):
            f = r + 1
            cols = slice(j * HD, (j + 1) * HD)
            value = kv[s * T : s * T + f + 1, :, 1, :, :, cols].reshape((f + 1) * tokens, HD)
            mixed = jnp.dot(rounded, value, preferred_element_type=jnp.float32)
            here = pl.ds(pl.multiple_of(x * cw + j * HD, HD), HD)
            ab[s * (T - 1) + r, c, :, here] = (mixed / total).astype(jnp.bfloat16)

        def attend_own(w):
            lane = lax.broadcasted_iota(jnp.int32, (half, HD), 1)
            stats = jnp.zeros((half, HD), jnp.float32)
            for j in range(hp):
                cols = slice(j * HD, (j + 1) * HD)
                query = qb[w, :, :, cols].reshape(half, HD)
                key = kv[w, :, 0, :, :, cols].reshape(tokens, HD)
                value = kv[w, :, 1, :, :, cols].reshape(tokens, HD)
                scores = (
                    lax.dot_general(
                        query, key, (((1,), (1,)), ((), ())), preferred_element_type=jnp.float32
                    )
                    * scale
                )
                peak = jnp.max(scores, axis=1, keepdims=True)
                lifted = jnp.exp(scores - peak)
                total = jnp.sum(lifted, axis=1, keepdims=True)
                mixed = jnp.dot(
                    lifted.astype(jnp.bfloat16), value, preferred_element_type=jnp.float32
                )
                so[w, :, cols] = (mixed / total).astype(jnp.bfloat16)
                stats = jnp.where(lane == 2 * j, peak, stats)
                stats = jnp.where(lane == 2 * j + 1, total, stats)
            st[w] = jnp.transpose(stats)[:8]
            for copy in handed(w):
                copy.start()

        def attend_last():
            landed(so.at[top], so_recv.at[0])
            landed(st.at[top], st_recv.at[0])
            stats = jnp.transpose(
                jnp.concatenate([st[top], jnp.zeros((HD - 8, half), jnp.float32)], axis=0)
            )
            allowed = jnp.concatenate(
                [
                    jnp.broadcast_to(mb[top, mask_row + g : mask_row + g + 1, 0:1], (1, tokens))
                    for g in range(top)
                ],
                axis=1,
            )
            for j in range(hp):
                cols = slice(j * HD, (j + 1) * HD)
                query = qb[top, :, :, cols].reshape(half, HD)
                key = kv[0:top, :, 0, :, :, cols].reshape(top * tokens, HD)
                value = kv[0:top, :, 1, :, :, cols].reshape(top * tokens, HD)
                scores = (
                    lax.dot_general(
                        query, key, (((1,), (1,)), ((), ())), preferred_element_type=jnp.float32
                    )
                    * scale
                )
                scores = jnp.where(allowed > 0.5, scores, -1e30)
                their_peak = stats[:, 2 * j : 2 * j + 1]
                peak = jnp.maximum(jnp.max(scores, axis=1, keepdims=True), their_peak)
                lifted = jnp.exp(scores - peak)
                theirs = jnp.exp(their_peak - peak) * stats[:, 2 * j + 1 : 2 * j + 2]
                total = jnp.sum(lifted, axis=1, keepdims=True) + theirs
                mixed = jnp.dot(
                    lifted.astype(jnp.bfloat16), value, preferred_element_type=jnp.float32
                )
                mixed += theirs * so[top, :, cols].astype(jnp.float32)
                here = pl.ds(pl.multiple_of(x * cw + j * HD, HD), HD)
                ab[low, c, :, here] = (mixed / total).astype(jnp.bfloat16)
            share_out(0, low)

        def share_out(s, r):
            i = s * (T - 1) + r
            for dx in range(1, G):
                across(i, dx).start()
                count["ax"] += 1
            for dc in range(1, C):
                aside(i, x, dc).start()
                count["ac"] += 1

        def attend(s, r):
            for j in range(hp):
                mix(s, r, j, *weigh(s, r, j))
            share_out(s, r)

        def attend_keys(s, r):
            for j in range(hp):
                rounded, total = weigh(s, r, j)
                lb[s, j] = rounded
                tb[s, j] = jnp.broadcast_to(total, (half, HD))

        def attend_values(s, r):
            for j in range(hp):
                mix(s, r, j, lb[s, j], tb[s, j])
            share_out(s, r)

        def hand_over(s, r):
            i = s * (T - 1) + r
            for dx in range(1, G):
                xs = lax.rem(x + G - dx, G)
                landed(mine(i, xs * cw, cw), ax_recv.at[i, dx - 1])
                for dc in range(1, C):
                    aside(i, xs, dc).start()
                    count["ac"] += 1

        def gathered(s, r):
            i = s * (T - 1) + r
            for dc in range(1, C):
                landed(ab.at[i, lax.rem(c + C - dc, C)], ac_recv.at[i, dc - 1])

        def product(r, p):
            if level == top:
                parts = ((1, wb),)
            elif level == low and r < low:
                parts = ((0, wb), (1, w3))
            else:
                parts = ((0, wb),)
            partial = 0.0
            for s, weight in parts:
                partial += jnp.dot(
                    ab[s * (T - 1) + r].reshape(tokens, G * cw), weight[:, cols_of(p)],
                    preferred_element_type=jnp.float32,
                )
            partial = partial * gb[r + 1 : r + 2, cols_of(p)]
            if level == r + 1:
                moved = [
                    rb[(xs * C + cs) * tl : (xs * C + cs + 1) * tl, cols_of(p)]
                    for cs in range(C)
                    for xs in range(G)
                ]
                partial += jnp.concatenate(moved, axis=0).astype(jnp.float32)
            return partial

        def send_down(r, p, value):
            down_out[spot(r), p] = value.astype(jnp.bfloat16)
            down(level, r, p).start()
            count["down"] += 1

        def send_up(r, p, value):
            up_out[spot(r), p] = value.astype(jnp.bfloat16)
            up(level, r, p).start()
            count["up"] += 1

        def from_down(r, p):
            landed(down_in.at[spot(r), p], dn_recv.at[spot(r), p])
            return down_in[spot(r), p].astype(jnp.float32)

        def from_up(r, p):
            landed(up_in.at[spot(r), p], up_recv.at[spot(r), p])
            return up_in[spot(r), p].astype(jnp.float32)

        def finish(p):
            r = level
            total = pb[r, p] + from_down(r, p)
            if r > 0:
                total += from_up(r, p)
            total = total.astype(out_ref.dtype)
            for cs in range(C):
                for xs in range(G):
                    row, token = (cs * G + xs) * tl, (xs * C + cs) * tl
                    out_ref[token : token + tl, cols_of(p)] = total[row : row + tl]

        scope = jax.named_scope
        early = (3 * pieces) // 5
        order = [(low - 1, p) for p in range(2)]
        order += [(r, p) for r in range(low - 1) for p in range(pieces)]
        order += [(low - 1, p) for p in range(2, pieces)]

        if level == top:
            for p in range(1, early):
                lifts[p].start()
            lower = tuple(reversed(range(low)))
            for w in lower:
                for dx in reversed(range(G)):
                    for kind in (1, 0, 2):
                        near(kind, w, dx).start()
                        if dx > 0:
                            count["near" if kind == 0 else "kv"] += 1
            for w in lower:
                send((0,), w)
            send((0, 1, 2), top)
            for w in lower:
                with scope(f"near{w}"):
                    take(0, w)
                    take_queries(0, w)
            for w in lower:
                with scope(f"own{w}"):
                    settle(0, w)
                    attend_own(w)
            for p in range(early, pieces):
                lifts[p].start()
            send((1, 2, 0), low)
            gates(level)
            for f in range(T):
                with scope(f"take{f}"):
                    take(1, f)
            with scope("settle"):
                take_queries(1, top)
                for f in range(T):
                    settle(1, f)
            with scope("attend"):
                attend(1, low)
            with scope("gather"):
                hand_over(1, low)
                gathered(1, low)
            with scope("project"):
                for p in range(pieces):
                    send_down(low, p, product(low, p))
            pltpu.make_async_copy(fresh_ref, out_ref, load_sem.at[3]).wait()
            landed(w3.at[own_rows], w_send.at[0])
        elif level == low:
            for w in range(low):
                send((1, 2, 0), w)
            send((1, 2, 0), low)
            send((1, 2, 0), top)
            send((1, 2), T)

            def exchange(p):
                with scope(f"trade{p}"):
                    landed(w3.at[own_rows, cols_of(p)], w_recv.at[p])
                for dg in range(1, groups):
                    trade(p, dg).start()

            def exchanged(p):
                for dg in range(1, groups):
                    theirs = pl.ds(
                        pl.multiple_of(lax.rem(group + groups - dg, groups) * share, 8), share
                    )
                    landed(w3.at[theirs, cols_of(p)], tr_recv.at[p, dg - 1])

            gates(level)
            for p in range(early - 1):
                exchange(p)
            with scope("take_early"):
                for f in (*range(low - 1), low):
                    for s in (0, 1):
                        take(s, f)
                for s in (0, 1):
                    take_queries(s, low)
            with scope("keys"):
                for s in (0, 1):
                    take(s, low - 1, (1,))
            exchange(early - 1)
            for s in (0, 1):
                with scope(f"settle{s}1"):
                    for f in range(low + 1):
                        settle(s, f, (1,))
                with scope(f"attend{s}{low - 1}1"):
                    attend_keys(s, low - 1)
            for s in (0, 1):
                with scope(f"values{s}"):
                    take(s, low - 1, (2,))
                with scope(f"settle{s}2"):
                    for f in range(low + 1):
                        settle(s, f, (2,))
                with scope(f"attend{s}{low - 1}2"):
                    attend_values(s, low - 1)
            for r in reversed(range(low - 1)):
                for s in (0, 1):
                    with scope(f"hand{s}{r + 1}"):
                        hand_over(s, r + 1)
                    with scope(f"q{r + 1}{s}"):
                        take_queries(s, r + 1)
                    with scope(f"attend{s}{r}"):
                        attend(s, r)
            ready = set()
            known = set()
            swapped = False

            def last_frame():
                with scope("take3"):
                    take(0, top)
                    take_queries(0, top)
                    settle(0, top)
                with scope("attend3"):
                    attend(0, low)

            for r, p in order:
                if p >= early and not swapped:
                    swapped = True
                    for q in range(early + 1, pieces):
                        exchange(q)
                if r not in ready:
                    ready.add(r)
                    if r == 0:
                        exchange(early)
                    with scope(f"gather{r}"):
                        for s in (0, 1):
                            if r == 0 and low > 1 or low == 1:
                                hand_over(s, r)
                        for s in (0, 1):
                            gathered(s, r)
                if p not in known:
                    known.add(p)
                    with scope(f"w{p}"):
                        exchanged(p)
                with scope(f"project{r}{p}"):
                    send_down(r, p, product(r, p))
            last_frame()
            with scope("gather3"):
                hand_over(0, low)
                gathered(0, low)
            with scope("project3"):
                for p in range(pieces):
                    pb[low, p] = product(low, p)
            for p in range(pieces):
                with scope(f"finish{p}"):
                    finish(p)
            landed(w3.at[own_rows], tr_send.at[0])
        else:
            if level > 0:
                for k, w in enumerate((low, top)):
                    for dx in range(1, G):
                        sidestep(k, w, dx).start()
                        count["near"] += 1
            for kind in (1, 2):
                for w in (low, top):
                    send((kind,), w)
            for w in (low, top):
                send((0,), w, (0,))
            for w in range(level + 1, low):
                send((1, 2, 0), w)
            for w in range(level):
                send((1, 2, 0), w)
            send((1, 2, 0), level)
            gates(level)
            if level > 0:
                for k, w in enumerate((low, top)):
                    for dx in range(1, G):
                        xs = lax.rem(x + dx, G)
                        landed(qb.at[T + k, xs], q_recv.at[T + k])
                        forward(k, w, level, xs).start()
                        count["q"] += 1
            stages = (
                (range(T - 1), range(T - 3, -1, -1)),
                (range(T - 1, T), range(T - 2, T - 1)),
            )
            if level > 0:
                stages = (
                    (range(level + 1), range(level)),
                    (range(level + 1, T), range(level, T - 1)),
                )
            for frames, rounds in stages:
                for f in frames:
                    with scope(f"take{f}"):
                        if f < top:
                            take(0, f)
                        if f > 0:
                            take_queries(0, f)
                for f in frames:
                    with scope(f"settle{f}"):
                        if f < top:
                            settle(0, f)
                for r in rounds:
                    with scope(f"attend{r}"):
                        if r < low:
                            attend(0, r)
                        else:
                            attend_last()
                for r in rounds:
                    with scope(f"gather{r}"):
                        hand_over(0, r)
                        gathered(0, r)
                    with scope(f"project{r}"):
                        for p in range(pieces):
                            value = product(r, p)
                            if level == 0 and r > 0:
                                send_up(r, p, value)
                            else:
                                pb[r, p] = value
            ups = [
                (q, p) for p in range(pieces) for q in reversed(range(level + 1, T - 1)) if level
            ]
            for n, (r, p) in enumerate(pair for pair in order if pair[0] <= level):
                if r == level:
                    with scope(f"finish{p}"):
                        finish(p)
                else:
                    with scope(f"down{r}{p}"):
                        send_down(r, p, pb[r, p] + from_down(r, p))
                if n >= 3 and ups:
                    q, p = ups.pop(0)
                    with scope(f"up{q}{p}"):
                        send_up(q, p, pb[q, p] + from_up(q, p))
            for q, p in ups:
                send_up(q, p, pb[q, p] + from_up(q, p))
        with scope("sends"):
            if told:
                landed(mb.at[: len(told)], meta_send.at[0])
            landed(kv.at[: count["kv"] // 2, 0, :, 0], kv_send.at[0])
            if count["q"]:
                landed(qb.at[: count["q"], 0], q_send.at[0])
            if count["near"]:
                landed(qb.at[: count["near"], 0], near_send.at[0])
            if level == top:
                landed(so.at[:low], so_send.at[0])
                landed(st.at[:low], st_send.at[0])
            if count["passed"]:
                landed(kv.at[: count["passed"] // 2, 0], pass_send.at[0])
            if count["raised"]:
                landed(kv.at[: count["raised"] // 2, 0], raise_send.at[0])
            if count["ax"]:
                landed(ab.at[: count["ax"], 0, :, :cw], ax_send.at[0])
            if count["ac"]:
                landed(ab.at[: count["ac"] // G, 0], ac_send.at[0])
            if count["down"]:
                landed(down_out.at[: count["down"] // pieces], dn_send.at[0])
            if count["up"]:
                landed(up_out.at[: count["up"] // pieces], up_send.at[0])

    for level in range(T):
        pl.when(t == level)(functools.partial(program, level))


def fused(T, H, heads, groups):
    def on_device_fused(
        queries, keys, values, residual, fresh_frame, out_weight, time_weight, noise_steps, frame_mask
    ):
        level_heads = heads // T
        G = math.gcd(level_heads, H)
        C = H // G
        hp = level_heads // G
        tl = queries.shape[1]
        tokens = tl * H
        width = out_weight.shape[1]
        pieces = width // (2 * HD)
        nb = width // pieces
        meta_rows = -(-(FREQ // HD + T) // 8) * 8
        cw = hp * HD
        bf16, f32 = jnp.bfloat16, jnp.float32
        dma = pltpu.SemaphoreType.DMA
        chunk = (T - 2, pieces, tokens, nb)
        out = pl.pallas_call(
            functools.partial(fused_kernel, T, G, C, hp, pieces, groups),
            out_shape=jax.ShapeDtypeStruct((tokens, width), bf16),
            in_specs=[pl.BlockSpec(memory_space=pltpu.HBM)] * 7
            + [pl.BlockSpec(memory_space=pltpu.SMEM)] * 2,
            out_specs=pl.BlockSpec(memory_space=pltpu.VMEM),
            scratch_shapes=[
                pltpu.VMEM((2 * T, G, tl, cw), bf16),
                pltpu.VMEM((2 * T, C, 2, G, tl, cw), bf16),
                pltpu.VMEM((2 * (T - 1), C, G * tl, G * cw), bf16),
                pltpu.VMEM((2, hp, G * tl, (T - 1) * tokens), bf16),
                pltpu.VMEM((2, hp, G * tl, HD), f32),
                pltpu.VMEM((T, G * tl, cw), bf16),
                pltpu.VMEM((T, 8, G * tl), f32),
                pltpu.VMEM((T, meta_rows, HD), f32),
                pltpu.VMEM((8, FREQ), f32),
                pltpu.VMEM((8, width), f32),
                pltpu.VMEM(out_weight.shape, bf16),
                pltpu.VMEM(out_weight.shape, bf16),
                pltpu.VMEM(time_weight.shape, bf16),
                pltpu.VMEM((tokens, width), bf16),
                pltpu.VMEM((T - 1, pieces, tokens, nb), f32),
                pltpu.VMEM(chunk, bf16),
                pltpu.VMEM(chunk, bf16),
                pltpu.VMEM(chunk, bf16),
                pltpu.VMEM(chunk, bf16),
                dma((4,)),
                dma((1,)),
                dma((1,)),
                dma((1,)),
                dma((1,)),
                dma((2, 2 * T)),
                dma((2 * T,)),
                dma((1,)),
                dma((2, 2 * T, C - 1)),
                dma((1,)),
                dma((1,)),
                dma((2 * (T - 1), G - 1)),
                dma((1,)),
                dma((2 * (T - 1), C - 1)),
                dma((1,)),
                dma((T - 2, pieces)),
                dma((1,)),
                dma((T - 2, pieces)),
                dma((1,)),
                dma((pieces,)),
                dma((1,)),
                dma((pieces, groups - 1)),
                dma((1,)),
                dma((1,)),
                dma((1,)),
                dma((1,)),
                dma((1,)),
            ],
            compiler_params=pltpu.CompilerParams(
                collective_id=0, has_side_effects=True, vmem_limit_bytes=32 * 1024 * 1024
            ),
        )(
            *(
                pltpu.with_memory_space_constraint(array, pltpu.HBM)
                for array in (
                    queries, keys, values, residual, fresh_frame, out_weight, time_weight
                )
            ),
            noise_steps,
            frame_mask,
        )
        return out[None]

    return on_device_fused


def solution(mesh):
    placed = (
        P(("groups", "tm"), "head", None),
        P(("groups", "tm"), "head", None),
        P(("groups", "tm"), "head", None),
        P(("groups", "tm"), None, "head"),
        P("groups", "head"),
        P("tm", "head"),
        P(None, "head"),
        P(("groups", "tm")),
        P(("groups", "tm"), None),
    )
    def whole(*args):
        frames, spread = mesh.shape["tm"], mesh.shape["head"]
        heads = args[0].shape[2] // HD
        fits = 2 < frames <= 4 and heads % frames == 0 and args[5].shape[1] % (spread * 2 * HD) == 0
        return jax.shard_map(
            fused(frames, spread, heads, mesh.shape["groups"]) if fits else on_device,
            mesh=mesh,
            in_specs=placed,
            out_specs=P(("groups", "tm"), None, "head"),
            check_vma=False,
        )(*args)

    return whole
```

```python
import functools
import math

import jax
import jax.numpy as jnp
from jax import lax
from jax.experimental import pallas as pl
from jax.experimental.pallas import tpu as pltpu
from jax.sharding import PartitionSpec as P

HD = 128
FREQ = 256
STEPS = 50


def shifted(value, axis, steps):
    count = lax.axis_size(axis)
    leading, last = (max(0, -steps), min(count, count - steps))
    return lax.ppermute(value, axis, [(source, source + steps) for source in range(leading, last)])


def time_features(noise_steps):
    timestep = 1000.0 * (noise_steps.astype(jnp.float32) + 1.0) / STEPS
    half = FREQ // 2
    rates = jnp.exp(-math.log(10000.0) * jnp.arange(half).astype(jnp.float32) / half)
    angles = timestep[:, None] * rates[None, :]
    return jnp.concatenate([jnp.cos(angles), jnp.sin(angles)], axis=1)


def on_device(
    queries, keys, values, residual, fresh_frame, out_weight, time_weight, noise_steps, frame_mask
):
    query_local, key_local, value_local = (
        lax.all_to_all(queries, "head", split_axis=2, concat_axis=1, tiled=True),
        lax.all_to_all(keys, "head", split_axis=2, concat_axis=1, tiled=True),
        lax.all_to_all(values, "head", split_axis=2, concat_axis=1, tiled=True),
    )
    tokens = query_local.shape[1]
    heads_here = query_local.shape[2] // HD
    scale = 1.0 / math.sqrt(HD)
    query_heads = query_local[0].reshape(tokens, heads_here, HD)
    key_value = jnp.stack([key_local[0], value_local[0]], axis=0)
    frame = lax.axis_index("tm")
    frames_total = lax.axis_size("tm")
    window = min(8, frames_total)
    mask_row = frame_mask[0]
    columns = jnp.arange(mask_row.shape[0], dtype=jnp.int32)

    def allowed_at(offset):
        hits = jnp.sum(jnp.where(columns == frame - offset, mask_row, 0))
        return hits > 0

    def absorb(state, block, allowed):
        running_max, weight_sum, accumulated = state
        key_heads = block[0].reshape(tokens, heads_here, HD)
        value_heads = block[1].reshape(tokens, heads_here, HD)
        scores = (
            jnp.einsum("qhd,khd->hqk", query_heads, key_heads, preferred_element_type=jnp.float32)
            * scale
        )
        new_max = jnp.where(allowed, jnp.maximum(running_max, jnp.max(scores, axis=2)), running_max)
        lifted = jnp.where(allowed, jnp.exp(jnp.minimum(scores - new_max[:, :, None], 0.0)), 0.0)
        factor = jnp.exp(running_max - new_max)
        weight_sum = weight_sum * factor + jnp.sum(lifted, axis=2)
        rounded = lifted.astype(jnp.bfloat16)
        accumulated = accumulated * jnp.transpose(factor)[:, :, None] + jnp.einsum(
            "hqk,khd->qhd", rounded, value_heads, preferred_element_type=jnp.float32
        )
        return (new_max, weight_sum, accumulated)

    state = (
        jnp.full((heads_here, tokens), -1e30, jnp.float32),
        jnp.zeros((heads_here, tokens), jnp.float32),
        jnp.zeros((tokens, heads_here, HD), jnp.float32),
    )
    state = absorb(state, key_value, allowed_at(0))
    moving = key_value
    for offset in range(1, window):
        moving = shifted(moving, "tm", 1)
        state = absorb(state, moving, allowed_at(offset))
    running_max, weight_sum, accumulated = state
    attention = (
        (accumulated / jnp.transpose(weight_sum)[:, :, None])
        .reshape(tokens, heads_here * HD)
        .astype(jnp.bfloat16)
    )
    weight_cols = lax.all_gather(out_weight, "tm", axis=0, tiled=True)
    projected = jnp.dot(
        lax.all_gather(attention, "head", axis=1, tiled=True),
        weight_cols,
        preferred_element_type=jnp.float32,
    )
    gate = jnp.dot(
        time_features(noise_steps), time_weight.astype(jnp.float32), precision=lax.Precision.HIGHEST
    )
    updated = (residual[0].astype(jnp.float32) + gate * projected).astype(jnp.bfloat16)
    moved = shifted(updated, "tm", -1)
    rolled = jnp.where(frame == frames_total - 1, fresh_frame, moved)
    return rolled[None]


def fused_kernel(
    T, G, C, hp, pieces, groups,
    q_ref, k_ref, v_ref, res_ref, fresh_ref, w_ref, tw_ref, steps_ref, mask_ref,
    out_ref,
    qb, kv, ab, lb, tb, so, st, mb, fb, gb, wb, w3, twb, rb, pb, down_out, down_in, up_out, up_in,
    load_sem, meta_send, meta_recv, kv_send, q_send, kv_recv, q_recv, pass_send, pass_recv,
    raise_send, ax_send, ax_recv, ac_send, ac_recv, dn_send, dn_recv, up_send, up_recv,
    w_send, w_recv, tr_send, tr_recv, near_send, so_send, so_recv, st_send, st_recv,
):
    t = lax.axis_index("tm")
    h = lax.axis_index("head")
    group = lax.axis_index("groups")
    x = h // C
    c = lax.rem(h, C)
    H = G * C
    tl = q_ref.shape[1]
    cw = hp * HD
    tokens = tl * H
    half = G * tl
    nb = w_ref.shape[1] // pieces
    mask_row = FREQ // HD
    share = w_ref.shape[0] // groups
    top, low = T - 1, T - 2
    scale = 1.0 / math.sqrt(HD)

    def to(tt, hh):
        return dict(device_id={"tm": tt, "head": hh}, device_id_type=pl.DeviceIdType.MESH)

    def beside(dg):
        return dict(
            device_id={"groups": lax.rem(group + dg, groups)}, device_id_type=pl.DeviceIdType.MESH
        )

    def landed(ref, sem):
        pltpu.make_async_copy(ref, ref, sem).wait()

    def cols_of(p):
        return slice(p * nb, (p + 1) * nb)

    def reaches(one, other):
        return one == other or (other < top or one == low)

    barrier = pltpu.get_barrier_semaphore()

    def entered(level):
        awaited = C - 1 + (groups - 1 if level == low else 0)
        for other in range(T):
            awaited += (G - 1 if other == level else G) * reaches(level, other)
        return awaited

    def announce(level):
        for other in reversed(range(T)):
            for dx in range(1 if other == level else 0, G):
                if reaches(other, level):
                    pl.semaphore_signal(
                        barrier, inc=1, **to(other, lax.rem(x + dx, G) * C + c)
                    )
        for dc in range(1, C):
            pl.semaphore_signal(barrier, inc=1, **to(level, x * C + lax.rem(c + dc, C)))
        if level == low:
            for dg in range(1, groups):
                pl.semaphore_signal(barrier, inc=1, **beside(dg))

    for level in range(T):
        pl.when(t == level)(functools.partial(announce, level))

    loads = [
        pltpu.make_async_copy(tw_ref, twb, load_sem.at[0]),
        pltpu.make_async_copy(w_ref, wb, load_sem.at[1]),
        pltpu.make_async_copy(res_ref.at[0], rb, load_sem.at[2]),
    ]
    for copy in loads:
        copy.start()

    @pl.when(t == top)
    def _():
        pltpu.make_async_copy(fresh_ref, out_ref, load_sem.at[3]).start()

    def features():
        timestep = 1000.0 * (jnp.full((1, HD), steps_ref[0], jnp.int32).astype(jnp.float32) + 1.0) / STEPS
        place = lax.broadcasted_iota(jnp.int32, (1, HD), 1).astype(jnp.float32)
        angles = timestep * jnp.exp(-math.log(10000.0) * place / (FREQ // 2))
        mb[t, 0:1, :] = jnp.cos(angles)
        mb[t, 1:2, :] = jnp.sin(angles)
        for g in range(T):
            row = mask_row + g
            mb[t, row : row + 1, :] = jnp.full((1, HD), mask_ref[0, g], jnp.int32).astype(jnp.float32)

    sources = (q_ref, k_ref, v_ref)

    def slot(kind, s, f, xs):
        return qb.at[s * T + f, xs] if kind == 0 else kv.at[s * T + f, c, kind - 1, xs]

    def sems(kind, s, f):
        if kind == 0:
            return q_send.at[0], q_recv.at[s * T + f]
        return kv_send.at[0], kv_recv.at[kind - 1, s * T + f]

    def block(kind, w, xx):
        column = pl.multiple_of((w * G + xx) * cw, HD)
        return sources[kind].at[0, :, pl.ds(column, cw)]

    def aim(f, key):
        w = min(key, top)
        if key < top:
            return w, 0, w
        return w, 1, (low if key == top and f < top else top)

    def outgoing(kind, f, key, dx):
        w, s, level = aim(f, key)
        xx = lax.rem(x + dx, G)
        leaves, lands = sems(kind, s, f)
        return pltpu.make_async_remote_copy(
            src_ref=block(kind, w, xx), dst_ref=slot(kind, s, f, x),
            send_sem=leaves, recv_sem=lands, **to(level, xx * C + c),
        )

    def own(kind, f, key):
        w, s, _ = aim(f, key)
        return pltpu.make_async_copy(block(kind, w, x), slot(kind, s, f, x), sems(kind, s, f)[1])

    def passed(i, kind, dc):
        return pltpu.make_async_remote_copy(
            src_ref=kv.at[i, c, kind - 1], dst_ref=kv.at[i, c, kind - 1],
            send_sem=pass_send.at[0], recv_sem=pass_recv.at[kind - 1, i, dc - 1],
            **to(t, x * C + lax.rem(c + dc, C)),
        )

    def raised(i, kind):
        return pltpu.make_async_remote_copy(
            src_ref=kv.at[i, c, kind - 1], dst_ref=kv.at[i, c, kind - 1],
            send_sem=raise_send.at[0], recv_sem=kv_recv.at[kind - 1, i], **to(top, h),
        )

    def near(kind, w, dx):
        xx = lax.rem(x + dx, G)
        leaves, lands = sems(kind, 0, w)
        if dx == 0:
            return pltpu.make_async_copy(block(kind, w, x), slot(kind, 0, w, x), lands)
        return pltpu.make_async_remote_copy(
            src_ref=block(kind, w, xx), dst_ref=slot(kind, 0, w, x),
            send_sem=near_send.at[0] if kind == 0 else leaves, recv_sem=lands,
            **to(top, xx * C + c),
        )

    def sidestep(k, key, dx):
        return pltpu.make_async_remote_copy(
            src_ref=block(0, key, lax.rem(x + dx, G)), dst_ref=qb.at[T + k, x],
            send_sem=near_send.at[0], recv_sem=q_recv.at[T + k],
            **to(t, lax.rem(x + dx, G) * C + c),
        )

    def forward(k, key, f, xs):
        return pltpu.make_async_remote_copy(
            src_ref=qb.at[T + k, xs], dst_ref=slot(0, k, f, xs),
            send_sem=q_send.at[0], recv_sem=q_recv.at[k * T + f], **to(low, h),
        )

    def handed(w):
        return [
            pltpu.make_async_remote_copy(
                src_ref=buffer.at[w], dst_ref=buffer.at[top],
                send_sem=leaves.at[0], recv_sem=lands.at[0], **to(w, h),
            )
            for buffer, leaves, lands in ((so, so_send, so_recv), (st, st_send, st_recv))
        ]

    own_rows = pl.ds(pl.multiple_of(group * share, 8), share)

    def lift(p):
        return pltpu.make_async_remote_copy(
            src_ref=w_ref.at[own_rows, cols_of(p)], dst_ref=w3.at[own_rows, cols_of(p)],
            send_sem=w_send.at[0], recv_sem=w_recv.at[p], **to(low, h),
        )

    def trade(p, dg):
        return pltpu.make_async_remote_copy(
            src_ref=w3.at[own_rows, cols_of(p)], dst_ref=w3.at[own_rows, cols_of(p)],
            send_sem=tr_send.at[0], recv_sem=tr_recv.at[p, dg - 1], **beside(dg),
        )

    def mine(i, column, size):
        return ab.at[i, c, :, pl.ds(pl.multiple_of(column, HD), size)]

    def across(i, dx):
        here = mine(i, x * cw, cw)
        return pltpu.make_async_remote_copy(
            src_ref=here, dst_ref=here, send_sem=ax_send.at[0], recv_sem=ax_recv.at[i, dx - 1],
            **to(t, lax.rem(x + dx, G) * C + c),
        )

    def aside(i, xs, dc):
        here = mine(i, xs * cw, cw)
        return pltpu.make_async_remote_copy(
            src_ref=here, dst_ref=here, send_sem=ac_send.at[0], recv_sem=ac_recv.at[i, dc - 1],
            **to(t, x * C + lax.rem(c + dc, C)),
        )

    def spot(r):
        return r % (T - 2)

    def down(level, r, p):
        return pltpu.make_async_remote_copy(
            src_ref=down_out.at[spot(r), p], dst_ref=down_in.at[spot(r), p],
            send_sem=dn_send.at[0], recv_sem=dn_recv.at[spot(r), p], **to(level - 1, h),
        )

    def up(level, r, p):
        return pltpu.make_async_remote_copy(
            src_ref=up_out.at[spot(r), p], dst_ref=up_in.at[spot(r), p],
            send_sem=up_send.at[0], recv_sem=up_recv.at[spot(r), p], **to(level + 1, h),
        )

    def gates(level):
        with jax.named_scope("loads"):
            for copy in loads:
                copy.wait()
        with jax.named_scope("meta"):
            fb[...] = jnp.zeros_like(fb)
            away = [f for f in range(1, T) if level != f and level < top]
            if away:
                landed(mb.at[: len(away)], meta_recv.at[0])
            for f in range(1, T) if level < top else (top,):
                for b in range(mask_row):
                    fb[f : f + 1, b * HD : (b + 1) * HD] = mb[f, b : b + 1, :]
        with jax.named_scope("gate"):
            gb[...] = jnp.dot(
                fb[...], twb[...].astype(jnp.float32),
                precision=lax.Precision.HIGHEST, preferred_element_type=jnp.float32,
            )

    def program(level):
        if level < top:
            features()
        with jax.named_scope("barrier"):
            pl.semaphore_wait(barrier, entered(level))
        if level == top:
            lifts = [lift(p) for p in range(pieces)]
            lifts[0].start()
            features()
        told = [other for other in range(top) if other != level and level > 0]
        for other in told:
            pltpu.make_async_remote_copy(
                src_ref=mb.at[t], dst_ref=mb.at[t], send_sem=meta_send.at[0],
                recv_sem=meta_recv.at[0], **to(other, h),
            ).start()
        count = dict(kv=0, q=0, passed=0, raised=0, near=0, ax=0, ac=0, down=0, up=0, traded=0)

        def send(kinds, key, dxs=tuple(reversed(range(G)))):
            for dx in dxs:
                for kind in kinds:
                    if kind == 0 and level == 0:
                        continue
                    if dx == 0 and aim(level, key)[2] == level:
                        own(kind, level, key).start()
                    else:
                        outgoing(kind, level, key, dx).start()
                        count["q" if kind == 0 else "kv"] += 1

        def take(s, f, kinds=(1, 2)):
            i = s * T + f
            for kind in kinds:
                landed(kv.at[i, c, kind - 1], kv_recv.at[kind - 1, i])
                for dc in range(1, C):
                    passed(i, kind, dc).start()
                    count["passed"] += 1
                if s == 1 and level == low and f < low:
                    raised(i, kind).start()
                    count["raised"] += 1

        def take_queries(s, f):
            landed(qb.at[s * T + f], q_recv.at[s * T + f])

        def settle(s, f, kinds=(1, 2)):
            i = s * T + f
            for kind in kinds:
                for dc in range(1, C):
                    landed(
                        kv.at[i, lax.rem(c + C - dc, C), kind - 1],
                        pass_recv.at[kind - 1, i, dc - 1],
                    )

        def weigh(s, r, j):
            f = r + 1
            keys_here = (f + 1) * tokens
            allowed = jnp.concatenate(
                [
                    jnp.broadcast_to(mb[f, mask_row + g : mask_row + g + 1, 0:1], (1, tokens))
                    for g in range(f + 1)
                ],
                axis=1,
            )
            cols = slice(j * HD, (j + 1) * HD)
            query = qb[s * T + f, :, :, cols].reshape(half, HD)
            key = kv[s * T : s * T + f + 1, :, 0, :, :, cols].reshape(keys_here, HD)
            scores = (
                lax.dot_general(
                    query, key, (((1,), (1,)), ((), ())), preferred_element_type=jnp.float32
                )
                * scale
            )
            scores = jnp.where(allowed > 0.5, scores, -1e30)
            peak = jnp.max(scores, axis=1, keepdims=True)
            lifted = jnp.exp(scores - peak)
            return lifted.astype(jnp.bfloat16), jnp.sum(lifted, axis=1, keepdims=True)

        def mix(s, r, j, rounded, total):
            f = r + 1
            cols = slice(j * HD, (j + 1) * HD)
            value = kv[s * T : s * T + f + 1, :, 1, :, :, cols].reshape((f + 1) * tokens, HD)
            mixed = jnp.dot(rounded, value, preferred_element_type=jnp.float32)
            here = pl.ds(pl.multiple_of(x * cw + j * HD, HD), HD)
            ab[s * (T - 1) + r, c, :, here] = (mixed / total).astype(jnp.bfloat16)

        def attend_own(w):
            lane = lax.broadcasted_iota(jnp.int32, (half, HD), 1)
            stats = jnp.zeros((half, HD), jnp.float32)
            for j in range(hp):
                cols = slice(j * HD, (j + 1) * HD)
                query = qb[w, :, :, cols].reshape(half, HD)
                key = kv[w, :, 0, :, :, cols].reshape(tokens, HD)
                value = kv[w, :, 1, :, :, cols].reshape(tokens, HD)
                scores = (
                    lax.dot_general(
                        query, key, (((1,), (1,)), ((), ())), preferred_element_type=jnp.float32
                    )
                    * scale
                )
                peak = jnp.max(scores, axis=1, keepdims=True)
                lifted = jnp.exp(scores - peak)
                total = jnp.sum(lifted, axis=1, keepdims=True)
                mixed = jnp.dot(
                    lifted.astype(jnp.bfloat16), value, preferred_element_type=jnp.float32
                )
                so[w, :, cols] = (mixed / total).astype(jnp.bfloat16)
                stats = jnp.where(lane == 2 * j, peak, stats)
                stats = jnp.where(lane == 2 * j + 1, total, stats)
            st[w] = jnp.transpose(stats)[:8]
            for copy in handed(w):
                copy.start()

        def attend_last():
            landed(so.at[top], so_recv.at[0])
            landed(st.at[top], st_recv.at[0])
            stats = jnp.transpose(
                jnp.concatenate([st[top], jnp.zeros((HD - 8, half), jnp.float32)], axis=0)
            )
            allowed = jnp.concatenate(
                [
                    jnp.broadcast_to(mb[top, mask_row + g : mask_row + g + 1, 0:1], (1, tokens))
                    for g in range(top)
                ],
                axis=1,
            )
            for j in range(hp):
                cols = slice(j * HD, (j + 1) * HD)
                query = qb[top, :, :, cols].reshape(half, HD)
                key = kv[0:top, :, 0, :, :, cols].reshape(top * tokens, HD)
                value = kv[0:top, :, 1, :, :, cols].reshape(top * tokens, HD)
                scores = (
                    lax.dot_general(
                        query, key, (((1,), (1,)), ((), ())), preferred_element_type=jnp.float32
                    )
                    * scale
                )
                scores = jnp.where(allowed > 0.5, scores, -1e30)
                their_peak = stats[:, 2 * j : 2 * j + 1]
                peak = jnp.maximum(jnp.max(scores, axis=1, keepdims=True), their_peak)
                lifted = jnp.exp(scores - peak)
                theirs = jnp.exp(their_peak - peak) * stats[:, 2 * j + 1 : 2 * j + 2]
                total = jnp.sum(lifted, axis=1, keepdims=True) + theirs
                mixed = jnp.dot(
                    lifted.astype(jnp.bfloat16), value, preferred_element_type=jnp.float32
                )
                mixed += theirs * so[top, :, cols].astype(jnp.float32)
                here = pl.ds(pl.multiple_of(x * cw + j * HD, HD), HD)
                ab[low, c, :, here] = (mixed / total).astype(jnp.bfloat16)
            share_out(0, low)

        def share_out(s, r):
            i = s * (T - 1) + r
            for dx in range(1, G):
                across(i, dx).start()
                count["ax"] += 1
            for dc in range(1, C):
                aside(i, x, dc).start()
                count["ac"] += 1

        def attend(s, r):
            for j in range(hp):
                mix(s, r, j, *weigh(s, r, j))
            share_out(s, r)

        def attend_keys(s, r):
            for j in range(hp):
                rounded, total = weigh(s, r, j)
                lb[s, j] = rounded
                tb[s, j] = jnp.broadcast_to(total, (half, HD))

        def attend_values(s, r):
            for j in range(hp):
                mix(s, r, j, lb[s, j], tb[s, j])
            share_out(s, r)

        def hand_over(s, r):
            i = s * (T - 1) + r
            for dx in range(1, G):
                xs = lax.rem(x + G - dx, G)
                landed(mine(i, xs * cw, cw), ax_recv.at[i, dx - 1])
                for dc in range(1, C):
                    aside(i, xs, dc).start()
                    count["ac"] += 1

        def gathered(s, r):
            i = s * (T - 1) + r
            for dc in range(1, C):
                landed(ab.at[i, lax.rem(c + C - dc, C)], ac_recv.at[i, dc - 1])

        def product(r, p):
            if level == top:
                parts = ((1, wb),)
            elif level == low and r < low:
                parts = ((0, wb), (1, w3))
            else:
                parts = ((0, wb),)
            partial = 0.0
            for s, weight in parts:
                partial += jnp.dot(
                    ab[s * (T - 1) + r].reshape(tokens, G * cw), weight[:, cols_of(p)],
                    preferred_element_type=jnp.float32,
                )
            partial = partial * gb[r + 1 : r + 2, cols_of(p)]
            if level == r + 1:
                moved = [
                    rb[(xs * C + cs) * tl : (xs * C + cs + 1) * tl, cols_of(p)]
                    for cs in range(C)
                    for xs in range(G)
                ]
                partial += jnp.concatenate(moved, axis=0).astype(jnp.float32)
            return partial

        def part(r, p, dc, going_up):
            cc = lax.rem(c + dc, C)
            parts = ((0, wb), (1, w3)) if level == low and r < low else ((0, wb),)
            partial = 0.0
            for s, weight in parts:
                partial += jnp.dot(
                    ab[s * (T - 1) + r, cc], weight[:, cols_of(p)],
                    preferred_element_type=jnp.float32,
                )
            partial = partial * gb[r + 1 : r + 2, cols_of(p)]
            if level == r + 1:
                moved = [
                    rb[pl.ds(pl.multiple_of((xs * C + cc) * tl, tl), tl), cols_of(p)]
                    for xs in range(G)
                ]
                partial += jnp.concatenate(moved, axis=0).astype(jnp.float32)
            rows = pl.ds(pl.multiple_of(cc * half, half), half)
            out, into = (up_out, up_in) if going_up else (down_out, down_in)
            leaves, lands = (up_send, up_recv) if going_up else (dn_send, dn_recv)
            out[spot(r), p, rows, :] = partial.astype(jnp.bfloat16)
            pltpu.make_async_remote_copy(
                src_ref=out.at[spot(r), p, rows], dst_ref=into.at[spot(r), p, rows],
                send_sem=leaves.at[0], recv_sem=lands.at[spot(r), p],
                **to(level + 1 if going_up else level - 1, h),
            ).start()

        def own_parts(r, going_up=False):
            for p in range(2):
                with scope(f"own{r}{p}"):
                    part(r, p, 0, going_up)
                count["up" if going_up else "down"] += 1

        def other_parts(r, going_up=False):
            for p in range(2):
                for dc in range(1, C):
                    with scope(f"other{r}{p}"):
                        part(r, p, dc, going_up)

        def send_down(r, p, value):
            down_out[spot(r), p] = value.astype(jnp.bfloat16)
            down(level, r, p).start()
            count["down"] += 1

        def send_up(r, p, value):
            up_out[spot(r), p] = value.astype(jnp.bfloat16)
            up(level, r, p).start()
            count["up"] += 1

        def from_down(r, p):
            landed(down_in.at[spot(r), p], dn_recv.at[spot(r), p])
            return down_in[spot(r), p].astype(jnp.float32)

        def from_up(r, p):
            landed(up_in.at[spot(r), p], up_recv.at[spot(r), p])
            return up_in[spot(r), p].astype(jnp.float32)

        def finish(p):
            r = level
            total = pb[r, p] + from_down(r, p)
            if r > 0:
                total += from_up(r, p)
            total = total.astype(out_ref.dtype)
            for cs in range(C):
                for xs in range(G):
                    row, token = (cs * G + xs) * tl, (xs * C + cs) * tl
                    out_ref[token : token + tl, cols_of(p)] = total[row : row + tl]

        scope = jax.named_scope
        early = (3 * pieces) // 5
        order = [(low - 1, p) for p in range(2)]
        order += [(r, p) for r in range(low - 1) for p in range(pieces)]
        order += [(low - 1, p) for p in range(2, pieces)]

        if level == top:
            for p in range(1, early):
                lifts[p].start()
            lower = tuple(reversed(range(low)))
            for w in lower:
                for dx in reversed(range(G)):
                    for kind in (1, 0, 2):
                        near(kind, w, dx).start()
                        if dx > 0:
                            count["near" if kind == 0 else "kv"] += 1
            for w in lower:
                send((0,), w)
            send((0, 1, 2), top)
            for w in lower:
                with scope(f"near{w}"):
                    take(0, w)
                    take_queries(0, w)
            for w in lower:
                with scope(f"own{w}"):
                    settle(0, w)
                    attend_own(w)
            for p in range(early, pieces):
                lifts[p].start()
            send((1, 2, 0), low)
            gates(level)
            for f in range(T):
                with scope(f"take{f}"):
                    take(1, f)
            with scope("settle"):
                take_queries(1, top)
                for f in range(T):
                    settle(1, f)
            with scope("attend"):
                attend(1, low)
            with scope("gather"):
                hand_over(1, low)
                gathered(1, low)
            with scope("project"):
                for p in range(pieces):
                    send_down(low, p, product(low, p))
            pltpu.make_async_copy(fresh_ref, out_ref, load_sem.at[3]).wait()
            landed(w3.at[own_rows], w_send.at[0])
        elif level == low:
            for w in range(low):
                send((1, 2, 0), w)
            send((1, 2, 0), low)
            send((1, 2, 0), top)
            send((1, 2), T)

            def exchange(p):
                with scope(f"trade{p}"):
                    landed(w3.at[own_rows, cols_of(p)], w_recv.at[p])
                for dg in range(1, groups):
                    trade(p, dg).start()

            def exchanged(p):
                for dg in range(1, groups):
                    theirs = pl.ds(
                        pl.multiple_of(lax.rem(group + groups - dg, groups) * share, 8), share
                    )
                    landed(w3.at[theirs, cols_of(p)], tr_recv.at[p, dg - 1])

            gates(level)
            for p in range(early - 1):
                exchange(p)
            with scope("take_early"):
                for f in (*range(low - 1), low):
                    for s in (0, 1):
                        take(s, f)
                for s in (0, 1):
                    take_queries(s, low)
            with scope("keys"):
                for s in (0, 1):
                    take(s, low - 1, (1,))
            exchange(early - 1)
            for s in (0, 1):
                with scope(f"settle{s}1"):
                    for f in range(low + 1):
                        settle(s, f, (1,))
                with scope(f"attend{s}{low - 1}1"):
                    attend_keys(s, low - 1)
            for s in (0, 1):
                with scope(f"values{s}"):
                    take(s, low - 1, (2,))
                with scope(f"settle{s}2"):
                    for f in range(low + 1):
                        settle(s, f, (2,))
                with scope(f"attend{s}{low - 1}2"):
                    attend_values(s, low - 1)
            for r in reversed(range(low - 1)):
                for s in (0, 1):
                    with scope(f"hand{s}{r + 1}"):
                        hand_over(s, r + 1)
                    if s == 1:
                        for p in range(2):
                            exchanged(p)
                        own_parts(r + 1)
                    with scope(f"q{r + 1}{s}"):
                        take_queries(s, r + 1)
                    with scope(f"attend{s}{r}"):
                        attend(s, r)
            ready = set()
            known = {0, 1} if low > 1 else set()
            swapped = False

            def last_frame():
                with scope("take3"):
                    take(0, top)
                    take_queries(0, top)
                    settle(0, top)
                with scope("attend3"):
                    attend(0, low)

            for r, p in order:
                if p >= early and not swapped:
                    swapped = True
                    for q in range(early + 1, pieces):
                        exchange(q)
                if r not in ready:
                    ready.add(r)
                    if r == 0:
                        exchange(early)
                    if r == 0:
                        for s in (0, 1):
                            with scope(f"hand{s}{r}"):
                                hand_over(s, r)
                        for q in range(2):
                            if q not in known:
                                known.add(q)
                                exchanged(q)
                        own_parts(r)
                    with scope(f"gather{r}"):
                        for s in (0, 1):
                            gathered(s, r)
                    other_parts(r)
                if p < 2:
                    continue
                if p not in known:
                    known.add(p)
                    with scope(f"w{p}"):
                        exchanged(p)
                with scope(f"project{r}{p}"):
                    send_down(r, p, product(r, p))
            last_frame()
            with scope("gather3"):
                hand_over(0, low)
                gathered(0, low)
            with scope("project3"):
                for p in range(pieces):
                    pb[low, p] = product(low, p)
            for p in range(pieces):
                with scope(f"finish{p}"):
                    finish(p)
            landed(w3.at[own_rows], tr_send.at[0])
        else:
            if level > 0:
                for k, w in enumerate((low, top)):
                    for dx in range(1, G):
                        sidestep(k, w, dx).start()
                        count["near"] += 1
            for kind in (1, 2):
                for w in (low, top):
                    send((kind,), w)
            for w in (low, top):
                send((0,), w, (0,))
            for w in range(level + 1, low):
                send((1, 2, 0), w)
            for w in range(level):
                send((1, 2, 0), w)
            send((1, 2, 0), level)
            gates(level)
            if level > 0:
                for k, w in enumerate((low, top)):
                    for dx in range(1, G):
                        xs = lax.rem(x + dx, G)
                        landed(qb.at[T + k, xs], q_recv.at[T + k])
                        forward(k, w, level, xs).start()
                        count["q"] += 1
            stages = (
                (range(T - 1), range(T - 3, -1, -1)),
                (range(T - 1, T), range(T - 2, T - 1)),
            )
            if level > 0:
                stages = (
                    (range(level + 1), range(level)),
                    (range(level + 1, T), range(level, T - 1)),
                )
            for frames, rounds in stages:
                for f in frames:
                    with scope(f"take{f}"):
                        if f < top:
                            take(0, f)
                        if f > 0:
                            take_queries(0, f)
                for f in frames:
                    with scope(f"settle{f}"):
                        if f < top:
                            settle(0, f)
                for r in rounds:
                    with scope(f"attend{r}"):
                        if r < low:
                            attend(0, r)
                        else:
                            attend_last()
                for r in rounds:
                    early_up = level == 0 and 0 < r < low
                    with scope(f"gather{r}"):
                        hand_over(0, r)
                    if early_up:
                        own_parts(r, True)
                    with scope(f"pair{r}"):
                        gathered(0, r)
                    if early_up:
                        other_parts(r, True)
                    with scope(f"project{r}"):
                        for p in range(2 if early_up else 0, pieces):
                            value = product(r, p)
                            if level == 0 and r > 0:
                                send_up(r, p, value)
                            else:
                                pb[r, p] = value
            ups = [
                (q, p) for p in range(pieces) for q in reversed(range(level + 1, T - 1)) if level
            ]
            for n, (r, p) in enumerate(pair for pair in order if pair[0] <= level):
                if r == level:
                    with scope(f"finish{p}"):
                        finish(p)
                else:
                    with scope(f"down{r}{p}"):
                        send_down(r, p, pb[r, p] + from_down(r, p))
                if n >= 3 and ups:
                    q, p = ups.pop(0)
                    with scope(f"up{q}{p}"):
                        send_up(q, p, pb[q, p] + from_up(q, p))
            for q, p in ups:
                send_up(q, p, pb[q, p] + from_up(q, p))
        with scope("sends"):
            if told:
                landed(mb.at[: len(told)], meta_send.at[0])
            landed(kv.at[: count["kv"] // 2, 0, :, 0], kv_send.at[0])
            if count["q"]:
                landed(qb.at[: count["q"], 0], q_send.at[0])
            if count["near"]:
                landed(qb.at[: count["near"], 0], near_send.at[0])
            if level == top:
                landed(so.at[:low], so_send.at[0])
                landed(st.at[:low], st_send.at[0])
            if count["passed"]:
                landed(kv.at[: count["passed"] // 2, 0], pass_send.at[0])
            if count["raised"]:
                landed(kv.at[: count["raised"] // 2, 0], raise_send.at[0])
            if count["ax"]:
                landed(ab.at[: count["ax"], 0, :, :cw], ax_send.at[0])
            if count["ac"]:
                landed(ab.at[: count["ac"] // G, 0], ac_send.at[0])
            if count["down"]:
                landed(down_out.at[: count["down"] // pieces], dn_send.at[0])
            if count["up"]:
                landed(up_out.at[: count["up"] // pieces], up_send.at[0])

    for level in range(T):
        pl.when(t == level)(functools.partial(program, level))


def fused(T, H, heads, groups):
    def on_device_fused(
        queries, keys, values, residual, fresh_frame, out_weight, time_weight, noise_steps, frame_mask
    ):
        level_heads = heads // T
        G = math.gcd(level_heads, H)
        C = H // G
        hp = level_heads // G
        tl = queries.shape[1]
        tokens = tl * H
        width = out_weight.shape[1]
        pieces = width // (2 * HD)
        nb = width // pieces
        meta_rows = -(-(FREQ // HD + T) // 8) * 8
        cw = hp * HD
        bf16, f32 = jnp.bfloat16, jnp.float32
        dma = pltpu.SemaphoreType.DMA
        chunk = (T - 2, pieces, tokens, nb)
        out = pl.pallas_call(
            functools.partial(fused_kernel, T, G, C, hp, pieces, groups),
            out_shape=jax.ShapeDtypeStruct((tokens, width), bf16),
            in_specs=[pl.BlockSpec(memory_space=pltpu.HBM)] * 7
            + [pl.BlockSpec(memory_space=pltpu.SMEM)] * 2,
            out_specs=pl.BlockSpec(memory_space=pltpu.VMEM),
            scratch_shapes=[
                pltpu.VMEM((2 * T, G, tl, cw), bf16),
                pltpu.VMEM((2 * T, C, 2, G, tl, cw), bf16),
                pltpu.VMEM((2 * (T - 1), C, G * tl, G * cw), bf16),
                pltpu.VMEM((2, hp, G * tl, (T - 1) * tokens), bf16),
                pltpu.VMEM((2, hp, G * tl, HD), f32),
                pltpu.VMEM((T, G * tl, cw), bf16),
                pltpu.VMEM((T, 8, G * tl), f32),
                pltpu.VMEM((T, meta_rows, HD), f32),
                pltpu.VMEM((8, FREQ), f32),
                pltpu.VMEM((8, width), f32),
                pltpu.VMEM(out_weight.shape, bf16),
                pltpu.VMEM(out_weight.shape, bf16),
                pltpu.VMEM(time_weight.shape, bf16),
                pltpu.VMEM((tokens, width), bf16),
                pltpu.VMEM((T - 1, pieces, tokens, nb), f32),
                pltpu.VMEM(chunk, bf16),
                pltpu.VMEM(chunk, bf16),
                pltpu.VMEM(chunk, bf16),
                pltpu.VMEM(chunk, bf16),
                dma((4,)),
                dma((1,)),
                dma((1,)),
                dma((1,)),
                dma((1,)),
                dma((2, 2 * T)),
                dma((2 * T,)),
                dma((1,)),
                dma((2, 2 * T, C - 1)),
                dma((1,)),
                dma((1,)),
                dma((2 * (T - 1), G - 1)),
                dma((1,)),
                dma((2 * (T - 1), C - 1)),
                dma((1,)),
                dma((T - 2, pieces)),
                dma((1,)),
                dma((T - 2, pieces)),
                dma((1,)),
                dma((pieces,)),
                dma((1,)),
                dma((pieces, groups - 1)),
                dma((1,)),
                dma((1,)),
                dma((1,)),
                dma((1,)),
                dma((1,)),
            ],
            compiler_params=pltpu.CompilerParams(
                collective_id=0, has_side_effects=True, vmem_limit_bytes=32 * 1024 * 1024
            ),
        )(
            *(
                pltpu.with_memory_space_constraint(array, pltpu.HBM)
                for array in (
                    queries, keys, values, residual, fresh_frame, out_weight, time_weight
                )
            ),
            noise_steps,
            frame_mask,
        )
        return out[None]

    return on_device_fused


def solution(mesh):
    placed = (
        P(("groups", "tm"), "head", None),
        P(("groups", "tm"), "head", None),
        P(("groups", "tm"), "head", None),
        P(("groups", "tm"), None, "head"),
        P("groups", "head"),
        P("tm", "head"),
        P(None, "head"),
        P(("groups", "tm")),
        P(("groups", "tm"), None),
    )
    def whole(*args):
        frames, spread = mesh.shape["tm"], mesh.shape["head"]
        heads = args[0].shape[2] // HD
        fits = 2 < frames <= 4 and heads % frames == 0 and args[5].shape[1] % (spread * 2 * HD) == 0
        return jax.shard_map(
            fused(frames, spread, heads, mesh.shape["groups"]) if fits else on_device,
            mesh=mesh,
            in_specs=placed,
            out_specs=P(("groups", "tm"), None, "head"),
            check_vma=False,
        )(*args)

    return whole
```

```python
import functools
import math

import jax
import jax.numpy as jnp
from jax import lax
from jax.experimental import pallas as pl
from jax.experimental.pallas import tpu as pltpu
from jax.sharding import PartitionSpec as P

HD = 128
FREQ = 256
STEPS = 50


def shifted(value, axis, steps):
    count = lax.axis_size(axis)
    leading, last = (max(0, -steps), min(count, count - steps))
    return lax.ppermute(value, axis, [(source, source + steps) for source in range(leading, last)])


def time_features(noise_steps):
    timestep = 1000.0 * (noise_steps.astype(jnp.float32) + 1.0) / STEPS
    half = FREQ // 2
    rates = jnp.exp(-math.log(10000.0) * jnp.arange(half).astype(jnp.float32) / half)
    angles = timestep[:, None] * rates[None, :]
    return jnp.concatenate([jnp.cos(angles), jnp.sin(angles)], axis=1)


def on_device(
    queries, keys, values, residual, fresh_frame, out_weight, time_weight, noise_steps, frame_mask
):
    query_local, key_local, value_local = (
        lax.all_to_all(queries, "head", split_axis=2, concat_axis=1, tiled=True),
        lax.all_to_all(keys, "head", split_axis=2, concat_axis=1, tiled=True),
        lax.all_to_all(values, "head", split_axis=2, concat_axis=1, tiled=True),
    )
    tokens = query_local.shape[1]
    heads_here = query_local.shape[2] // HD
    scale = 1.0 / math.sqrt(HD)
    query_heads = query_local[0].reshape(tokens, heads_here, HD)
    key_value = jnp.stack([key_local[0], value_local[0]], axis=0)
    frame = lax.axis_index("tm")
    frames_total = lax.axis_size("tm")
    window = min(8, frames_total)
    mask_row = frame_mask[0]
    columns = jnp.arange(mask_row.shape[0], dtype=jnp.int32)

    def allowed_at(offset):
        hits = jnp.sum(jnp.where(columns == frame - offset, mask_row, 0))
        return hits > 0

    def absorb(state, block, allowed):
        running_max, weight_sum, accumulated = state
        key_heads = block[0].reshape(tokens, heads_here, HD)
        value_heads = block[1].reshape(tokens, heads_here, HD)
        scores = (
            jnp.einsum("qhd,khd->hqk", query_heads, key_heads, preferred_element_type=jnp.float32)
            * scale
        )
        new_max = jnp.where(allowed, jnp.maximum(running_max, jnp.max(scores, axis=2)), running_max)
        lifted = jnp.where(allowed, jnp.exp(jnp.minimum(scores - new_max[:, :, None], 0.0)), 0.0)
        factor = jnp.exp(running_max - new_max)
        weight_sum = weight_sum * factor + jnp.sum(lifted, axis=2)
        rounded = lifted.astype(jnp.bfloat16)
        accumulated = accumulated * jnp.transpose(factor)[:, :, None] + jnp.einsum(
            "hqk,khd->qhd", rounded, value_heads, preferred_element_type=jnp.float32
        )
        return (new_max, weight_sum, accumulated)

    state = (
        jnp.full((heads_here, tokens), -1e30, jnp.float32),
        jnp.zeros((heads_here, tokens), jnp.float32),
        jnp.zeros((tokens, heads_here, HD), jnp.float32),
    )
    state = absorb(state, key_value, allowed_at(0))
    moving = key_value
    for offset in range(1, window):
        moving = shifted(moving, "tm", 1)
        state = absorb(state, moving, allowed_at(offset))
    running_max, weight_sum, accumulated = state
    attention = (
        (accumulated / jnp.transpose(weight_sum)[:, :, None])
        .reshape(tokens, heads_here * HD)
        .astype(jnp.bfloat16)
    )
    weight_cols = lax.all_gather(out_weight, "tm", axis=0, tiled=True)
    projected = jnp.dot(
        lax.all_gather(attention, "head", axis=1, tiled=True),
        weight_cols,
        preferred_element_type=jnp.float32,
    )
    gate = jnp.dot(
        time_features(noise_steps), time_weight.astype(jnp.float32), precision=lax.Precision.HIGHEST
    )
    updated = (residual[0].astype(jnp.float32) + gate * projected).astype(jnp.bfloat16)
    moved = shifted(updated, "tm", -1)
    rolled = jnp.where(frame == frames_total - 1, fresh_frame, moved)
    return rolled[None]


def fused_kernel(
    T, G, C, hp, pieces, groups,
    q_ref, k_ref, v_ref, res_ref, fresh_ref, w_ref, tw_ref, steps_ref, mask_ref,
    out_ref,
    qb, kv, ab, lb, tb, so, st, mb, fb, gb, wb, w3, twb, rb, pb, down_out, down_in, up_out, up_in,
    load_sem, meta_send, meta_recv, kv_send, q_send, kv_recv, q_recv, pass_send, pass_recv,
    raise_send, ax_send, ax_recv, ac_send, ac_recv, dn_send, dn_recv, up_send, up_recv,
    w_send, tr_send, tr_recv, near_send, so_send, so_recv, st_send, st_recv,
):
    t = lax.axis_index("tm")
    h = lax.axis_index("head")
    group = lax.axis_index("groups")
    x = h // C
    c = lax.rem(h, C)
    H = G * C
    tl = q_ref.shape[1]
    cw = hp * HD
    tokens = tl * H
    half = G * tl
    nb = w_ref.shape[1] // pieces
    mask_row = FREQ // HD
    share = w_ref.shape[0] // groups
    top, low = T - 1, T - 2
    scale = 1.0 / math.sqrt(HD)

    def to(tt, hh):
        return dict(device_id={"tm": tt, "head": hh}, device_id_type=pl.DeviceIdType.MESH)

    def beside(dg):
        return dict(
            device_id={"groups": lax.rem(group + dg, groups)}, device_id_type=pl.DeviceIdType.MESH
        )

    def landed(ref, sem):
        pltpu.make_async_copy(ref, ref, sem).wait()

    def cols_of(p):
        return slice(p * nb, (p + 1) * nb)

    def reaches(one, other):
        return one == other or (other < top or one == low)

    barrier = pltpu.get_barrier_semaphore()

    def entered(level):
        awaited = C - 1 + (groups - 1 if level == low else 0)
        for other in range(T):
            awaited += (G - 1 if other == level else G) * reaches(level, other)
        return awaited

    def announce(level):
        for other in reversed(range(T)):
            for dx in range(1 if other == level else 0, G):
                if reaches(other, level):
                    pl.semaphore_signal(
                        barrier, inc=1, **to(other, lax.rem(x + dx, G) * C + c)
                    )
        for dc in range(1, C):
            pl.semaphore_signal(barrier, inc=1, **to(level, x * C + lax.rem(c + dc, C)))
        if level == low:
            for dg in range(1, groups):
                pl.semaphore_signal(barrier, inc=1, **beside(dg))

    for level in range(T):
        pl.when(t == level)(functools.partial(announce, level))

    loads = [
        pltpu.make_async_copy(tw_ref, twb, load_sem.at[0]),
        pltpu.make_async_copy(w_ref, wb, load_sem.at[1]),
        pltpu.make_async_copy(res_ref.at[0], rb, load_sem.at[2]),
    ]
    for copy in loads:
        copy.start()

    @pl.when(t == top)
    def _():
        pltpu.make_async_copy(fresh_ref, out_ref, load_sem.at[3]).start()

    def features():
        timestep = 1000.0 * (jnp.full((1, HD), steps_ref[0], jnp.int32).astype(jnp.float32) + 1.0) / STEPS
        place = lax.broadcasted_iota(jnp.int32, (1, HD), 1).astype(jnp.float32)
        angles = timestep * jnp.exp(-math.log(10000.0) * place / (FREQ // 2))
        mb[t, 0:1, :] = jnp.cos(angles)
        mb[t, 1:2, :] = jnp.sin(angles)
        for g in range(T):
            row = mask_row + g
            mb[t, row : row + 1, :] = jnp.full((1, HD), mask_ref[0, g], jnp.int32).astype(jnp.float32)

    sources = (q_ref, k_ref, v_ref)

    def slot(kind, s, f, xs):
        return qb.at[s * T + f, xs] if kind == 0 else kv.at[s * T + f, c, kind - 1, xs]

    def sems(kind, s, f):
        if kind == 0:
            return q_send.at[0], q_recv.at[s * T + f]
        return kv_send.at[0], kv_recv.at[kind - 1, s * T + f]

    def block(kind, w, xx):
        column = pl.multiple_of((w * G + xx) * cw, HD)
        return sources[kind].at[0, :, pl.ds(column, cw)]

    def aim(f, key):
        w = min(key, top)
        if key < top:
            return w, 0, w
        return w, 1, (low if key == top and f < top else top)

    def outgoing(kind, f, key, dx):
        w, s, level = aim(f, key)
        xx = lax.rem(x + dx, G)
        leaves, lands = sems(kind, s, f)
        return pltpu.make_async_remote_copy(
            src_ref=block(kind, w, xx), dst_ref=slot(kind, s, f, x),
            send_sem=leaves, recv_sem=lands, **to(level, xx * C + c),
        )

    def own(kind, f, key):
        w, s, _ = aim(f, key)
        return pltpu.make_async_copy(block(kind, w, x), slot(kind, s, f, x), sems(kind, s, f)[1])

    def passed(i, kind, dc, late):
        return pltpu.make_async_remote_copy(
            src_ref=kv.at[i, c, kind - 1], dst_ref=kv.at[i, c, kind - 1],
            send_sem=pass_send.at[0], recv_sem=pass_recv.at[kind - 1, late, dc - 1],
            **to(t, x * C + lax.rem(c + dc, C)),
        )

    def raised(i, kind):
        return pltpu.make_async_remote_copy(
            src_ref=kv.at[i, c, kind - 1], dst_ref=kv.at[i, c, kind - 1],
            send_sem=raise_send.at[0], recv_sem=kv_recv.at[kind - 1, i], **to(top, h),
        )

    def near(kind, w, dx):
        xx = lax.rem(x + dx, G)
        leaves, lands = sems(kind, 0, w)
        if dx == 0:
            return pltpu.make_async_copy(block(kind, w, x), slot(kind, 0, w, x), lands)
        return pltpu.make_async_remote_copy(
            src_ref=block(kind, w, xx), dst_ref=slot(kind, 0, w, x),
            send_sem=near_send.at[0] if kind == 0 else leaves, recv_sem=lands,
            **to(top, xx * C + c),
        )

    def sidestep(k, key, dx):
        return pltpu.make_async_remote_copy(
            src_ref=block(0, key, lax.rem(x + dx, G)), dst_ref=qb.at[T + k, x],
            send_sem=near_send.at[0], recv_sem=q_recv.at[T + k],
            **to(t, lax.rem(x + dx, G) * C + c),
        )

    def forward(k, key, f, xs):
        return pltpu.make_async_remote_copy(
            src_ref=qb.at[T + k, xs], dst_ref=slot(0, k, f, xs),
            send_sem=q_send.at[0], recv_sem=q_recv.at[k * T + f], **to(low, h),
        )

    def handed(w):
        return [
            pltpu.make_async_remote_copy(
                src_ref=buffer.at[w], dst_ref=buffer.at[top],
                send_sem=leaves.at[0], recv_sem=lands.at[0], **to(w, h),
            )
            for buffer, leaves, lands in ((so, so_send, so_recv), (st, st_send, st_recv))
        ]

    own_rows = pl.ds(pl.multiple_of(group * share, 8), share)

    def lift(p):
        return pltpu.make_async_remote_copy(
            src_ref=w_ref.at[own_rows, cols_of(p)], dst_ref=w3.at[own_rows, cols_of(p)],
            send_sem=w_send.at[0], recv_sem=dn_recv.at[1, p], **to(low, h),
        )

    def trade(p, dg):
        return pltpu.make_async_remote_copy(
            src_ref=w3.at[own_rows, cols_of(p)], dst_ref=w3.at[own_rows, cols_of(p)],
            send_sem=tr_send.at[0], recv_sem=tr_recv.at[p, dg - 1], **beside(dg),
        )

    def mine(i, column, size):
        return ab.at[i, c, :, pl.ds(pl.multiple_of(column, HD), size)]

    def across(i, dx):
        here = mine(i, x * cw, cw)
        return pltpu.make_async_remote_copy(
            src_ref=here, dst_ref=here, send_sem=ax_send.at[0], recv_sem=ax_recv.at[i, dx - 1],
            **to(t, lax.rem(x + dx, G) * C + c),
        )

    def aside(i, xs, dc):
        here = mine(i, xs * cw, cw)
        return pltpu.make_async_remote_copy(
            src_ref=here, dst_ref=here, send_sem=ac_send.at[0], recv_sem=ac_recv.at[i, dc - 1],
            **to(t, x * C + lax.rem(c + dc, C)),
        )

    def spot(r):
        return r % (T - 2)

    def down(level, r, p):
        return pltpu.make_async_remote_copy(
            src_ref=down_out.at[spot(r), p], dst_ref=down_in.at[spot(r), p],
            send_sem=dn_send.at[0], recv_sem=dn_recv.at[spot(r), p], **to(level - 1, h),
        )

    def up(level, r, p):
        return pltpu.make_async_remote_copy(
            src_ref=up_out.at[spot(r), p], dst_ref=up_in.at[spot(r), p],
            send_sem=up_send.at[0], recv_sem=up_recv.at[spot(r), p], **to(level + 1, h),
        )

    def gates(level):
        with jax.named_scope("loads"):
            for copy in loads:
                copy.wait()
        with jax.named_scope("meta"):
            fb[...] = jnp.zeros_like(fb)
            away = [f for f in range(1, T) if level != f and level < top]
            if away:
                landed(mb.at[: len(away)], meta_recv.at[0])
            for f in range(1, T) if level < top else (top,):
                for b in range(mask_row):
                    fb[f : f + 1, b * HD : (b + 1) * HD] = mb[f, b : b + 1, :]
        with jax.named_scope("gate"):
            gb[...] = jnp.dot(
                fb[...], twb[...].astype(jnp.float32),
                precision=lax.Precision.HIGHEST, preferred_element_type=jnp.float32,
            )

    def program(level):
        if level < top:
            features()
        with jax.named_scope("barrier"):
            pl.semaphore_wait(barrier, entered(level))
        if level == top:
            lifts = [lift(p) for p in range(pieces)]
            lifts[0].start()
            features()
        told = [other for other in range(top) if other != level and level > 0]
        for other in told:
            pltpu.make_async_remote_copy(
                src_ref=mb.at[t], dst_ref=mb.at[t], send_sem=meta_send.at[0],
                recv_sem=meta_recv.at[0], **to(other, h),
            ).start()
        count = dict(kv=0, q=0, passed=0, raised=0, near=0, ax=0, ac=0, down=0, up=0, traded=0)

        def send(kinds, key, dxs=tuple(reversed(range(G)))):
            for dx in dxs:
                for kind in kinds:
                    if kind == 0 and level == 0:
                        continue
                    if dx == 0 and aim(level, key)[2] == level:
                        own(kind, level, key).start()
                    else:
                        outgoing(kind, level, key, dx).start()
                        count["q" if kind == 0 else "kv"] += 1

        def group_of(s, f):
            if level == top:
                return T if s else f
            if level == low:
                return 2 * s + (f == top)
            return int(0 < level < f)

        def take(s, f, kinds=(1, 2)):
            i = s * T + f
            for kind in kinds:
                landed(kv.at[i, c, kind - 1], kv_recv.at[kind - 1, i])
                for dc in range(1, C):
                    passed(i, kind, dc, group_of(s, f)).start()
                    count["passed"] += 1
                if s == 1 and level == low and f < low:
                    raised(i, kind).start()
                    count["raised"] += 1

        def take_queries(s, f):
            landed(qb.at[s * T + f], q_recv.at[s * T + f])

        def settle(s, frames, kinds=(1, 2)):
            i = s * T + frames[0]
            for kind in kinds:
                for dc in range(1, C):
                    landed(
                        kv.at[i : i + len(frames), lax.rem(c + C - dc, C), kind - 1],
                        pass_recv.at[kind - 1, group_of(s, frames[0]), dc - 1],
                    )

        def weigh(s, r, j):
            f = r + 1
            keys_here = (f + 1) * tokens
            allowed = jnp.concatenate(
                [
                    jnp.broadcast_to(mb[f, mask_row + g : mask_row + g + 1, 0:1], (1, tokens))
                    for g in range(f + 1)
                ],
                axis=1,
            )
            cols = slice(j * HD, (j + 1) * HD)
            query = qb[s * T + f, :, :, cols].reshape(half, HD)
            key = kv[s * T : s * T + f + 1, :, 0, :, :, cols].reshape(keys_here, HD)
            scores = (
                lax.dot_general(
                    query, key, (((1,), (1,)), ((), ())), preferred_element_type=jnp.float32
                )
                * scale
            )
            scores = jnp.where(allowed > 0.5, scores, -1e30)
            peak = jnp.max(scores, axis=1, keepdims=True)
            lifted = jnp.exp(scores - peak)
            return lifted.astype(jnp.bfloat16), jnp.sum(lifted, axis=1, keepdims=True)

        def mix(s, r, j, rounded, total):
            f = r + 1
            cols = slice(j * HD, (j + 1) * HD)
            value = kv[s * T : s * T + f + 1, :, 1, :, :, cols].reshape((f + 1) * tokens, HD)
            mixed = jnp.dot(rounded, value, preferred_element_type=jnp.float32)
            here = pl.ds(pl.multiple_of(x * cw + j * HD, HD), HD)
            ab[s * (T - 1) + r, c, :, here] = (mixed / total).astype(jnp.bfloat16)

        def attend_own(w):
            lane = lax.broadcasted_iota(jnp.int32, (half, HD), 1)
            stats = jnp.zeros((half, HD), jnp.float32)
            for j in range(hp):
                cols = slice(j * HD, (j + 1) * HD)
                query = qb[w, :, :, cols].reshape(half, HD)
                key = kv[w, :, 0, :, :, cols].reshape(tokens, HD)
                value = kv[w, :, 1, :, :, cols].reshape(tokens, HD)
                scores = (
                    lax.dot_general(
                        query, key, (((1,), (1,)), ((), ())), preferred_element_type=jnp.float32
                    )
                    * scale
                )
                peak = jnp.max(scores, axis=1, keepdims=True)
                lifted = jnp.exp(scores - peak)
                total = jnp.sum(lifted, axis=1, keepdims=True)
                mixed = jnp.dot(
                    lifted.astype(jnp.bfloat16), value, preferred_element_type=jnp.float32
                )
                so[w, :, cols] = (mixed / total).astype(jnp.bfloat16)
                stats = jnp.where(lane == 2 * j, peak, stats)
                stats = jnp.where(lane == 2 * j + 1, total, stats)
            st[w] = jnp.transpose(stats)[:8]
            for copy in handed(w):
                copy.start()

        def attend_last():
            landed(so.at[top], so_recv.at[0])
            landed(st.at[top], st_recv.at[0])
            stats = jnp.transpose(
                jnp.concatenate([st[top], jnp.zeros((HD - 8, half), jnp.float32)], axis=0)
            )
            allowed = jnp.concatenate(
                [
                    jnp.broadcast_to(mb[top, mask_row + g : mask_row + g + 1, 0:1], (1, tokens))
                    for g in range(top)
                ],
                axis=1,
            )
            for j in range(hp):
                cols = slice(j * HD, (j + 1) * HD)
                query = qb[top, :, :, cols].reshape(half, HD)
                key = kv[0:top, :, 0, :, :, cols].reshape(top * tokens, HD)
                value = kv[0:top, :, 1, :, :, cols].reshape(top * tokens, HD)
                scores = (
                    lax.dot_general(
                        query, key, (((1,), (1,)), ((), ())), preferred_element_type=jnp.float32
                    )
                    * scale
                )
                scores = jnp.where(allowed > 0.5, scores, -1e30)
                their_peak = stats[:, 2 * j : 2 * j + 1]
                peak = jnp.maximum(jnp.max(scores, axis=1, keepdims=True), their_peak)
                lifted = jnp.exp(scores - peak)
                theirs = jnp.exp(their_peak - peak) * stats[:, 2 * j + 1 : 2 * j + 2]
                total = jnp.sum(lifted, axis=1, keepdims=True) + theirs
                mixed = jnp.dot(
                    lifted.astype(jnp.bfloat16), value, preferred_element_type=jnp.float32
                )
                mixed += theirs * so[top, :, cols].astype(jnp.float32)
                here = pl.ds(pl.multiple_of(x * cw + j * HD, HD), HD)
                ab[low, c, :, here] = (mixed / total).astype(jnp.bfloat16)
            share_out(0, low)

        def share_out(s, r):
            i = s * (T - 1) + r
            for dx in range(1, G):
                across(i, dx).start()
                count["ax"] += 1
            for dc in range(1, C):
                aside(i, x, dc).start()
                count["ac"] += 1

        def attend(s, r):
            for j in range(hp):
                mix(s, r, j, *weigh(s, r, j))
            share_out(s, r)

        def attend_keys(s, r):
            for j in range(hp):
                rounded, total = weigh(s, r, j)
                lb[s, j] = rounded
                tb[s, j] = jnp.broadcast_to(total, (half, HD))

        def attend_values(s, r):
            for j in range(hp):
                mix(s, r, j, lb[s, j], tb[s, j])
            share_out(s, r)

        def hand_over(s, r):
            i = s * (T - 1) + r
            for dx in range(1, G):
                xs = lax.rem(x + G - dx, G)
                landed(mine(i, xs * cw, cw), ax_recv.at[i, dx - 1])
                for dc in range(1, C):
                    aside(i, xs, dc).start()
                    count["ac"] += 1

        def gathered(s, r):
            i = s * (T - 1) + r
            for dc in range(1, C):
                landed(ab.at[i, lax.rem(c + C - dc, C)], ac_recv.at[i, dc - 1])

        def product(r, p):
            if level == top:
                parts = ((1, wb),)
            elif level == low and r < low:
                parts = ((0, wb), (1, w3))
            else:
                parts = ((0, wb),)
            partial = 0.0
            for s, weight in parts:
                partial += jnp.dot(
                    ab[s * (T - 1) + r].reshape(tokens, G * cw), weight[:, cols_of(p)],
                    preferred_element_type=jnp.float32,
                )
            partial = partial * gb[r + 1 : r + 2, cols_of(p)]
            if level == r + 1:
                moved = [
                    rb[(xs * C + cs) * tl : (xs * C + cs + 1) * tl, cols_of(p)]
                    for cs in range(C)
                    for xs in range(G)
                ]
                partial += jnp.concatenate(moved, axis=0).astype(jnp.float32)
            return partial

        def part(r, p, dc, going_up):
            cc = lax.rem(c + dc, C)
            parts = ((0, wb), (1, w3)) if level == low and r < low else ((0, wb),)
            partial = 0.0
            for s, weight in parts:
                partial += jnp.dot(
                    ab[s * (T - 1) + r, cc], weight[:, cols_of(p)],
                    preferred_element_type=jnp.float32,
                )
            partial = partial * gb[r + 1 : r + 2, cols_of(p)]
            if level == r + 1:
                moved = [
                    rb[pl.ds(pl.multiple_of((xs * C + cc) * tl, tl), tl), cols_of(p)]
                    for xs in range(G)
                ]
                partial += jnp.concatenate(moved, axis=0).astype(jnp.float32)
            rows = pl.ds(pl.multiple_of(cc * half, half), half)
            out, into = (up_out, up_in) if going_up else (down_out, down_in)
            leaves, lands = (up_send, up_recv) if going_up else (dn_send, dn_recv)
            out[spot(r), p, rows, :] = partial.astype(jnp.bfloat16)
            pltpu.make_async_remote_copy(
                src_ref=out.at[spot(r), p, rows], dst_ref=into.at[spot(r), p, rows],
                send_sem=leaves.at[0], recv_sem=lands.at[spot(r), p],
                **to(level + 1 if going_up else level - 1, h),
            ).start()

        def own_parts(r, going_up=False):
            for p in range(2):
                with scope(f"own{r}{p}"):
                    part(r, p, 0, going_up)
                count["up" if going_up else "down"] += 1

        def other_parts(r, going_up=False):
            for p in range(2):
                for dc in range(1, C):
                    with scope(f"other{r}{p}"):
                        part(r, p, dc, going_up)

        def send_down(r, p, value):
            down_out[spot(r), p] = value.astype(jnp.bfloat16)
            down(level, r, p).start()
            count["down"] += 1

        def send_up(r, p, value):
            up_out[spot(r), p] = value.astype(jnp.bfloat16)
            up(level, r, p).start()
            count["up"] += 1

        def from_down(r, p):
            landed(down_in.at[spot(r), p], dn_recv.at[spot(r), p])
            return down_in[spot(r), p].astype(jnp.float32)

        def from_up(r, p):
            landed(up_in.at[spot(r), p], up_recv.at[spot(r), p])
            return up_in[spot(r), p].astype(jnp.float32)

        def finish(p):
            r = level
            total = pb[r, p] + from_down(r, p)
            if r > 0:
                total += from_up(r, p)
            total = total.astype(out_ref.dtype)
            for cs in range(C):
                for xs in range(G):
                    row, token = (cs * G + xs) * tl, (xs * C + cs) * tl
                    out_ref[token : token + tl, cols_of(p)] = total[row : row + tl]

        scope = jax.named_scope
        early = (3 * pieces) // 5
        order = [(low - 1, p) for p in range(2)]
        order += [(r, p) for r in range(low - 1) for p in range(pieces)]
        order += [(low - 1, p) for p in range(2, pieces)]

        if level == top:
            for p in range(1, early):
                lifts[p].start()
            lower = tuple(reversed(range(low)))
            for w in lower:
                for dx in reversed(range(G)):
                    for kind in (1, 0, 2):
                        near(kind, w, dx).start()
                        if dx > 0:
                            count["near" if kind == 0 else "kv"] += 1
            for w in lower:
                send((0,), w)
            send((0, 1, 2), top)
            for w in lower:
                with scope(f"near{w}"):
                    take(0, w)
                    take_queries(0, w)
            for w in lower:
                with scope(f"own{w}"):
                    settle(0, (w,))
                    attend_own(w)
            for p in range(early, pieces):
                lifts[p].start()
            send((1, 2, 0), low)
            gates(level)
            for f in range(T):
                with scope(f"take{f}"):
                    take(1, f)
            with scope("settle"):
                take_queries(1, top)
                settle(1, range(T))
            with scope("attend"):
                attend(1, low)
            with scope("gather"):
                hand_over(1, low)
                gathered(1, low)
            with scope("project"):
                for p in range(pieces):
                    send_down(low, p, product(low, p))
            pltpu.make_async_copy(fresh_ref, out_ref, load_sem.at[3]).wait()
            landed(w3.at[own_rows], w_send.at[0])
        elif level == low:
            for w in range(low):
                send((1, 2, 0), w)
            send((1, 2, 0), low)
            send((1, 2, 0), top)
            send((1, 2), T)

            def exchange(p):
                with scope(f"trade{p}"):
                    landed(w3.at[own_rows, cols_of(p)], dn_recv.at[1, p])
                for dg in range(1, groups):
                    trade(p, dg).start()

            def exchanged(p):
                for dg in range(1, groups):
                    theirs = pl.ds(
                        pl.multiple_of(lax.rem(group + groups - dg, groups) * share, 8), share
                    )
                    landed(w3.at[theirs, cols_of(p)], tr_recv.at[p, dg - 1])

            gates(level)
            for p in range(early - 1):
                exchange(p)
            with scope("take_early"):
                for f in (*range(low - 1), low):
                    for s in (0, 1):
                        take(s, f)
                for s in (0, 1):
                    take_queries(s, low)
            with scope("keys"):
                for s in (0, 1):
                    take(s, low - 1, (1,))
            exchange(early - 1)
            for s in (0, 1):
                with scope(f"settle{s}1"):
                    settle(s, range(low + 1), (1,))
                with scope(f"attend{s}{low - 1}1"):
                    attend_keys(s, low - 1)
            for s in (0, 1):
                with scope(f"values{s}"):
                    take(s, low - 1, (2,))
                with scope(f"settle{s}2"):
                    settle(s, range(low + 1), (2,))
                with scope(f"attend{s}{low - 1}2"):
                    attend_values(s, low - 1)
            for r in reversed(range(low - 1)):
                for s in (0, 1):
                    with scope(f"hand{s}{r + 1}"):
                        hand_over(s, r + 1)
                    if s == 1:
                        for p in range(2):
                            exchanged(p)
                        own_parts(r + 1)
                    with scope(f"q{r + 1}{s}"):
                        take_queries(s, r + 1)
                    with scope(f"attend{s}{r}"):
                        attend(s, r)
            ready = set()
            known = {0, 1} if low > 1 else set()
            swapped = False

            def last_frame():
                with scope("take3"):
                    take(0, top)
                    take_queries(0, top)
                    settle(0, (top,))
                with scope("attend3"):
                    attend(0, low)

            for r, p in order:
                if p >= early and not swapped:
                    swapped = True
                    for q in range(early + 1, pieces):
                        exchange(q)
                if r not in ready:
                    ready.add(r)
                    if r == 0:
                        exchange(early)
                    if r == 0:
                        for s in (0, 1):
                            with scope(f"hand{s}{r}"):
                                hand_over(s, r)
                        for q in range(2):
                            if q not in known:
                                known.add(q)
                                exchanged(q)
                        own_parts(r)
                    with scope(f"gather{r}"):
                        for s in (0, 1):
                            gathered(s, r)
                    other_parts(r)
                if p < 2:
                    continue
                if p not in known:
                    known.add(p)
                    with scope(f"w{p}"):
                        exchanged(p)
                with scope(f"project{r}{p}"):
                    send_down(r, p, product(r, p))
            last_frame()
            with scope("gather3"):
                hand_over(0, low)
                gathered(0, low)
            with scope("project3"):
                for p in range(pieces):
                    pb[low, p] = product(low, p)
            for p in range(pieces):
                with scope(f"finish{p}"):
                    finish(p)
            landed(w3.at[own_rows], tr_send.at[0])
        else:
            if level > 0:
                for k, w in enumerate((low, top)):
                    for dx in range(1, G):
                        sidestep(k, w, dx).start()
                        count["near"] += 1
            for kind in (1, 2):
                for w in (low, top):
                    send((kind,), w)
            for w in (low, top):
                send((0,), w, (0,))
            for w in range(level + 1, low):
                send((1, 2, 0), w)
            for w in range(level):
                send((1, 2, 0), w)
            send((1, 2, 0), level)
            gates(level)
            if level > 0:
                for k, w in enumerate((low, top)):
                    for dx in range(1, G):
                        xs = lax.rem(x + dx, G)
                        landed(qb.at[T + k, xs], q_recv.at[T + k])
                        forward(k, w, level, xs).start()
                        count["q"] += 1
            stages = (
                (range(T - 1), range(T - 3, -1, -1)),
                (range(T - 1, T), range(T - 2, T - 1)),
            )
            if level > 0:
                stages = (
                    (range(level + 1), range(level)),
                    (range(level + 1, T), range(level, T - 1)),
                )
            for frames, rounds in stages:
                for f in frames:
                    with scope(f"take{f}"):
                        if f < top:
                            take(0, f)
                        if f > 0:
                            take_queries(0, f)
                if frames[0] < top:
                    settle(0, range(frames[0], min(frames[-1] + 1, top)))
                for r in rounds:
                    with scope(f"attend{r}"):
                        if r < low:
                            attend(0, r)
                        else:
                            attend_last()
                for r in rounds:
                    early_up = level == 0 and 0 < r < low
                    with scope(f"gather{r}"):
                        hand_over(0, r)
                    if early_up:
                        own_parts(r, True)
                    with scope(f"pair{r}"):
                        gathered(0, r)
                    if early_up:
                        other_parts(r, True)
                    with scope(f"project{r}"):
                        for p in range(2 if early_up else 0, pieces - early_up):
                            value = product(r, p)
                            if level == 0 and r > 0:
                                send_up(r, p, value)
                            else:
                                pb[r, p] = value
            if level == 0:
                for r in range(1, low):
                    send_up(r, pieces - 1, product(r, pieces - 1))
            ups = [
                (q, p) for p in range(pieces) for q in reversed(range(level + 1, T - 1)) if level
            ]
            for n, (r, p) in enumerate(pair for pair in order if pair[0] <= level):
                if r == level:
                    with scope(f"finish{p}"):
                        finish(p)
                else:
                    with scope(f"down{r}{p}"):
                        send_down(r, p, pb[r, p] + from_down(r, p))
                if n >= 2 and ups:
                    q, p = ups.pop(0)
                    with scope(f"up{q}{p}"):
                        send_up(q, p, pb[q, p] + from_up(q, p))
            for q, p in ups:
                send_up(q, p, pb[q, p] + from_up(q, p))
        with scope("sends"):
            if told:
                landed(mb.at[: len(told)], meta_send.at[0])
            landed(kv.at[: count["kv"] // 2, 0, :, 0], kv_send.at[0])
            if count["q"]:
                landed(qb.at[: count["q"], 0], q_send.at[0])
            if count["near"]:
                landed(qb.at[: count["near"], 0], near_send.at[0])
            if level == top:
                landed(so.at[:low], so_send.at[0])
                landed(st.at[:low], st_send.at[0])
            if count["passed"]:
                landed(kv.at[: count["passed"] // 2, 0], pass_send.at[0])
            if count["raised"]:
                landed(kv.at[: count["raised"] // 2, 0], raise_send.at[0])
            if count["ax"]:
                landed(ab.at[: count["ax"], 0, :, :cw], ax_send.at[0])
            if count["ac"]:
                landed(ab.at[: count["ac"] // G, 0], ac_send.at[0])
            if count["down"]:
                landed(down_out.at[: count["down"] // pieces], dn_send.at[0])
            if count["up"]:
                landed(up_out.at[: count["up"] // pieces], up_send.at[0])

    for level in range(T):
        pl.when(t == level)(functools.partial(program, level))


def fused(T, H, heads, groups):
    def on_device_fused(
        queries, keys, values, residual, fresh_frame, out_weight, time_weight, noise_steps, frame_mask
    ):
        level_heads = heads // T
        G = math.gcd(level_heads, H)
        C = H // G
        hp = level_heads // G
        tl = queries.shape[1]
        tokens = tl * H
        width = out_weight.shape[1]
        pieces = width // (2 * HD)
        nb = width // pieces
        meta_rows = -(-(FREQ // HD + T) // 8) * 8
        cw = hp * HD
        bf16, f32 = jnp.bfloat16, jnp.float32
        dma = pltpu.SemaphoreType.DMA
        chunk = (T - 2, pieces, tokens, nb)
        out = pl.pallas_call(
            functools.partial(fused_kernel, T, G, C, hp, pieces, groups),
            out_shape=jax.ShapeDtypeStruct((tokens, width), bf16),
            in_specs=[pl.BlockSpec(memory_space=pltpu.HBM)] * 7
            + [pl.BlockSpec(memory_space=pltpu.SMEM)] * 2,
            out_specs=pl.BlockSpec(memory_space=pltpu.VMEM),
            scratch_shapes=[
                pltpu.VMEM((2 * T, G, tl, cw), bf16),
                pltpu.VMEM((2 * T, C, 2, G, tl, cw), bf16),
                pltpu.VMEM((2 * (T - 1), C, G * tl, G * cw), bf16),
                pltpu.VMEM((2, hp, G * tl, (T - 1) * tokens), bf16),
                pltpu.VMEM((2, hp, G * tl, HD), f32),
                pltpu.VMEM((T, G * tl, cw), bf16),
                pltpu.VMEM((T, 8, G * tl), f32),
                pltpu.VMEM((T, meta_rows, HD), f32),
                pltpu.VMEM((8, FREQ), f32),
                pltpu.VMEM((8, width), f32),
                pltpu.VMEM(out_weight.shape, bf16),
                pltpu.VMEM(out_weight.shape, bf16),
                pltpu.VMEM(time_weight.shape, bf16),
                pltpu.VMEM((tokens, width), bf16),
                pltpu.VMEM((T - 1, pieces, tokens, nb), f32),
                pltpu.VMEM(chunk, bf16),
                pltpu.VMEM(chunk, bf16),
                pltpu.VMEM(chunk, bf16),
                pltpu.VMEM(chunk, bf16),
                dma((4,)),
                dma((1,)),
                dma((1,)),
                dma((1,)),
                dma((1,)),
                dma((2, 2 * T)),
                dma((2 * T,)),
                dma((1,)),
                dma((2, T + 1, C - 1)),
                dma((1,)),
                dma((1,)),
                dma((2 * (T - 1), G - 1)),
                dma((1,)),
                dma((2 * (T - 1), C - 1)),
                dma((1,)),
                dma((2, pieces)),
                dma((1,)),
                dma((2, pieces)),
                dma((1,)),
                dma((1,)),
                dma((pieces, groups - 1)),
                dma((1,)),
                dma((1,)),
                dma((1,)),
                dma((1,)),
                dma((1,)),
            ],
            compiler_params=pltpu.CompilerParams(
                collective_id=0, has_side_effects=True, vmem_limit_bytes=32 * 1024 * 1024
            ),
        )(
            *(
                pltpu.with_memory_space_constraint(array, pltpu.HBM)
                for array in (
                    queries, keys, values, residual, fresh_frame, out_weight, time_weight
                )
            ),
            noise_steps,
            frame_mask,
        )
        return out[None]

    return on_device_fused


def solution(mesh):
    placed = (
        P(("groups", "tm"), "head", None),
        P(("groups", "tm"), "head", None),
        P(("groups", "tm"), "head", None),
        P(("groups", "tm"), None, "head"),
        P("groups", "head"),
        P("tm", "head"),
        P(None, "head"),
        P(("groups", "tm")),
        P(("groups", "tm"), None),
    )
    def whole(*args):
        frames, spread = mesh.shape["tm"], mesh.shape["head"]
        heads = args[0].shape[2] // HD
        fits = 2 < frames <= 4 and heads % frames == 0 and args[5].shape[1] % (spread * 2 * HD) == 0
        return jax.shard_map(
            fused(frames, spread, heads, mesh.shape["groups"]) if fits else on_device,
            mesh=mesh,
            in_specs=placed,
            out_specs=P(("groups", "tm"), None, "head"),
            check_vma=False,
        )(*args)

    return whole
```

```python
import functools
import math

import jax
import jax.numpy as jnp
from jax import lax
from jax.experimental import pallas as pl
from jax.experimental.pallas import tpu as pltpu
from jax.sharding import PartitionSpec as P

HD = 128
FREQ = 256
STEPS = 50


def shifted(value, axis, steps):
    count = lax.axis_size(axis)
    leading, last = (max(0, -steps), min(count, count - steps))
    return lax.ppermute(value, axis, [(source, source + steps) for source in range(leading, last)])


def time_features(noise_steps):
    timestep = 1000.0 * (noise_steps.astype(jnp.float32) + 1.0) / STEPS
    half = FREQ // 2
    rates = jnp.exp(-math.log(10000.0) * jnp.arange(half).astype(jnp.float32) / half)
    angles = timestep[:, None] * rates[None, :]
    return jnp.concatenate([jnp.cos(angles), jnp.sin(angles)], axis=1)


def on_device(
    queries, keys, values, residual, fresh_frame, out_weight, time_weight, noise_steps, frame_mask
):
    query_local, key_local, value_local = (
        lax.all_to_all(queries, "head", split_axis=2, concat_axis=1, tiled=True),
        lax.all_to_all(keys, "head", split_axis=2, concat_axis=1, tiled=True),
        lax.all_to_all(values, "head", split_axis=2, concat_axis=1, tiled=True),
    )
    tokens = query_local.shape[1]
    heads_here = query_local.shape[2] // HD
    scale = 1.0 / math.sqrt(HD)
    query_heads = query_local[0].reshape(tokens, heads_here, HD)
    key_value = jnp.stack([key_local[0], value_local[0]], axis=0)
    frame = lax.axis_index("tm")
    frames_total = lax.axis_size("tm")
    window = min(8, frames_total)
    mask_row = frame_mask[0]
    columns = jnp.arange(mask_row.shape[0], dtype=jnp.int32)

    def allowed_at(offset):
        hits = jnp.sum(jnp.where(columns == frame - offset, mask_row, 0))
        return hits > 0

    def absorb(state, block, allowed):
        running_max, weight_sum, accumulated = state
        key_heads = block[0].reshape(tokens, heads_here, HD)
        value_heads = block[1].reshape(tokens, heads_here, HD)
        scores = (
            jnp.einsum("qhd,khd->hqk", query_heads, key_heads, preferred_element_type=jnp.float32)
            * scale
        )
        new_max = jnp.where(allowed, jnp.maximum(running_max, jnp.max(scores, axis=2)), running_max)
        lifted = jnp.where(allowed, jnp.exp(jnp.minimum(scores - new_max[:, :, None], 0.0)), 0.0)
        factor = jnp.exp(running_max - new_max)
        weight_sum = weight_sum * factor + jnp.sum(lifted, axis=2)
        rounded = lifted.astype(jnp.bfloat16)
        accumulated = accumulated * jnp.transpose(factor)[:, :, None] + jnp.einsum(
            "hqk,khd->qhd", rounded, value_heads, preferred_element_type=jnp.float32
        )
        return (new_max, weight_sum, accumulated)

    state = (
        jnp.full((heads_here, tokens), -1e30, jnp.float32),
        jnp.zeros((heads_here, tokens), jnp.float32),
        jnp.zeros((tokens, heads_here, HD), jnp.float32),
    )
    state = absorb(state, key_value, allowed_at(0))
    moving = key_value
    for offset in range(1, window):
        moving = shifted(moving, "tm", 1)
        state = absorb(state, moving, allowed_at(offset))
    running_max, weight_sum, accumulated = state
    attention = (
        (accumulated / jnp.transpose(weight_sum)[:, :, None])
        .reshape(tokens, heads_here * HD)
        .astype(jnp.bfloat16)
    )
    weight_cols = lax.all_gather(out_weight, "tm", axis=0, tiled=True)
    projected = jnp.dot(
        lax.all_gather(attention, "head", axis=1, tiled=True),
        weight_cols,
        preferred_element_type=jnp.float32,
    )
    gate = jnp.dot(
        time_features(noise_steps), time_weight.astype(jnp.float32), precision=lax.Precision.HIGHEST
    )
    updated = (residual[0].astype(jnp.float32) + gate * projected).astype(jnp.bfloat16)
    moved = shifted(updated, "tm", -1)
    rolled = jnp.where(frame == frames_total - 1, fresh_frame, moved)
    return rolled[None]


def fused_kernel(
    T, G, C, hp, pieces, groups,
    q_ref, k_ref, v_ref, res_ref, fresh_ref, w_ref, tw_ref, steps_ref, mask_ref,
    out_ref,
    qb, kv, ab, lb, tb, so, st, mb, fb, gb, wb, w3, twb, rb, pb, down_out, down_in, up_out, up_in,
    load_sem, meta_send, meta_recv, kv_send, q_send, kv_recv, q_recv, pass_send, pass_recv,
    raise_send, ax_send, ax_recv, ac_send, ac_recv, dn_send, dn_recv, up_send, up_recv,
    w_send, tr_send, tr_recv, near_send, so_send, so_recv, st_send, st_recv, vh_recv, vp_recv,
):
    t = lax.axis_index("tm")
    h = lax.axis_index("head")
    group = lax.axis_index("groups")
    x = h // C
    c = lax.rem(h, C)
    H = G * C
    tl = q_ref.shape[1]
    cw = hp * HD
    tokens = tl * H
    half = G * tl
    nb = w_ref.shape[1] // pieces
    mask_row = FREQ // HD
    share = w_ref.shape[0] // groups
    top, low = T - 1, T - 2
    scale = 1.0 / math.sqrt(HD)

    def to(tt, hh):
        return dict(device_id={"tm": tt, "head": hh}, device_id_type=pl.DeviceIdType.MESH)

    def beside(dg):
        return dict(
            device_id={"groups": lax.rem(group + dg, groups)}, device_id_type=pl.DeviceIdType.MESH
        )

    def landed(ref, sem):
        pltpu.make_async_copy(ref, ref, sem).wait()

    def cols_of(p):
        return slice(p * nb, (p + 1) * nb)

    def reaches(one, other):
        return one == other or (other < top or one == low)

    barrier = pltpu.get_barrier_semaphore()

    def entered(level):
        awaited = C - 1 + (groups - 1 if level == low else 0)
        for other in range(T):
            awaited += (G - 1 if other == level else G) * reaches(level, other)
        return awaited

    def announce(level):
        for other in reversed(range(T)):
            for dx in range(1 if other == level else 0, G):
                if reaches(other, level):
                    pl.semaphore_signal(
                        barrier, inc=1, **to(other, lax.rem(x + dx, G) * C + c)
                    )
        for dc in range(1, C):
            pl.semaphore_signal(barrier, inc=1, **to(level, x * C + lax.rem(c + dc, C)))
        if level == low:
            for dg in range(1, groups):
                pl.semaphore_signal(barrier, inc=1, **beside(dg))

    for level in range(T):
        pl.when(t == level)(functools.partial(announce, level))

    loads = [
        pltpu.make_async_copy(tw_ref, twb, load_sem.at[0]),
        pltpu.make_async_copy(w_ref, wb, load_sem.at[1]),
        pltpu.make_async_copy(res_ref.at[0], rb, load_sem.at[2]),
    ]
    for copy in loads:
        copy.start()

    @pl.when(t == top)
    def _():
        pltpu.make_async_copy(fresh_ref, out_ref, load_sem.at[3]).start()

    def features():
        timestep = 1000.0 * (jnp.full((1, HD), steps_ref[0], jnp.int32).astype(jnp.float32) + 1.0) / STEPS
        place = lax.broadcasted_iota(jnp.int32, (1, HD), 1).astype(jnp.float32)
        angles = timestep * jnp.exp(-math.log(10000.0) * place / (FREQ // 2))
        mb[t, 0:1, :] = jnp.cos(angles)
        mb[t, 1:2, :] = jnp.sin(angles)
        for g in range(T):
            row = mask_row + g
            mb[t, row : row + 1, :] = jnp.full((1, HD), mask_ref[0, g], jnp.int32).astype(jnp.float32)

    sources = (q_ref, k_ref, v_ref)

    def slot(kind, s, f, xs):
        return qb.at[s * T + f, xs] if kind == 0 else kv.at[s * T + f, c, kind - 1, xs]

    def sems(kind, s, f):
        if kind == 0:
            return q_send.at[0], q_recv.at[s * T + f]
        return kv_send.at[0], kv_recv.at[kind - 1, s * T + f]

    def block(kind, w, xx):
        column = pl.multiple_of((w * G + xx) * cw, HD)
        return sources[kind].at[0, :, pl.ds(column, cw)]

    def aim(f, key):
        w = min(key, top)
        if key < top:
            return w, 0, w
        return w, 1, (low if key == top and f < top else top)

    def outgoing(kind, f, key, dx):
        w, s, level = aim(f, key)
        xx = lax.rem(x + dx, G)
        leaves, lands = sems(kind, s, f)
        return pltpu.make_async_remote_copy(
            src_ref=block(kind, w, xx), dst_ref=slot(kind, s, f, x),
            send_sem=leaves, recv_sem=lands, **to(level, xx * C + c),
        )

    def own(kind, f, key):
        w, s, _ = aim(f, key)
        return pltpu.make_async_copy(block(kind, w, x), slot(kind, s, f, x), sems(kind, s, f)[1])

    def passed(i, kind, dc, late):
        return pltpu.make_async_remote_copy(
            src_ref=kv.at[i, c, kind - 1], dst_ref=kv.at[i, c, kind - 1],
            send_sem=pass_send.at[0], recv_sem=pass_recv.at[kind - 1, late, dc - 1],
            **to(t, x * C + lax.rem(c + dc, C)),
        )

    def raised(i, kind):
        return pltpu.make_async_remote_copy(
            src_ref=kv.at[i, c, kind - 1], dst_ref=kv.at[i, c, kind - 1],
            send_sem=raise_send.at[0], recv_sem=kv_recv.at[kind - 1, i], **to(top, h),
        )

    def near(kind, w, dx):
        xx = lax.rem(x + dx, G)
        leaves, lands = sems(kind, 0, w)
        if dx == 0:
            return pltpu.make_async_copy(block(kind, w, x), slot(kind, 0, w, x), lands)
        return pltpu.make_async_remote_copy(
            src_ref=block(kind, w, xx), dst_ref=slot(kind, 0, w, x),
            send_sem=near_send.at[0] if kind == 0 else leaves, recv_sem=lands,
            **to(top, xx * C + c),
        )

    def sidestep(k, key, dx):
        return pltpu.make_async_remote_copy(
            src_ref=block(0, key, lax.rem(x + dx, G)), dst_ref=qb.at[T + k, x],
            send_sem=near_send.at[0], recv_sem=q_recv.at[T + k],
            **to(t, lax.rem(x + dx, G) * C + c),
        )

    def forward(k, key, f, xs):
        return pltpu.make_async_remote_copy(
            src_ref=qb.at[T + k, xs], dst_ref=slot(0, k, f, xs),
            send_sem=q_send.at[0], recv_sem=q_recv.at[k * T + f], **to(low, h),
        )

    def head_of(j):
        return slice(j * HD, (j + 1) * HD)

    def value_head(f, j, dx):
        xx = lax.rem(x + dx, G)
        column = pl.multiple_of((top * G + xx) * cw + j * HD, HD)
        return pltpu.make_async_remote_copy(
            src_ref=v_ref.at[0, :, pl.ds(column, HD)],
            dst_ref=kv.at[T + f, c, 1, x, :, head_of(j)],
            send_sem=kv_send.at[0], recv_sem=vh_recv.at[j], **to(low, xx * C + c),
        )

    def passed_head(i, j, dc):
        here = kv.at[i, c, 1, :, :, head_of(j)]
        return pltpu.make_async_remote_copy(
            src_ref=here, dst_ref=here, send_sem=pass_send.at[0],
            recv_sem=vp_recv.at[j, dc - 1], **to(t, x * C + lax.rem(c + dc, C)),
        )

    def handed(w):
        return [
            pltpu.make_async_remote_copy(
                src_ref=buffer.at[w], dst_ref=buffer.at[top],
                send_sem=leaves.at[0], recv_sem=lands.at[0], **to(w, h),
            )
            for buffer, leaves, lands in ((so, so_send, so_recv), (st, st_send, st_recv))
        ]

    own_rows = pl.ds(pl.multiple_of(group * share, 8), share)

    def lift(p):
        return pltpu.make_async_remote_copy(
            src_ref=w_ref.at[own_rows, cols_of(p)], dst_ref=w3.at[own_rows, cols_of(p)],
            send_sem=w_send.at[0], recv_sem=dn_recv.at[1, p], **to(low, h),
        )

    def trade(p, dg):
        return pltpu.make_async_remote_copy(
            src_ref=w3.at[own_rows, cols_of(p)], dst_ref=w3.at[own_rows, cols_of(p)],
            send_sem=tr_send.at[0], recv_sem=tr_recv.at[p, dg - 1], **beside(dg),
        )

    def mine(i, column, size):
        return ab.at[i, c, :, pl.ds(pl.multiple_of(column, HD), size)]

    def across(i, dx, j=None):
        here = mine(i, x * cw, cw) if j is None else mine(i, x * cw + j * HD, HD)
        return pltpu.make_async_remote_copy(
            src_ref=here, dst_ref=here, send_sem=ax_send.at[0], recv_sem=ax_recv.at[i, dx - 1],
            **to(t, lax.rem(x + dx, G) * C + c),
        )

    def aside(i, xs, dc):
        here = mine(i, xs * cw, cw)
        return pltpu.make_async_remote_copy(
            src_ref=here, dst_ref=here, send_sem=ac_send.at[0], recv_sem=ac_recv.at[i, dc - 1],
            **to(t, x * C + lax.rem(c + dc, C)),
        )

    def spot(r):
        return r % (T - 2)

    def down(level, r, p):
        return pltpu.make_async_remote_copy(
            src_ref=down_out.at[spot(r), p], dst_ref=down_in.at[spot(r), p],
            send_sem=dn_send.at[0], recv_sem=dn_recv.at[spot(r), p], **to(level - 1, h),
        )

    def up(level, r, p):
        return pltpu.make_async_remote_copy(
            src_ref=up_out.at[spot(r), p], dst_ref=up_in.at[spot(r), p],
            send_sem=up_send.at[0], recv_sem=up_recv.at[spot(r), p], **to(level + 1, h),
        )

    def gates(level):
        with jax.named_scope("loads"):
            for copy in loads:
                copy.wait()
        with jax.named_scope("meta"):
            fb[...] = jnp.zeros_like(fb)
            away = [f for f in range(1, T) if level != f and level < top]
            if away:
                landed(mb.at[: len(away)], meta_recv.at[0])
            for f in range(1, T) if level < top else (top,):
                for b in range(mask_row):
                    fb[f : f + 1, b * HD : (b + 1) * HD] = mb[f, b : b + 1, :]
        with jax.named_scope("gate"):
            gb[...] = jnp.dot(
                fb[...], twb[...].astype(jnp.float32),
                precision=lax.Precision.HIGHEST, preferred_element_type=jnp.float32,
            )

    def program(level):
        if level < top:
            features()
        with jax.named_scope("barrier"):
            pl.semaphore_wait(barrier, entered(level))
        if level == top:
            lifts = [lift(p) for p in range(pieces)]
            lifts[0].start()
            features()
        told = [other for other in range(top) if other != level and level > 0]
        for other in told:
            pltpu.make_async_remote_copy(
                src_ref=mb.at[t], dst_ref=mb.at[t], send_sem=meta_send.at[0],
                recv_sem=meta_recv.at[0], **to(other, h),
            ).start()
        count = dict(kv=0, q=0, passed=0, raised=0, near=0, ax=0, ac=0, down=0, up=0, traded=0)

        def send(kinds, key, dxs=tuple(reversed(range(G)))):
            for dx in dxs:
                for kind in kinds:
                    if kind == 0 and level == 0:
                        continue
                    if dx == 0 and aim(level, key)[2] == level:
                        own(kind, level, key).start()
                    else:
                        outgoing(kind, level, key, dx).start()
                        count["q" if kind == 0 else "kv"] += 1

        def group_of(s, f):
            if level == top:
                return T if s else f
            if level == low:
                return 2 * s + (f == top)
            return int(0 < level < f)

        def take(s, f, kinds=(1, 2)):
            i = s * T + f
            for kind in kinds:
                landed(kv.at[i, c, kind - 1], kv_recv.at[kind - 1, i])
                for dc in range(1, C):
                    passed(i, kind, dc, group_of(s, f)).start()
                    count["passed"] += 1
                if s == 1 and level == low and f < low:
                    raised(i, kind).start()
                    count["raised"] += 1

        def take_queries(s, f):
            landed(qb.at[s * T + f], q_recv.at[s * T + f])

        def settle(s, frames, kinds=(1, 2)):
            i = s * T + frames[0]
            for kind in kinds:
                for dc in range(1, C):
                    landed(
                        kv.at[i : i + len(frames), lax.rem(c + C - dc, C), kind - 1],
                        pass_recv.at[kind - 1, group_of(s, frames[0]), dc - 1],
                    )

        def weigh(s, r, j):
            f = r + 1
            keys_here = (f + 1) * tokens
            allowed = jnp.concatenate(
                [
                    jnp.broadcast_to(mb[f, mask_row + g : mask_row + g + 1, 0:1], (1, tokens))
                    for g in range(f + 1)
                ],
                axis=1,
            )
            cols = slice(j * HD, (j + 1) * HD)
            query = qb[s * T + f, :, :, cols].reshape(half, HD)
            key = kv[s * T : s * T + f + 1, :, 0, :, :, cols].reshape(keys_here, HD)
            scores = (
                lax.dot_general(
                    query, key, (((1,), (1,)), ((), ())), preferred_element_type=jnp.float32
                )
                * scale
            )
            scores = jnp.where(allowed > 0.5, scores, -1e30)
            peak = jnp.max(scores, axis=1, keepdims=True)
            lifted = jnp.exp(scores - peak)
            return lifted.astype(jnp.bfloat16), jnp.sum(lifted, axis=1, keepdims=True)

        def mix(s, r, j, rounded, total):
            f = r + 1
            cols = slice(j * HD, (j + 1) * HD)
            value = kv[s * T : s * T + f + 1, :, 1, :, :, cols].reshape((f + 1) * tokens, HD)
            mixed = jnp.dot(rounded, value, preferred_element_type=jnp.float32)
            here = pl.ds(pl.multiple_of(x * cw + j * HD, HD), HD)
            ab[s * (T - 1) + r, c, :, here] = (mixed / total).astype(jnp.bfloat16)

        def attend_own(w):
            lane = lax.broadcasted_iota(jnp.int32, (half, HD), 1)
            stats = jnp.zeros((half, HD), jnp.float32)
            for j in range(hp):
                cols = slice(j * HD, (j + 1) * HD)
                query = qb[w, :, :, cols].reshape(half, HD)
                key = kv[w, :, 0, :, :, cols].reshape(tokens, HD)
                value = kv[w, :, 1, :, :, cols].reshape(tokens, HD)
                scores = (
                    lax.dot_general(
                        query, key, (((1,), (1,)), ((), ())), preferred_element_type=jnp.float32
                    )
                    * scale
                )
                peak = jnp.max(scores, axis=1, keepdims=True)
                lifted = jnp.exp(scores - peak)
                total = jnp.sum(lifted, axis=1, keepdims=True)
                mixed = jnp.dot(
                    lifted.astype(jnp.bfloat16), value, preferred_element_type=jnp.float32
                )
                so[w, :, cols] = (mixed / total).astype(jnp.bfloat16)
                stats = jnp.where(lane == 2 * j, peak, stats)
                stats = jnp.where(lane == 2 * j + 1, total, stats)
            st[w] = jnp.transpose(stats)[:8]
            for copy in handed(w):
                copy.start()

        def attend_last():
            landed(so.at[top], so_recv.at[0])
            landed(st.at[top], st_recv.at[0])
            stats = jnp.transpose(
                jnp.concatenate([st[top], jnp.zeros((HD - 8, half), jnp.float32)], axis=0)
            )
            allowed = jnp.concatenate(
                [
                    jnp.broadcast_to(mb[top, mask_row + g : mask_row + g + 1, 0:1], (1, tokens))
                    for g in range(top)
                ],
                axis=1,
            )
            for j in range(hp):
                cols = slice(j * HD, (j + 1) * HD)
                query = qb[top, :, :, cols].reshape(half, HD)
                key = kv[0:top, :, 0, :, :, cols].reshape(top * tokens, HD)
                value = kv[0:top, :, 1, :, :, cols].reshape(top * tokens, HD)
                scores = (
                    lax.dot_general(
                        query, key, (((1,), (1,)), ((), ())), preferred_element_type=jnp.float32
                    )
                    * scale
                )
                scores = jnp.where(allowed > 0.5, scores, -1e30)
                their_peak = stats[:, 2 * j : 2 * j + 1]
                peak = jnp.maximum(jnp.max(scores, axis=1, keepdims=True), their_peak)
                lifted = jnp.exp(scores - peak)
                theirs = jnp.exp(their_peak - peak) * stats[:, 2 * j + 1 : 2 * j + 2]
                total = jnp.sum(lifted, axis=1, keepdims=True) + theirs
                mixed = jnp.dot(
                    lifted.astype(jnp.bfloat16), value, preferred_element_type=jnp.float32
                )
                mixed += theirs * so[top, :, cols].astype(jnp.float32)
                here = pl.ds(pl.multiple_of(x * cw + j * HD, HD), HD)
                ab[low, c, :, here] = (mixed / total).astype(jnp.bfloat16)
            share_out(0, low)

        def share_out(s, r):
            i = s * (T - 1) + r
            for dx in range(1, G):
                across(i, dx).start()
                count["ax"] += 1
            for dc in range(1, C):
                aside(i, x, dc).start()
                count["ac"] += 1

        def attend(s, r):
            for j in range(hp):
                mix(s, r, j, *weigh(s, r, j))
            share_out(s, r)

        def attend_keys(s, r):
            for j in range(hp):
                rounded, total = weigh(s, r, j)
                lb[s, j] = rounded
                tb[s, j] = jnp.broadcast_to(total, (half, HD))

        def attend_values(s, r):
            for j in range(hp):
                mix(s, r, j, lb[s, j], tb[s, j])
            share_out(s, r)

        def attend_heads(r):
            i, n = T + low - 1, T - 1 + r

            def pass_on(j):
                landed(kv.at[i, c, 1, :, :, head_of(j)], vh_recv.at[j])
                for dc in range(1, C):
                    passed_head(i, j, dc).start()

            settle(1, (*range(low - 1), low), (2,))
            pass_on(0)
            for j in range(hp):
                if j + 1 < hp:
                    pass_on(j + 1)
                for dc in range(1, C):
                    landed(
                        kv.at[i, lax.rem(c + C - dc, C), 1, :, :, head_of(j)],
                        vp_recv.at[j, dc - 1],
                    )
                mix(1, r, j, lb[1, j], tb[1, j])
                for dx in range(1, G):
                    across(n, dx, j).start()
            count["ax"] += G - 1
            count["passed"] += C - 1
            if low - 1 < low:
                raised(i, 2).start()
                count["raised"] += 1
            for dc in range(1, C):
                aside(n, x, dc).start()
                count["ac"] += 1

        def hand_over(s, r):
            i = s * (T - 1) + r
            for dx in range(1, G):
                xs = lax.rem(x + G - dx, G)
                landed(mine(i, xs * cw, cw), ax_recv.at[i, dx - 1])
                for dc in range(1, C):
                    aside(i, xs, dc).start()
                    count["ac"] += 1

        def gathered(s, r):
            i = s * (T - 1) + r
            for dc in range(1, C):
                landed(ab.at[i, lax.rem(c + C - dc, C)], ac_recv.at[i, dc - 1])

        def product(r, p):
            if level == top:
                parts = ((1, wb),)
            elif level == low and r < low:
                parts = ((0, wb), (1, w3))
            else:
                parts = ((0, wb),)
            partial = 0.0
            for s, weight in parts:
                partial += jnp.dot(
                    ab[s * (T - 1) + r].reshape(tokens, G * cw), weight[:, cols_of(p)],
                    preferred_element_type=jnp.float32,
                )
            partial = partial * gb[r + 1 : r + 2, cols_of(p)]
            if level == r + 1:
                moved = [
                    rb[(xs * C + cs) * tl : (xs * C + cs + 1) * tl, cols_of(p)]
                    for cs in range(C)
                    for xs in range(G)
                ]
                partial += jnp.concatenate(moved, axis=0).astype(jnp.float32)
            return partial

        def part(r, p, dc, going_up):
            cc = lax.rem(c + dc, C)
            parts = ((0, wb), (1, w3)) if level == low and r < low else ((0, wb),)
            partial = 0.0
            for s, weight in parts:
                partial += jnp.dot(
                    ab[s * (T - 1) + r, cc], weight[:, cols_of(p)],
                    preferred_element_type=jnp.float32,
                )
            partial = partial * gb[r + 1 : r + 2, cols_of(p)]
            if level == r + 1:
                moved = [
                    rb[pl.ds(pl.multiple_of((xs * C + cc) * tl, tl), tl), cols_of(p)]
                    for xs in range(G)
                ]
                partial += jnp.concatenate(moved, axis=0).astype(jnp.float32)
            rows = pl.ds(pl.multiple_of(cc * half, half), half)
            out, into = (up_out, up_in) if going_up else (down_out, down_in)
            leaves, lands = (up_send, up_recv) if going_up else (dn_send, dn_recv)
            out[spot(r), p, rows, :] = partial.astype(jnp.bfloat16)
            pltpu.make_async_remote_copy(
                src_ref=out.at[spot(r), p, rows], dst_ref=into.at[spot(r), p, rows],
                send_sem=leaves.at[0], recv_sem=lands.at[spot(r), p],
                **to(level + 1 if going_up else level - 1, h),
            ).start()

        def own_parts(r, going_up=False):
            for p in range(2):
                with scope(f"own{r}{p}"):
                    part(r, p, 0, going_up)
                count["up" if going_up else "down"] += 1

        def other_parts(r, going_up=False):
            for p in range(2):
                for dc in range(1, C):
                    with scope(f"other{r}{p}"):
                        part(r, p, dc, going_up)

        def send_down(r, p, value):
            down_out[spot(r), p] = value.astype(jnp.bfloat16)
            down(level, r, p).start()
            count["down"] += 1

        def send_up(r, p, value):
            up_out[spot(r), p] = value.astype(jnp.bfloat16)
            up(level, r, p).start()
            count["up"] += 1

        def from_down(r, p):
            landed(down_in.at[spot(r), p], dn_recv.at[spot(r), p])
            return down_in[spot(r), p].astype(jnp.float32)

        def from_up(r, p):
            landed(up_in.at[spot(r), p], up_recv.at[spot(r), p])
            return up_in[spot(r), p].astype(jnp.float32)

        def finish(p):
            r = level
            total = pb[r, p] + from_down(r, p)
            if r > 0:
                total += from_up(r, p)
            total = total.astype(out_ref.dtype)
            for cs in range(C):
                for xs in range(G):
                    row, token = (cs * G + xs) * tl, (xs * C + cs) * tl
                    out_ref[token : token + tl, cols_of(p)] = total[row : row + tl]

        scope = jax.named_scope
        early = (3 * pieces) // 5
        order = [(low - 1, p) for p in range(2)]
        order += [(r, p) for r in range(low - 1) for p in range(pieces)]
        order += [(low - 1, p) for p in range(2, pieces)]

        if level == top:
            for p in range(1, early):
                lifts[p].start()
            lower = tuple(reversed(range(low)))
            for w in lower:
                for dx in reversed(range(G)):
                    for kind in (1, 0, 2):
                        near(kind, w, dx).start()
                        if dx > 0:
                            count["near" if kind == 0 else "kv"] += 1
            for w in lower:
                send((0,), w)
            send((0, 1, 2), top)
            for w in lower:
                with scope(f"near{w}"):
                    take(0, w)
                    take_queries(0, w)
            for w in lower:
                with scope(f"own{w}"):
                    settle(0, (w,))
                    attend_own(w)
            for p in range(early, pieces):
                lifts[p].start()
            send((1, 2, 0), low)
            gates(level)
            for f in range(T):
                with scope(f"take{f}"):
                    take(1, f)
            with scope("settle"):
                take_queries(1, top)
                settle(1, range(T))
            with scope("attend"):
                attend(1, low)
            with scope("gather"):
                hand_over(1, low)
                gathered(1, low)
            with scope("project"):
                for p in range(pieces):
                    send_down(low, p, product(low, p))
            pltpu.make_async_copy(fresh_ref, out_ref, load_sem.at[3]).wait()
            landed(w3.at[own_rows], w_send.at[0])
        elif level == low:
            for w in range(low):
                send((1, 2, 0), w)
            send((1, 2, 0), low)
            send((1, 2, 0), top)
            send((1, 2), T)

            def exchange(p):
                with scope(f"trade{p}"):
                    landed(w3.at[own_rows, cols_of(p)], dn_recv.at[1, p])
                for dg in range(1, groups):
                    trade(p, dg).start()

            def exchanged(p):
                for dg in range(1, groups):
                    theirs = pl.ds(
                        pl.multiple_of(lax.rem(group + groups - dg, groups) * share, 8), share
                    )
                    landed(w3.at[theirs, cols_of(p)], tr_recv.at[p, dg - 1])

            gates(level)
            for p in range(early - 1):
                exchange(p)
            with scope("take_early"):
                for f in (*range(low - 1), low):
                    for s in (0, 1):
                        take(s, f)
                for s in (0, 1):
                    take_queries(s, low)
            with scope("keys"):
                for s in (0, 1):
                    take(s, low - 1, (1,))
            exchange(early - 1)
            for s in (0, 1):
                with scope(f"settle{s}1"):
                    settle(s, range(low + 1), (1,))
                with scope(f"attend{s}{low - 1}1"):
                    attend_keys(s, low - 1)
            with scope("values0"):
                take(0, low - 1, (2,))
            with scope("settle02"):
                settle(0, range(low + 1), (2,))
            with scope("attend02"):
                attend_values(0, low - 1)
            with scope("attend12"):
                attend_heads(low - 1)
            for r in reversed(range(low - 1)):
                with scope(f"hand0{r + 1}"):
                    hand_over(0, r + 1)
                for s in (0, 1):
                    with scope(f"q{r + 1}{s}"):
                        take_queries(s, r + 1)
                    with scope(f"attend{s}{r}"):
                        attend(s, r)
                with scope(f"hand1{r + 1}"):
                    hand_over(1, r + 1)
                for p in range(2):
                    exchanged(p)
                own_parts(r + 1)
            ready = set()
            known = {0, 1} if low > 1 else set()
            swapped = False

            def last_frame():
                with scope("take3"):
                    take(0, top)
                    take_queries(0, top)
                    settle(0, (top,))
                with scope("attend3"):
                    attend(0, low)

            for r, p in order:
                if p >= early and not swapped:
                    swapped = True
                    for q in range(early + 1, pieces):
                        exchange(q)
                if r not in ready:
                    ready.add(r)
                    if r == 0:
                        exchange(early)
                    if r == 0:
                        for s in (0, 1):
                            with scope(f"hand{s}{r}"):
                                hand_over(s, r)
                        for q in range(2):
                            if q not in known:
                                known.add(q)
                                exchanged(q)
                        own_parts(r)
                    with scope(f"gather{r}"):
                        for s in (0, 1):
                            gathered(s, r)
                    other_parts(r)
                if p < 2:
                    continue
                if p not in known:
                    known.add(p)
                    with scope(f"w{p}"):
                        exchanged(p)
                with scope(f"project{r}{p}"):
                    send_down(r, p, product(r, p))
            last_frame()
            with scope("gather3"):
                hand_over(0, low)
                gathered(0, low)
            with scope("project3"):
                for p in range(pieces):
                    pb[low, p] = product(low, p)
            for p in range(pieces):
                with scope(f"finish{p}"):
                    finish(p)
            landed(w3.at[own_rows], tr_send.at[0])
        else:
            if level > 0:
                for k, w in enumerate((low, top)):
                    for dx in range(1, G):
                        sidestep(k, w, dx).start()
                        count["near"] += 1
            for kind in (1, 2):
                for w in (low, top):
                    if kind == 2 and w == top and level == low - 1:
                        for j in range(hp):
                            for dx in reversed(range(G)):
                                value_head(level, j, dx).start()
                        count["kv"] += G
                    else:
                        send((kind,), w)
            for w in (low, top):
                send((0,), w, (0,))
            for w in range(level + 1, low):
                send((1, 2, 0), w)
            for w in range(level):
                send((1, 2, 0), w)
            send((1, 2, 0), level)
            gates(level)
            if level > 0:
                for k, w in enumerate((low, top)):
                    for dx in range(1, G):
                        xs = lax.rem(x + dx, G)
                        landed(qb.at[T + k, xs], q_recv.at[T + k])
                        forward(k, w, level, xs).start()
                        count["q"] += 1
            stages = (
                (range(T - 1), range(T - 3, -1, -1)),
                (range(T - 1, T), range(T - 2, T - 1)),
            )
            if level > 0:
                stages = (
                    (range(level + 1), range(level)),
                    (range(level + 1, T), range(level, T - 1)),
                )
            for frames, rounds in stages:
                for f in frames:
                    with scope(f"take{f}"):
                        if f < top:
                            take(0, f)
                        if f > 0:
                            take_queries(0, f)
                if frames[0] < top:
                    settle(0, range(frames[0], min(frames[-1] + 1, top)))
                for r in rounds:
                    with scope(f"attend{r}"):
                        if r < low:
                            attend(0, r)
                        else:
                            attend_last()
                for r in rounds:
                    early_up = level == 0 and 0 < r < low
                    with scope(f"gather{r}"):
                        hand_over(0, r)
                    if early_up:
                        own_parts(r, True)
                    with scope(f"pair{r}"):
                        gathered(0, r)
                    if early_up:
                        other_parts(r, True)
                    with scope(f"project{r}"):
                        for p in range(2 if early_up else 0, pieces - early_up):
                            value = product(r, p)
                            if level == 0 and r > 0:
                                send_up(r, p, value)
                            else:
                                pb[r, p] = value
            if level == 0:
                for r in range(1, low):
                    send_up(r, pieces - 1, product(r, pieces - 1))
            ups = [
                (q, p) for p in range(pieces) for q in reversed(range(level + 1, T - 1)) if level
            ]
            for n, (r, p) in enumerate(pair for pair in order if pair[0] <= level):
                if r == level:
                    with scope(f"finish{p}"):
                        finish(p)
                else:
                    with scope(f"down{r}{p}"):
                        send_down(r, p, pb[r, p] + from_down(r, p))
                if n >= 2 and ups:
                    q, p = ups.pop(0)
                    with scope(f"up{q}{p}"):
                        send_up(q, p, pb[q, p] + from_up(q, p))
            for q, p in ups:
                send_up(q, p, pb[q, p] + from_up(q, p))
        with scope("sends"):
            if told:
                landed(mb.at[: len(told)], meta_send.at[0])
            landed(kv.at[: count["kv"] // 2, 0, :, 0], kv_send.at[0])
            if count["q"]:
                landed(qb.at[: count["q"], 0], q_send.at[0])
            if count["near"]:
                landed(qb.at[: count["near"], 0], near_send.at[0])
            if level == top:
                landed(so.at[:low], so_send.at[0])
                landed(st.at[:low], st_send.at[0])
            if count["passed"]:
                landed(kv.at[: count["passed"] // 2, 0], pass_send.at[0])
            if count["raised"]:
                landed(kv.at[: count["raised"] // 2, 0], raise_send.at[0])
            if count["ax"]:
                landed(ab.at[: count["ax"], 0, :, :cw], ax_send.at[0])
            if count["ac"]:
                landed(ab.at[: count["ac"] // G, 0], ac_send.at[0])
            if count["down"]:
                landed(down_out.at[: count["down"] // pieces], dn_send.at[0])
            if count["up"]:
                landed(up_out.at[: count["up"] // pieces], up_send.at[0])

    for level in range(T):
        pl.when(t == level)(functools.partial(program, level))


def fused(T, H, heads, groups):
    def on_device_fused(
        queries, keys, values, residual, fresh_frame, out_weight, time_weight, noise_steps, frame_mask
    ):
        level_heads = heads // T
        G = math.gcd(level_heads, H)
        C = H // G
        hp = level_heads // G
        tl = queries.shape[1]
        tokens = tl * H
        width = out_weight.shape[1]
        pieces = width // (2 * HD)
        nb = width // pieces
        meta_rows = -(-(FREQ // HD + T) // 8) * 8
        cw = hp * HD
        bf16, f32 = jnp.bfloat16, jnp.float32
        dma = pltpu.SemaphoreType.DMA
        chunk = (T - 2, pieces, tokens, nb)
        out = pl.pallas_call(
            functools.partial(fused_kernel, T, G, C, hp, pieces, groups),
            out_shape=jax.ShapeDtypeStruct((tokens, width), bf16),
            in_specs=[pl.BlockSpec(memory_space=pltpu.HBM)] * 7
            + [pl.BlockSpec(memory_space=pltpu.SMEM)] * 2,
            out_specs=pl.BlockSpec(memory_space=pltpu.VMEM),
            scratch_shapes=[
                pltpu.VMEM((2 * T, G, tl, cw), bf16),
                pltpu.VMEM((2 * T, C, 2, G, tl, cw), bf16),
                pltpu.VMEM((2 * (T - 1), C, G * tl, G * cw), bf16),
                pltpu.VMEM((2, hp, G * tl, (T - 1) * tokens), bf16),
                pltpu.VMEM((2, hp, G * tl, HD), f32),
                pltpu.VMEM((T, G * tl, cw), bf16),
                pltpu.VMEM((T, 8, G * tl), f32),
                pltpu.VMEM((T, meta_rows, HD), f32),
                pltpu.VMEM((8, FREQ), f32),
                pltpu.VMEM((8, width), f32),
                pltpu.VMEM(out_weight.shape, bf16),
                pltpu.VMEM(out_weight.shape, bf16),
                pltpu.VMEM(time_weight.shape, bf16),
                pltpu.VMEM((tokens, width), bf16),
                pltpu.VMEM((T - 1, pieces, tokens, nb), f32),
                pltpu.VMEM(chunk, bf16),
                pltpu.VMEM(chunk, bf16),
                pltpu.VMEM(chunk, bf16),
                pltpu.VMEM(chunk, bf16),
                dma((4,)),
                dma((1,)),
                dma((1,)),
                dma((1,)),
                dma((1,)),
                dma((2, 2 * T)),
                dma((2 * T,)),
                dma((1,)),
                dma((2, T + 1, C - 1)),
                dma((1,)),
                dma((1,)),
                dma((2 * (T - 1), G - 1)),
                dma((1,)),
                dma((2 * (T - 1), C - 1)),
                dma((1,)),
                dma((2, pieces)),
                dma((1,)),
                dma((2, pieces)),
                dma((1,)),
                dma((1,)),
                dma((pieces, groups - 1)),
                dma((1,)),
                dma((1,)),
                dma((1,)),
                dma((1,)),
                dma((1,)),
                dma((hp,)),
                dma((hp, C - 1)),
            ],
            compiler_params=pltpu.CompilerParams(
                collective_id=0, has_side_effects=True, vmem_limit_bytes=32 * 1024 * 1024
            ),
        )(
            *(
                pltpu.with_memory_space_constraint(array, pltpu.HBM)
                for array in (
                    queries, keys, values, residual, fresh_frame, out_weight, time_weight
                )
            ),
            noise_steps,
            frame_mask,
        )
        return out[None]

    return on_device_fused


def solution(mesh):
    placed = (
        P(("groups", "tm"), "head", None),
        P(("groups", "tm"), "head", None),
        P(("groups", "tm"), "head", None),
        P(("groups", "tm"), None, "head"),
        P("groups", "head"),
        P("tm", "head"),
        P(None, "head"),
        P(("groups", "tm")),
        P(("groups", "tm"), None),
    )
    def whole(*args):
        frames, spread = mesh.shape["tm"], mesh.shape["head"]
        heads = args[0].shape[2] // HD
        fits = 2 < frames <= 4 and heads % frames == 0 and args[5].shape[1] % (spread * 2 * HD) == 0
        return jax.shard_map(
            fused(frames, spread, heads, mesh.shape["groups"]) if fits else on_device,
            mesh=mesh,
            in_specs=placed,
            out_specs=P(("groups", "tm"), None, "head"),
            check_vma=False,
        )(*args)

    return whole
```
